256 devices in a mesh: rows: 32 (over y, x, core), outs: 8 (over z).
Axes of the slice: x: 4, y: 4, z: 8, core: 2. Of those that a mesh axis runs over, the one named last changes fastest.
Arguments:
- codes: int32 [49152, 256], P('rows'), may hold values from 0 to 31
- node_of_row: int32 [49152], P('rows'), may hold values from 0 to 15
- grad: bfloat16 [49152, 128], P('rows', 'outs'), may hold values from -6 to 6
- hess: bfloat16 [49152, 128], P('rows', 'outs'), may hold values from 0.099609375 to 1
- small_side: int32 [8], replicated, may hold values from 0 to 1
- evicted: int32 [8], replicated, may hold values from 0 to 1, as said below
- parent_hist: float32 [2, 8, 128, 8192], P(None, None, 'outs', 'rows'), as said below
Outputs:
- node_hist: float32 [2, 16, 128, 8192], P(None, None, 'outs', 'rows')
- split_gain: float32 [16, 8192], P(None, 'rows')
- best_gain: float32 [16], replicated
The draws below stay inside these ranges and needn't reach their ends.
Inputs may be any that keep to these rules, and one draw needn't show every extreme that they name: `evicted`: exactly 3 of the 8 entries are 1. `parent_hist`: the hessian component is not negative.
All inputs are finite; a program needn't handle non-finite values.
Results may differ from the reference program's by a relative error of at most 0.0003.
Values may be sent and summed in bfloat16 or wider, within the bound.
A program may use at most 256 MiB of HBM per device.

```python
import math
import jax
import jax.numpy as jnp
import numpy as np
from jax import lax

F = 256
BINS = 32
TARGETS = 128
PAIRS = 8
EVICT = 3
NODES = 16
ROWS = 49152


def draw_evicted(key, part):
    order = jax.random.permutation(jax.random.fold_in(key, 11), PAIRS)
    return (order < EVICT).astype(jnp.int32)


def draw_parent_hist(key, part):
    mean_rows = 2.0 * ROWS / (NODES * BINS)
    key_grad, key_hess = jax.random.split(jax.random.fold_in(key, 5))
    shape = (PAIRS, TARGETS, F * BINS)
    grad_part = jnp.clip(jax.random.normal(key_grad, shape, jnp.float32), -6.0, 6.0) * mean_rows ** 0.5
    hess_part = jax.random.uniform(key_hess, shape, jnp.float32, 0.0, 1.0) * 0.8 * mean_rows
    return jnp.stack([grad_part, hess_part], axis=0)


def plant(result, rng, least, high):
    dims = result.shape
    index_at = [jax.random.randint(jax.random.fold_in(rng, axis), (), 0, dims[axis]) for axis in range(len(dims))]
    result = result.at[tuple(index_at)].set(least)
    longest = dims.index(max(dims))
    index_at[longest] = (index_at[longest] + 1) % dims[longest]
    return result.at[tuple(index_at)].set(high)


def steps_of(own_key, shape, cuts, least, high):
    level, own = 1.0, jax.random.fold_in(own_key, 6)
    for dim, parts in cuts:
        draws = jnp.exp(jax.random.uniform(jax.random.fold_in(own, dim), (parts,), jnp.float32, least / len(cuts), high / len(cuts)))
        level = level * jnp.repeat(draws, shape[dim] // parts).reshape([-1 if axis == dim else 1 for axis in range(len(shape))])
    return level


def cumulative_ranks(count, skew):
    portions = [(1 << 20) // math.isqrt(grade ** skew) + 1 for grade in range(1, count + 1)]
    deviation = 1 + sum(portions) // (1 << 30)
    return np.cumsum(np.array([max(1, weight // deviation) for weight in portions]))


def skewed_ids(stream_key, shape, count, slope):
    grid = cumulative_ranks(count, slope)
    pick = jax.random.randint(jax.random.fold_in(stream_key, 1), shape, 0, int(grid[count - 1]))
    grade = jnp.searchsorted(jnp.asarray(grid, jnp.int32), pick, side="right")
    return jax.random.permutation(jax.random.fold_in(stream_key, 2), count)[grade].astype(jnp.int32)


def centred(key, shape, scale, reach, shards=(), kind=jnp.bfloat16):
    level = steps_of(key, shape, shards, -0.22, 0.18) if shards else 1.0
    drawn = jax.random.normal(key, shape, jnp.float32) * scale * level
    return jnp.minimum(jnp.maximum(drawn, -reach), reach).astype(kind)


def setup_inputs(seed: int = 0) -> dict:
    key_list = jax.random.split(jax.random.key(seed), 8)
    codes = plant(jax.random.randint(key_list[0], (ROWS, F), 0, BINS), jax.random.fold_in(key_list[0], 1), 0, BINS - 1).astype(jnp.int32)
    node_of_row = plant(skewed_ids(key_list[1], (ROWS,), NODES, 2), jax.random.fold_in(key_list[1], 3), 0, NODES - 1).astype(jnp.int32)
    grad = centred(key_list[2], (ROWS, TARGETS), 1.0, 6.0, ((0, 32), (1, 8)))
    hess = jnp.clip(jnp.exp(math.log(1.0) - 2.306499 * jax.random.uniform(key_list[3], (ROWS, TARGETS), jnp.float32) ** steps_of(key_list[3], (ROWS, TARGETS), ((0, 32), (1, 8)), -0.2, 0.2)), 0.099609375, 1.0).astype(jnp.bfloat16)
    small_side = plant(jax.random.randint(key_list[4], (PAIRS,), 0, 2), jax.random.fold_in(key_list[4], 1), 0, 1).astype(jnp.int32)
    evicted = draw_evicted(jax.random.fold_in(key_list[7], 71), 0)
    parent_hist = draw_parent_hist(jax.random.fold_in(key_list[7], 71), 0)
    return dict(codes=codes, node_of_row=node_of_row, grad=grad, hess=hess, small_side=small_side, evicted=evicted, parent_hist=parent_hist)


def build_all(codes, node_of_row, grad, hess):
    data = jnp.concatenate([grad.astype(jnp.float32), hess.astype(jnp.float32)], axis=1)

    def one_feature(column):
        segment = node_of_row * BINS + column
        return jax.ops.segment_sum(data, segment, num_segments=NODES * BINS)

    per_feature = lax.map(one_feature, jnp.transpose(codes))
    hist = per_feature.reshape(F, NODES, BINS, 2, TARGETS)
    return jnp.transpose(hist, (3, 1, 4, 0, 2)).reshape(2, NODES, TARGETS, F * BINS)


def gain_terms(node_hist):
    grads = node_hist[0]
    hesses = node_hist[1]
    nodes, targets, span = grads.shape
    grads = grads.reshape(nodes, targets, span // BINS, BINS)
    hesses = hesses.reshape(nodes, targets, span // BINS, BINS)
    left_g = jnp.cumsum(grads, axis=3)
    left_h = jnp.cumsum(hesses, axis=3)
    total_g = left_g[..., -1:]
    total_h = left_h[..., -1:]

    def score(a, s):
        return a * a / (jnp.maximum(s, 0.0) + 1.0)

    gain = score(left_g, left_h) + score(total_g - left_g, total_h - left_h) - score(total_g, total_h)
    return jnp.sum(gain, axis=1).reshape(nodes, span)


def reference(codes, node_of_row, grad, hess, small_side, evicted, parent_hist):
    built = build_all(codes, node_of_row, grad, hess)
    pairs = small_side.shape[0]
    pair_view = built.reshape(2, pairs, 2, TARGETS, F * BINS)
    small = (small_side == 0)[None, :, None, None]
    child = jnp.where(small, pair_view[:, :, 0], pair_view[:, :, 1])
    rebuilt = jnp.where(small, pair_view[:, :, 1], pair_view[:, :, 0])
    gone = (evicted == 1)[None, :, None, None]
    sibling = jnp.where(gone, rebuilt, parent_hist - child)
    first = jnp.where(small, child, sibling)
    second = jnp.where(small, sibling, child)
    node_hist = jnp.stack([first, second], axis=2).reshape(2, NODES, TARGETS, F * BINS)
    split_gain = gain_terms(node_hist) / TARGETS
    best_gain = jnp.max(split_gain, axis=1)
    return node_hist, split_gain, best_gain
```

```python
import functools

import jax
import jax.numpy as jnp
import numpy as np
from jax import lax
from jax.experimental import pallas as pl
from jax.experimental.pallas import tpu as pltpu
from jax.sharding import PartitionSpec as P

BINS = 32
ROW_TILE = 2048


def hist_kernel(codes_ref, v_ref, node_ref, out_ref, *, nodes):
    @pl.when(pl.program_id(0) == 0)
    def _():
        out_ref[...] = jnp.zeros_like(out_ref)

    feats, rows = codes_ref.shape
    one = jnp.ones((), jnp.bfloat16)
    zero = jnp.zeros((), jnp.bfloat16)
    bins = lax.broadcasted_iota(jnp.int32, (BINS, rows), 0)
    onehot = jnp.concatenate(
        [jnp.where(codes_ref[f : f + 1, :] == bins, one, zero) for f in range(feats)], axis=0
    )
    node = node_ref[...]
    v = v_ref[...]
    tl = v.shape[0] // 2
    blocks = []
    for c in range(2):
        vc = v[c * tl : (c + 1) * tl]
        for n in range(nodes):
            blocks.append(jnp.where(node == n, vc, zero))
    vals = jnp.concatenate(blocks, axis=0)
    out_ref[...] += lax.dot_general(
        vals, onehot, (((1,), (1,)), ((), ())), preferred_element_type=jnp.float32
    )


def build_hist(codes_t, v_t, node_all, nodes):
    feats, total = codes_t.shape
    width = v_t.shape[0]
    tile = min(ROW_TILE, total)
    steps = total // tile
    out_rows = width * nodes
    cols = feats * BINS
    return pl.pallas_call(
        functools.partial(hist_kernel, nodes=nodes),
        out_shape=jax.ShapeDtypeStruct((out_rows, cols), jnp.float32),
        grid=(steps,),
        in_specs=[
            pl.BlockSpec((feats, tile), lambda i: (0, i)),
            pl.BlockSpec((width, tile), lambda i: (0, i)),
            pl.BlockSpec((1, tile), lambda i: (0, i)),
        ],
        out_specs=pl.BlockSpec((out_rows, cols), lambda i: (0, 0)),
        cost_estimate=pl.CostEstimate(
            flops=2 * out_rows * cols * total,
            bytes_accessed=total * (feats * 4 + width * 2 + 4) + out_rows * cols * 4,
            transcendentals=0,
        ),
    )(codes_t, v_t, node_all)


def prefix_matrices(span):
    i = np.arange(span)[:, None]
    j = np.arange(span)[None, :]
    same = (i // BINS) == (j // BINS)
    tri = (same & (i <= j)).astype(np.float32)
    last = (i == (j // BINS) * BINS + BINS - 1).astype(np.float32)
    return jnp.asarray(tri), jnp.asarray(last)


def gain_terms(node_hist):
    _, nodes, targets, span = node_hist.shape
    tri, last = prefix_matrices(span)
    flat = node_hist.reshape(2 * nodes * targets, span)
    left = jnp.dot(flat, tri, precision=lax.Precision.HIGHEST, preferred_element_type=jnp.float32)
    total = jnp.dot(left, last, precision=lax.Precision.HIGHEST, preferred_element_type=jnp.float32)
    left = left.reshape(2, nodes, targets, span)
    total = total.reshape(2, nodes, targets, span)
    left_g, left_h = left[0], left[1]
    total_g, total_h = total[0], total[1]

    def score(a, s):
        return a * a / (jnp.maximum(s, 0.0) + 1.0)

    gain = (
        score(left_g, left_h) + score(total_g - left_g, total_h - left_h) - score(total_g, total_h)
    )
    return jnp.sum(gain, axis=1)


def local(codes, node_of_row, grad, hess, small_side, evicted, parent_hist):
    pairs = small_side.shape[0]
    nodes = 2 * pairs
    local_targets = grad.shape[1]
    targets = local_targets * lax.axis_size("outs")
    codes_t = lax.all_to_all(
        codes.astype(jnp.int16).T, "rows", 0, 1, tiled=True
    ).astype(jnp.int32)
    v_t = lax.all_gather(jnp.concatenate([grad.T, hess.T], axis=0), "rows", axis=1, tiled=True)
    node_all = lax.all_gather(node_of_row.reshape(1, -1), "rows", axis=1, tiled=True)
    span = codes_t.shape[0] * BINS
    built = build_hist(codes_t, v_t, node_all, nodes).reshape(2, nodes, local_targets, span)
    small = (small_side == 0)[None, :, None, None]
    pair_view = built.reshape(2, pairs, 2, local_targets, span)
    child = jnp.where(small, pair_view[:, :, 0], pair_view[:, :, 1])
    rebuilt = jnp.where(small, pair_view[:, :, 1], pair_view[:, :, 0])
    gone = (evicted == 1)[None, :, None, None]
    sibling = jnp.where(gone, rebuilt, parent_hist - child)
    first = jnp.where(small, child, sibling)
    second = jnp.where(small, sibling, child)
    node_hist = jnp.stack([first, second], axis=2).reshape(2, nodes, local_targets, span)
    partial_gain = gain_terms(node_hist)
    split_gain = lax.psum(partial_gain, "outs") / targets
    best_gain = lax.pmax(jnp.max(split_gain, axis=1), "rows")
    return (node_hist, split_gain, best_gain)


def solution(mesh):
    return jax.shard_map(
        local,
        mesh=mesh,
        in_specs=(
            P("rows", None),
            P("rows"),
            P("rows", "outs"),
            P("rows", "outs"),
            P(),
            P(),
            P(None, None, "outs", "rows"),
        ),
        out_specs=(P(None, None, "outs", "rows"), P(None, "rows"), P()),
        check_vma=False,
    )
```

```python
import functools

import jax
import jax.numpy as jnp
import numpy as np
from jax import lax
from jax.experimental import pallas as pl
from jax.experimental.pallas import tpu as pltpu
from jax.sharding import PartitionSpec as P

BINS = 32
ROW_TILE = 2048


def hist_kernel(codes_ref, v_ref, out_ref, *, nodes):
    @pl.when(pl.program_id(0) == 0)
    def _():
        out_ref[...] = jnp.zeros_like(out_ref)

    feats, rows = codes_ref.shape
    one = jnp.ones((), jnp.bfloat16)
    zero = jnp.zeros((), jnp.bfloat16)
    bins = lax.broadcasted_iota(jnp.int32, (BINS, rows), 0)
    onehot = jnp.concatenate(
        [jnp.where(codes_ref[f : f + 1, :] == bins, one, zero) for f in range(feats)], axis=0
    )
    v = v_ref[...]
    tl = v.shape[0] // 2
    node = v[2 * tl : 2 * tl + 1]
    blocks = []
    for c in range(2):
        vc = v[c * tl : (c + 1) * tl]
        for n in range(nodes):
            blocks.append(jnp.where(node == jnp.asarray(n, jnp.bfloat16), vc, zero))
    vals = jnp.concatenate(blocks, axis=0)
    out_ref[...] += lax.dot_general(
        vals, onehot, (((1,), (1,)), ((), ())), preferred_element_type=jnp.float32
    )


def build_hist(codes_t, v_t, nodes):
    feats, total = codes_t.shape
    width = v_t.shape[0]
    tile = min(ROW_TILE, total)
    steps = total // tile
    out_rows = (width - 1) * nodes
    cols = feats * BINS
    return pl.pallas_call(
        functools.partial(hist_kernel, nodes=nodes),
        out_shape=jax.ShapeDtypeStruct((out_rows, cols), jnp.float32),
        grid=(steps,),
        in_specs=[
            pl.BlockSpec((feats, tile), lambda i: (0, i)),
            pl.BlockSpec((width, tile), lambda i: (0, i)),
        ],
        out_specs=pl.BlockSpec((out_rows, cols), lambda i: (0, 0)),
        cost_estimate=pl.CostEstimate(
            flops=2 * out_rows * cols * total,
            bytes_accessed=total * (feats * 4 + width * 2) + out_rows * cols * 4,
            transcendentals=0,
        ),
    )(codes_t, v_t)


def prefix_matrices(span):
    i = np.arange(span)[:, None]
    j = np.arange(span)[None, :]
    same = (i // BINS) == (j // BINS)
    tri = (same & (i <= j)).astype(np.float32)
    last = (i == (j // BINS) * BINS + BINS - 1).astype(np.float32)
    return jnp.asarray(tri), jnp.asarray(last)


def gain_terms(node_hist):
    _, nodes, targets, span = node_hist.shape
    tri, last = prefix_matrices(span)
    flat = node_hist.reshape(2 * nodes * targets, span)
    left = jnp.dot(flat, tri, precision=lax.Precision.HIGHEST, preferred_element_type=jnp.float32)
    total = jnp.dot(left, last, precision=lax.Precision.HIGHEST, preferred_element_type=jnp.float32)
    left = left.reshape(2, nodes, targets, span)
    total = total.reshape(2, nodes, targets, span)
    left_g, left_h = left[0], left[1]
    total_g, total_h = total[0], total[1]

    def score(a, s):
        return a * a / (jnp.maximum(s, 0.0) + 1.0)

    gain = (
        score(left_g, left_h) + score(total_g - left_g, total_h - left_h) - score(total_g, total_h)
    )
    return jnp.sum(gain, axis=1)


MESH_ID = pl.DeviceIdType.MESH


def exchange_kernel(p_ref, split_ref, best_ref, gbuf, mbuf, gsend, grecv, msend, mrecv, *, targets):
    n_rows = lax.axis_size("rows")
    n_outs = lax.axis_size("outs")
    r = lax.axis_index("rows")
    o = lax.axis_index("outs")
    barrier = pltpu.get_barrier_semaphore()
    for k in range(1, n_outs):
        pl.semaphore_signal(barrier, 1, device_id=(r, (o + k) % n_outs), device_id_type=MESH_ID)
    for k in range(1, n_rows):
        pl.semaphore_signal(barrier, 1, device_id=((r + k) % n_rows, o), device_id_type=MESH_ID)
    pl.semaphore_wait(barrier, n_outs - 1 + n_rows - 1)

    sends = []
    for k in range(1, n_outs):
        copy = pltpu.make_async_remote_copy(
            src_ref=p_ref,
            dst_ref=gbuf.at[o],
            send_sem=gsend.at[k],
            recv_sem=grecv.at[o],
            device_id=(r, (o + k) % n_outs),
            device_id_type=MESH_ID,
        )
        copy.start()
        sends.append(copy)
    gbuf[o] = p_ref[...]
    for k in range(1, n_outs):
        src = (o + n_outs - k) % n_outs
        pltpu.make_async_remote_copy(
            src_ref=p_ref,
            dst_ref=gbuf.at[src],
            send_sem=gsend.at[k],
            recv_sem=grecv.at[src],
            device_id=(r, src),
            device_id_type=MESH_ID,
        ).wait_recv()
    for copy in sends:
        copy.wait_send()
    acc = gbuf[0]
    for j in range(1, n_outs):
        acc = acc + gbuf[j]
    split = acc / targets
    split_ref[...] = split
    width = mbuf.shape[2]
    mbuf[r] = jnp.broadcast_to(jnp.max(split, axis=1, keepdims=True), (split.shape[0], width))

    sends = []
    for k in range(1, n_rows):
        copy = pltpu.make_async_remote_copy(
            src_ref=mbuf.at[r],
            dst_ref=mbuf.at[r],
            send_sem=msend.at[k],
            recv_sem=mrecv.at[r],
            device_id=((r + k) % n_rows, o),
            device_id_type=MESH_ID,
        )
        copy.start()
        sends.append(copy)
    for k in range(1, n_rows):
        src = (r + n_rows - k) % n_rows
        pltpu.make_async_remote_copy(
            src_ref=mbuf.at[src],
            dst_ref=mbuf.at[src],
            send_sem=msend.at[k],
            recv_sem=mrecv.at[src],
            device_id=(src, o),
            device_id_type=MESH_ID,
        ).wait_recv()
    for copy in sends:
        copy.wait_send()
    best = mbuf[0]
    for j in range(1, n_rows):
        best = jnp.maximum(best, mbuf[j])
    best_ref[...] = best


def exchange_gains(partial_gain, targets):
    nodes, span = partial_gain.shape
    n_rows = lax.axis_size("rows")
    n_outs = lax.axis_size("outs")
    width = 128
    return pl.pallas_call(
        functools.partial(exchange_kernel, targets=targets),
        out_shape=(
            jax.ShapeDtypeStruct((nodes, span), jnp.float32),
            jax.ShapeDtypeStruct((nodes, width), jnp.float32),
        ),
        in_specs=[pl.BlockSpec(memory_space=pltpu.VMEM)],
        out_specs=(pl.BlockSpec(memory_space=pltpu.VMEM), pl.BlockSpec(memory_space=pltpu.VMEM)),
        scratch_shapes=[
            pltpu.VMEM((n_outs, nodes, span), jnp.float32),
            pltpu.VMEM((n_rows, nodes, width), jnp.float32),
            pltpu.SemaphoreType.DMA((n_outs,)),
            pltpu.SemaphoreType.DMA((n_outs,)),
            pltpu.SemaphoreType.DMA((n_rows,)),
            pltpu.SemaphoreType.DMA((n_rows,)),
        ],
        compiler_params=pltpu.CompilerParams(collective_id=0, has_side_effects=True),
    )(partial_gain)


def local(codes, node_of_row, grad, hess, small_side, evicted, parent_hist):
    pairs = small_side.shape[0]
    nodes = 2 * pairs
    local_targets = grad.shape[1]
    targets = local_targets * lax.axis_size("outs")
    codes_t = lax.all_to_all(
        codes.astype(jnp.int16).T, "rows", 0, 1, tiled=True
    ).astype(jnp.int32)
    node_row = node_of_row.astype(jnp.bfloat16).reshape(1, -1)
    v_t = lax.all_gather(jnp.concatenate([grad.T, hess.T, node_row], axis=0), "rows", axis=1, tiled=True)
    span = codes_t.shape[0] * BINS
    built = build_hist(codes_t, v_t, nodes).reshape(2, nodes, local_targets, span)
    small = (small_side == 0)[None, :, None, None]
    pair_view = built.reshape(2, pairs, 2, local_targets, span)
    child = jnp.where(small, pair_view[:, :, 0], pair_view[:, :, 1])
    rebuilt = jnp.where(small, pair_view[:, :, 1], pair_view[:, :, 0])
    gone = (evicted == 1)[None, :, None, None]
    sibling = jnp.where(gone, rebuilt, parent_hist - child)
    first = jnp.where(small, child, sibling)
    second = jnp.where(small, sibling, child)
    node_hist = jnp.stack([first, second], axis=2).reshape(2, nodes, local_targets, span)
    partial_gain = gain_terms(node_hist)
    split_gain, best = exchange_gains(partial_gain, targets)
    best_gain = best[:, 0]
    return (node_hist, split_gain, best_gain)


def solution(mesh):
    return jax.shard_map(
        local,
        mesh=mesh,
        in_specs=(
            P("rows", None),
            P("rows"),
            P("rows", "outs"),
            P("rows", "outs"),
            P(),
            P(),
            P(None, None, "outs", "rows"),
        ),
        out_specs=(P(None, None, "outs", "rows"), P(None, "rows"), P()),
        check_vma=False,
    )
```

```python
import functools

import jax
import jax.numpy as jnp
import numpy as np
from jax import lax
from jax.experimental import pallas as pl
from jax.experimental.pallas import tpu as pltpu
from jax.sharding import PartitionSpec as P

BINS = 32


def prefix_matrices(span):
    i = np.arange(span)[:, None]
    j = np.arange(span)[None, :]
    same = (i // BINS) == (j // BINS)
    tri = (same & (i <= j)).astype(np.float32)
    last = (i == (j // BINS) * BINS + BINS - 1).astype(np.float32)
    return jnp.asarray(tri), jnp.asarray(last)


def gain_terms(node_hist):
    _, nodes, targets, span = node_hist.shape
    tri, last = prefix_matrices(span)
    flat = node_hist.reshape(2 * nodes * targets, span)
    left = jnp.dot(flat, tri, precision=lax.Precision.HIGHEST, preferred_element_type=jnp.float32)
    total = jnp.dot(left, last, precision=lax.Precision.HIGHEST, preferred_element_type=jnp.float32)
    left = left.reshape(2, nodes, targets, span)
    total = total.reshape(2, nodes, targets, span)
    left_g, left_h = left[0], left[1]
    total_g, total_h = total[0], total[1]

    def score(a, s):
        return a * a / (jnp.maximum(s, 0.0) + 1.0)

    gain = (
        score(left_g, left_h) + score(total_g - left_g, total_h - left_h) - score(total_g, total_h)
    )
    return jnp.sum(gain, axis=1)


MESH_ID = pl.DeviceIdType.MESH


def exchange_kernel(p_ref, split_ref, best_ref, gbuf, mbuf, gsend, grecv, msend, mrecv, *, targets):
    n_rows = lax.axis_size("rows")
    n_outs = lax.axis_size("outs")
    r = lax.axis_index("rows")
    o = lax.axis_index("outs")
    barrier = pltpu.get_barrier_semaphore()
    for k in range(1, n_outs):
        pl.semaphore_signal(barrier, 1, device_id=(r, (o + k) % n_outs), device_id_type=MESH_ID)
    for k in range(1, n_rows):
        pl.semaphore_signal(barrier, 1, device_id=((r + k) % n_rows, o), device_id_type=MESH_ID)
    pl.semaphore_wait(barrier, n_outs - 1 + n_rows - 1)

    sends = []
    for k in range(1, n_outs):
        copy = pltpu.make_async_remote_copy(
            src_ref=p_ref,
            dst_ref=gbuf.at[o],
            send_sem=gsend.at[k],
            recv_sem=grecv.at[o],
            device_id=(r, (o + k) % n_outs),
            device_id_type=MESH_ID,
        )
        copy.start()
        sends.append(copy)
    gbuf[o] = p_ref[...]
    for k in range(1, n_outs):
        src = (o + n_outs - k) % n_outs
        pltpu.make_async_remote_copy(
            src_ref=p_ref,
            dst_ref=gbuf.at[src],
            send_sem=gsend.at[k],
            recv_sem=grecv.at[src],
            device_id=(r, src),
            device_id_type=MESH_ID,
        ).wait_recv()
    for copy in sends:
        copy.wait_send()
    acc = gbuf[0]
    for j in range(1, n_outs):
        acc = acc + gbuf[j]
    split = acc / targets
    split_ref[...] = split
    width = mbuf.shape[2]
    mbuf[r] = jnp.broadcast_to(jnp.max(split, axis=1, keepdims=True), (split.shape[0], width))

    sends = []
    for k in range(1, n_rows):
        copy = pltpu.make_async_remote_copy(
            src_ref=mbuf.at[r],
            dst_ref=mbuf.at[r],
            send_sem=msend.at[k],
            recv_sem=mrecv.at[r],
            device_id=((r + k) % n_rows, o),
            device_id_type=MESH_ID,
        )
        copy.start()
        sends.append(copy)
    for k in range(1, n_rows):
        src = (r + n_rows - k) % n_rows
        pltpu.make_async_remote_copy(
            src_ref=mbuf.at[src],
            dst_ref=mbuf.at[src],
            send_sem=msend.at[k],
            recv_sem=mrecv.at[src],
            device_id=(src, o),
            device_id_type=MESH_ID,
        ).wait_recv()
    for copy in sends:
        copy.wait_send()
    best = mbuf[0]
    for j in range(1, n_rows):
        best = jnp.maximum(best, mbuf[j])
    best_ref[...] = best


def exchange_gains(partial_gain, targets):
    nodes, span = partial_gain.shape
    n_rows = lax.axis_size("rows")
    n_outs = lax.axis_size("outs")
    width = 128
    return pl.pallas_call(
        functools.partial(exchange_kernel, targets=targets),
        out_shape=(
            jax.ShapeDtypeStruct((nodes, span), jnp.float32),
            jax.ShapeDtypeStruct((nodes, width), jnp.float32),
        ),
        in_specs=[pl.BlockSpec(memory_space=pltpu.VMEM)],
        out_specs=(pl.BlockSpec(memory_space=pltpu.VMEM), pl.BlockSpec(memory_space=pltpu.VMEM)),
        scratch_shapes=[
            pltpu.VMEM((n_outs, nodes, span), jnp.float32),
            pltpu.VMEM((n_rows, nodes, width), jnp.float32),
            pltpu.SemaphoreType.DMA((n_outs,)),
            pltpu.SemaphoreType.DMA((n_outs,)),
            pltpu.SemaphoreType.DMA((n_rows,)),
            pltpu.SemaphoreType.DMA((n_rows,)),
        ],
        compiler_params=pltpu.CompilerParams(collective_id=0, has_side_effects=True),
    )(partial_gain)


def block_hist(acc_ref, v, s, nodes):
    tl = v.shape[0] // 2
    half = s.shape[1]
    feats = s.shape[0] // 2
    one = jnp.ones((), jnp.bfloat16)
    zero = jnp.zeros((), jnp.bfloat16)
    bins = lax.broadcasted_iota(jnp.int32, (BINS, half), 0)
    for h in range(2):
        vh = v[:, h * half : (h + 1) * half]
        node = s[h : h + 1] >> 5
        onehot = jnp.concatenate(
            [jnp.where((s[2 * f + h : 2 * f + h + 1] & (BINS - 1)) == bins, one, zero) for f in range(feats)],
            axis=0,
        )
        blocks = []
        for c in range(2):
            vc = vh[c * tl : (c + 1) * tl]
            for n in range(nodes):
                blocks.append(jnp.where(node == n, vc, zero))
        vals = jnp.concatenate(blocks, axis=0)
        acc_ref[...] += lax.dot_general(
            vals, onehot, (((1,), (1,)), ((), ())), preferred_element_type=jnp.float32
        )


def gather_hist_kernel(seg_ref, v_ref, acc_ref, vbuf, sbuf, vsend, vrecv, ssend, srecv, *, nodes):
    n_rows = lax.axis_size("rows")
    r = lax.axis_index("rows")
    o = lax.axis_index("outs")
    barrier = pltpu.get_barrier_semaphore()

    def greet(k, carry):
        pl.semaphore_signal(barrier, 1, device_id=((r + k) % n_rows, o), device_id_type=MESH_ID)
        return carry

    lax.fori_loop(1, n_rows, greet, 0)
    pl.semaphore_wait(barrier, n_rows - 1)

    def v_copy(k, peer, slot):
        return pltpu.make_async_remote_copy(
            src_ref=v_ref, dst_ref=vbuf.at[slot], send_sem=vsend.at[k], recv_sem=vrecv.at[slot],
            device_id=(peer, o), device_id_type=MESH_ID,
        )

    def s_copy(k, peer, slot):
        return pltpu.make_async_remote_copy(
            src_ref=seg_ref.at[peer], dst_ref=sbuf.at[slot], send_sem=ssend.at[k], recv_sem=srecv.at[slot],
            device_id=(peer, o), device_id_type=MESH_ID,
        )

    def send(k, carry):
        peer = (r + k) % n_rows
        v_copy(k, peer, r).start()
        s_copy(k, peer, r).start()
        return carry

    lax.fori_loop(1, n_rows, send, 0)
    acc_ref[...] = jnp.zeros_like(acc_ref)
    block_hist(acc_ref, v_ref[...], seg_ref[r].astype(jnp.int32), nodes)

    def take(k, carry):
        src = (r + n_rows - k) % n_rows
        v_copy(k, src, src).wait_recv()
        s_copy(k, src, src).wait_recv()
        block_hist(acc_ref, vbuf[src], sbuf[src].astype(jnp.int32), nodes)
        return carry

    lax.fori_loop(1, n_rows, take, 0)

    def drain(k, carry):
        peer = (r + k) % n_rows
        v_copy(k, peer, r).wait_send()
        s_copy(k, peer, r).wait_send()
        return carry

    lax.fori_loop(1, n_rows, drain, 0)


def gather_hist(seg_p, v_loc, nodes):
    n_rows, width, half = seg_p.shape
    vw, rows = v_loc.shape
    feats = width // 2
    out_rows = vw * nodes
    cols = feats * BINS
    total = n_rows * rows
    return pl.pallas_call(
        functools.partial(gather_hist_kernel, nodes=nodes),
        out_shape=jax.ShapeDtypeStruct((out_rows, cols), jnp.float32),
        in_specs=[pl.BlockSpec(memory_space=pltpu.VMEM)] * 2,
        out_specs=pl.BlockSpec(memory_space=pltpu.VMEM),
        scratch_shapes=[
            pltpu.VMEM((n_rows, vw, rows), v_loc.dtype),
            pltpu.VMEM((n_rows, width, half), seg_p.dtype),
            pltpu.SemaphoreType.DMA((n_rows,)),
            pltpu.SemaphoreType.DMA((n_rows,)),
            pltpu.SemaphoreType.DMA((n_rows,)),
            pltpu.SemaphoreType.DMA((n_rows,)),
        ],
        compiler_params=pltpu.CompilerParams(collective_id=1, has_side_effects=True),
        cost_estimate=pl.CostEstimate(
            flops=2 * out_rows * cols * total,
            bytes_accessed=total * (vw * 2 + feats * 2) + out_rows * cols * 4,
            transcendentals=0,
        ),
    )(seg_p, v_loc)


def local(codes, node_of_row, grad, hess, small_side, evicted, parent_hist):
    pairs = small_side.shape[0]
    nodes = 2 * pairs
    local_targets = grad.shape[1]
    targets = local_targets * lax.axis_size("outs")
    n_rows = lax.axis_size("rows")
    count, features = codes.shape
    feats = features // n_rows
    half = count // 2
    seg = (node_of_row[:, None] * BINS + codes).astype(jnp.int16)
    seg_p = jnp.transpose(seg.reshape(2, half, n_rows, feats), (2, 3, 0, 1)).reshape(n_rows, 2 * feats, half)
    v_loc = jnp.concatenate([grad.T, hess.T], axis=0)
    span = feats * BINS
    built = gather_hist(seg_p, v_loc, nodes).reshape(2, nodes, local_targets, span)
    small = (small_side == 0)[None, :, None, None]
    pair_view = built.reshape(2, pairs, 2, local_targets, span)
    child = jnp.where(small, pair_view[:, :, 0], pair_view[:, :, 1])
    rebuilt = jnp.where(small, pair_view[:, :, 1], pair_view[:, :, 0])
    gone = (evicted == 1)[None, :, None, None]
    sibling = jnp.where(gone, rebuilt, parent_hist - child)
    first = jnp.where(small, child, sibling)
    second = jnp.where(small, sibling, child)
    node_hist = jnp.stack([first, second], axis=2).reshape(2, nodes, local_targets, span)
    partial_gain = gain_terms(node_hist)
    split_gain, best = exchange_gains(partial_gain, targets)
    best_gain = best[:, 0]
    return (node_hist, split_gain, best_gain)


def solution(mesh):
    return jax.shard_map(
        local,
        mesh=mesh,
        in_specs=(
            P("rows", None),
            P("rows"),
            P("rows", "outs"),
            P("rows", "outs"),
            P(),
            P(),
            P(None, None, "outs", "rows"),
        ),
        out_specs=(P(None, None, "outs", "rows"), P(None, "rows"), P()),
        check_vma=False,
    )
```

```python
import functools

import jax
import jax.numpy as jnp
import numpy as np
from jax import lax
from jax.experimental import pallas as pl
from jax.experimental.pallas import tpu as pltpu
from jax.sharding import PartitionSpec as P

BINS = 32


def prefix_matrices(span):
    i = np.arange(span)[:, None]
    j = np.arange(span)[None, :]
    same = (i // BINS) == (j // BINS)
    tri = (same & (i <= j)).astype(np.float32)
    last = (i == (j // BINS) * BINS + BINS - 1).astype(np.float32)
    return jnp.asarray(tri), jnp.asarray(last)


def gain_terms(node_hist):
    _, nodes, targets, span = node_hist.shape
    tri, last = prefix_matrices(span)
    flat = node_hist.reshape(2 * nodes * targets, span)
    left = jnp.dot(flat, tri, precision=lax.Precision.HIGHEST, preferred_element_type=jnp.float32)
    total = jnp.dot(left, last, precision=lax.Precision.HIGHEST, preferred_element_type=jnp.float32)
    left = left.reshape(2, nodes, targets, span)
    total = total.reshape(2, nodes, targets, span)
    left_g, left_h = left[0], left[1]
    total_g, total_h = total[0], total[1]

    def score(a, s):
        return a * a / (jnp.maximum(s, 0.0) + 1.0)

    gain = (
        score(left_g, left_h) + score(total_g - left_g, total_h - left_h) - score(total_g, total_h)
    )
    return jnp.sum(gain, axis=1)


MESH_ID = pl.DeviceIdType.MESH


def exchange_kernel(p_ref, split_ref, best_ref, gbuf, mbuf, gsend, grecv, msend, mrecv, *, targets):
    n_rows = lax.axis_size("rows")
    n_outs = lax.axis_size("outs")
    r = lax.axis_index("rows")
    o = lax.axis_index("outs")
    barrier = pltpu.get_barrier_semaphore()
    for k in range(1, n_outs):
        pl.semaphore_signal(barrier, 1, device_id=(r, (o + k) % n_outs), device_id_type=MESH_ID)
    for k in range(1, n_rows):
        pl.semaphore_signal(barrier, 1, device_id=((r + k) % n_rows, o), device_id_type=MESH_ID)
    pl.semaphore_wait(barrier, n_outs - 1 + n_rows - 1)

    sends = []
    for k in range(1, n_outs):
        copy = pltpu.make_async_remote_copy(
            src_ref=p_ref,
            dst_ref=gbuf.at[o],
            send_sem=gsend.at[k],
            recv_sem=grecv.at[o],
            device_id=(r, (o + k) % n_outs),
            device_id_type=MESH_ID,
        )
        copy.start()
        sends.append(copy)
    gbuf[o] = p_ref[...]
    for k in range(1, n_outs):
        src = (o + n_outs - k) % n_outs
        pltpu.make_async_remote_copy(
            src_ref=p_ref,
            dst_ref=gbuf.at[src],
            send_sem=gsend.at[k],
            recv_sem=grecv.at[src],
            device_id=(r, src),
            device_id_type=MESH_ID,
        ).wait_recv()
    for copy in sends:
        copy.wait_send()
    acc = gbuf[0]
    for j in range(1, n_outs):
        acc = acc + gbuf[j]
    split = acc / targets
    split_ref[...] = split
    width = mbuf.shape[2]
    mbuf[r] = jnp.broadcast_to(jnp.max(split, axis=1, keepdims=True), (split.shape[0], width))

    sends = []
    for k in range(1, n_rows):
        copy = pltpu.make_async_remote_copy(
            src_ref=mbuf.at[r],
            dst_ref=mbuf.at[r],
            send_sem=msend.at[k],
            recv_sem=mrecv.at[r],
            device_id=((r + k) % n_rows, o),
            device_id_type=MESH_ID,
        )
        copy.start()
        sends.append(copy)
    for k in range(1, n_rows):
        src = (r + n_rows - k) % n_rows
        pltpu.make_async_remote_copy(
            src_ref=mbuf.at[src],
            dst_ref=mbuf.at[src],
            send_sem=msend.at[k],
            recv_sem=mrecv.at[src],
            device_id=(src, o),
            device_id_type=MESH_ID,
        ).wait_recv()
    for copy in sends:
        copy.wait_send()
    best = mbuf[0]
    for j in range(1, n_rows):
        best = jnp.maximum(best, mbuf[j])
    best_ref[...] = best


def exchange_gains(partial_gain, targets):
    nodes, span = partial_gain.shape
    n_rows = lax.axis_size("rows")
    n_outs = lax.axis_size("outs")
    width = 128
    return pl.pallas_call(
        functools.partial(exchange_kernel, targets=targets),
        out_shape=(
            jax.ShapeDtypeStruct((nodes, span), jnp.float32),
            jax.ShapeDtypeStruct((nodes, width), jnp.float32),
        ),
        in_specs=[pl.BlockSpec(memory_space=pltpu.VMEM)],
        out_specs=(pl.BlockSpec(memory_space=pltpu.VMEM), pl.BlockSpec(memory_space=pltpu.VMEM)),
        scratch_shapes=[
            pltpu.VMEM((n_outs, nodes, span), jnp.float32),
            pltpu.VMEM((n_rows, nodes, width), jnp.float32),
            pltpu.SemaphoreType.DMA((n_outs,)),
            pltpu.SemaphoreType.DMA((n_outs,)),
            pltpu.SemaphoreType.DMA((n_rows,)),
            pltpu.SemaphoreType.DMA((n_rows,)),
        ],
        compiler_params=pltpu.CompilerParams(collective_id=0, has_side_effects=True),
    )(partial_gain)


def block_hist(acc_ref, v, s, nodes):
    tl = v.shape[0] // 2
    half = s.shape[1]
    feats = s.shape[0] // 2
    one = jnp.ones((), jnp.bfloat16)
    zero = jnp.zeros((), jnp.bfloat16)
    bins = lax.broadcasted_iota(jnp.int32, (BINS, half), 0)
    for h in range(2):
        vh = v[:, h * half : (h + 1) * half]
        node = s[h : h + 1] >> 5
        onehot = jnp.concatenate(
            [jnp.where((s[2 * f + h : 2 * f + h + 1] & (BINS - 1)) == bins, one, zero) for f in range(feats)],
            axis=0,
        )
        blocks = []
        for c in range(2):
            vc = vh[c * tl : (c + 1) * tl]
            for n in range(nodes):
                blocks.append(jnp.where(node == n, vc, zero))
        vals = jnp.concatenate(blocks, axis=0)
        acc_ref[...] += lax.dot_general(
            vals, onehot, (((1,), (1,)), ((), ())), preferred_element_type=jnp.float32
        )


def gather_hist_kernel(seg_ref, v_ref, acc_ref, vbuf, sbuf, vsend, fsend, vrecv, ssend, srecv, *, nodes):
    n_rows = lax.axis_size("rows")
    chips = n_rows // 2
    r = lax.axis_index("rows")
    o = lax.axis_index("outs")
    core = r % 2
    chip = r // 2
    partner = chip * 2 + 1 - core
    barrier = pltpu.get_barrier_semaphore()

    def greet(k, carry):
        pl.semaphore_signal(barrier, 1, device_id=((r + k) % n_rows, o), device_id_type=MESH_ID)
        return carry

    lax.fori_loop(1, n_rows, greet, 0)
    pl.semaphore_wait(barrier, n_rows - 1)

    def s_copy(k, peer, slot):
        return pltpu.make_async_remote_copy(
            src_ref=seg_ref.at[peer], dst_ref=sbuf.at[slot], send_sem=ssend.at[k], recv_sem=srecv.at[slot],
            device_id=(peer, o), device_id_type=MESH_ID,
        )

    def v_copy(k, peer, slot):
        return pltpu.make_async_remote_copy(
            src_ref=v_ref, dst_ref=vbuf.at[slot], send_sem=vsend.at[k], recv_sem=vrecv.at[slot],
            device_id=(peer, o), device_id_type=MESH_ID,
        )

    def f_copy(k, slot):
        return pltpu.make_async_remote_copy(
            src_ref=vbuf.at[slot], dst_ref=vbuf.at[slot], send_sem=fsend.at[k], recv_sem=vrecv.at[slot],
            device_id=(partner, o), device_id_type=MESH_ID,
        )

    own = pltpu.make_async_remote_copy(
        src_ref=v_ref, dst_ref=vbuf.at[r], send_sem=fsend.at[0], recv_sem=vrecv.at[r],
        device_id=(partner, o), device_id_type=MESH_ID,
    )
    own.start()

    def send(k, carry):
        v_copy(k, ((chip + k) % chips) * 2 + core, r).start()
        return carry

    lax.fori_loop(1, chips, send, 0)

    def send_seg(k, carry):
        s_copy(k, (r + k) % n_rows, r).start()
        return carry

    lax.fori_loop(1, n_rows, send_seg, 0)
    acc_ref[...] = jnp.zeros_like(acc_ref)
    block_hist(acc_ref, v_ref[...], seg_ref[r].astype(jnp.int32), nodes)

    def take_direct(k, carry):
        src = ((chip + chips - k) % chips) * 2 + core
        v_copy(k, src, src).wait_recv()
        f_copy(k, src).start()
        s_copy(k, src, src).wait_recv()
        block_hist(acc_ref, vbuf[src], sbuf[src].astype(jnp.int32), nodes)
        return carry

    lax.fori_loop(1, chips, take_direct, 0)

    def take_forwarded(k, carry):
        src = ((chip + chips - k) % chips) * 2 + 1 - core
        f_copy(k, src).wait_recv()
        s_copy(k, src, src).wait_recv()
        block_hist(acc_ref, vbuf[src], sbuf[src].astype(jnp.int32), nodes)
        return carry

    lax.fori_loop(0, chips, take_forwarded, 0)

    def drain(k, carry):
        s_copy(k, (r + k) % n_rows, r).wait_send()
        return carry

    lax.fori_loop(1, n_rows, drain, 0)

    def drain_v(k, carry):
        v_copy(k, ((chip + k) % chips) * 2 + core, r).wait_send()
        return carry

    lax.fori_loop(1, chips, drain_v, 0)
    own.wait_send()

    def drain_f(k, carry):
        f_copy(k, ((chip + chips - k) % chips) * 2 + core).wait_send()
        return carry

    lax.fori_loop(1, chips, drain_f, 0)


def gather_hist(seg_p, v_loc, nodes):
    n_rows, width, half = seg_p.shape
    vw, rows = v_loc.shape
    feats = width // 2
    out_rows = vw * nodes
    cols = feats * BINS
    total = n_rows * rows
    return pl.pallas_call(
        functools.partial(gather_hist_kernel, nodes=nodes),
        out_shape=jax.ShapeDtypeStruct((out_rows, cols), jnp.float32),
        in_specs=[pl.BlockSpec(memory_space=pltpu.VMEM)] * 2,
        out_specs=pl.BlockSpec(memory_space=pltpu.VMEM),
        scratch_shapes=[
            pltpu.VMEM((n_rows, vw, rows), v_loc.dtype),
            pltpu.VMEM((n_rows, width, half), seg_p.dtype),
            pltpu.SemaphoreType.DMA((n_rows // 2,)),
            pltpu.SemaphoreType.DMA((n_rows // 2,)),
            pltpu.SemaphoreType.DMA((n_rows,)),
            pltpu.SemaphoreType.DMA((n_rows,)),
            pltpu.SemaphoreType.DMA((n_rows,)),
        ],
        compiler_params=pltpu.CompilerParams(collective_id=1, has_side_effects=True),
        cost_estimate=pl.CostEstimate(
            flops=2 * out_rows * cols * total,
            bytes_accessed=total * (vw * 2 + feats * 2) + out_rows * cols * 4,
            transcendentals=0,
        ),
    )(seg_p, v_loc)


def local(codes, node_of_row, grad, hess, small_side, evicted, parent_hist):
    pairs = small_side.shape[0]
    nodes = 2 * pairs
    local_targets = grad.shape[1]
    targets = local_targets * lax.axis_size("outs")
    n_rows = lax.axis_size("rows")
    count, features = codes.shape
    feats = features // n_rows
    half = count // 2
    seg = (node_of_row[:, None] * BINS + codes).astype(jnp.int16)
    seg_p = jnp.transpose(seg.reshape(2, half, n_rows, feats), (2, 3, 0, 1)).reshape(n_rows, 2 * feats, half)
    v_loc = jnp.concatenate([grad.T, hess.T], axis=0)
    span = feats * BINS
    built = gather_hist(seg_p, v_loc, nodes).reshape(2, nodes, local_targets, span)
    small = (small_side == 0)[None, :, None, None]
    pair_view = built.reshape(2, pairs, 2, local_targets, span)
    child = jnp.where(small, pair_view[:, :, 0], pair_view[:, :, 1])
    rebuilt = jnp.where(small, pair_view[:, :, 1], pair_view[:, :, 0])
    gone = (evicted == 1)[None, :, None, None]
    sibling = jnp.where(gone, rebuilt, parent_hist - child)
    first = jnp.where(small, child, sibling)
    second = jnp.where(small, sibling, child)
    node_hist = jnp.stack([first, second], axis=2).reshape(2, nodes, local_targets, span)
    partial_gain = gain_terms(node_hist)
    split_gain, best = exchange_gains(partial_gain, targets)
    best_gain = best[:, 0]
    return (node_hist, split_gain, best_gain)


def solution(mesh):
    return jax.shard_map(
        local,
        mesh=mesh,
        in_specs=(
            P("rows", None),
            P("rows"),
            P("rows", "outs"),
            P("rows", "outs"),
            P(),
            P(),
            P(None, None, "outs", "rows"),
        ),
        out_specs=(P(None, None, "outs", "rows"), P(None, "rows"), P()),
        check_vma=False,
    )
```

```python
import functools

import jax
import jax.numpy as jnp
import numpy as np
from jax import lax
from jax.experimental import pallas as pl
from jax.experimental.pallas import tpu as pltpu
from jax.sharding import PartitionSpec as P

BINS = 32


def prefix_matrices(span):
    i = np.arange(span)[:, None]
    j = np.arange(span)[None, :]
    same = (i // BINS) == (j // BINS)
    tri = (same & (i <= j)).astype(np.float32)
    last = (i == (j // BINS) * BINS + BINS - 1).astype(np.float32)
    return jnp.asarray(tri), jnp.asarray(last)


def gain_terms(node_hist):
    _, nodes, targets, span = node_hist.shape
    tri, last = prefix_matrices(span)
    flat = node_hist.reshape(2 * nodes * targets, span)
    left = jnp.dot(flat, tri, precision=lax.Precision.HIGHEST, preferred_element_type=jnp.float32)
    total = jnp.dot(left, last, precision=lax.Precision.HIGHEST, preferred_element_type=jnp.float32)
    left = left.reshape(2, nodes, targets, span)
    total = total.reshape(2, nodes, targets, span)
    left_g, left_h = left[0], left[1]
    total_g, total_h = total[0], total[1]

    def score(a, s):
        return a * a / (jnp.maximum(s, 0.0) + 1.0)

    gain = (
        score(left_g, left_h) + score(total_g - left_g, total_h - left_h) - score(total_g, total_h)
    )
    return jnp.sum(gain, axis=1)


MESH_ID = pl.DeviceIdType.MESH


def row_stages(r, n_rows):
    chips = n_rows // 2
    nx = 4 if chips % 4 == 0 else chips
    ny = chips // nx
    chip = r // 2
    core = r % 2
    y = chip // nx
    x = chip % nx
    stages = [
        [chip * 2 + 1 - core],
        [(y * nx + (x + k) % nx) * 2 + core for k in range(1, nx)],
        [(((y + k) % ny) * nx + x) * 2 + core for k in range(1, ny)],
    ]
    return [stage for stage in stages if stage]


def row_peers(r, n_rows):
    return [peer for stage in row_stages(r, n_rows) for peer in stage]


def exchange_kernel(p_ref, split_ref, best_ref, gbuf, mbuf, gsend, grecv, msend, mrecv, *, targets):
    n_rows = lax.axis_size("rows")
    n_outs = lax.axis_size("outs")
    r = lax.axis_index("rows")
    o = lax.axis_index("outs")
    barrier = pltpu.get_barrier_semaphore()
    for k in range(1, n_outs):
        pl.semaphore_signal(barrier, 1, device_id=(r, (o + k) % n_outs), device_id_type=MESH_ID)
    for peer in row_peers(r, n_rows):
        pl.semaphore_signal(barrier, 1, device_id=(peer, o), device_id_type=MESH_ID)
    pl.semaphore_wait(barrier, n_outs - 1 + len(row_peers(r, n_rows)))

    sends = []
    for k in range(1, n_outs):
        copy = pltpu.make_async_remote_copy(
            src_ref=p_ref,
            dst_ref=gbuf.at[o],
            send_sem=gsend.at[k],
            recv_sem=grecv.at[o],
            device_id=(r, (o + k) % n_outs),
            device_id_type=MESH_ID,
        )
        copy.start()
        sends.append(copy)
    gbuf[o] = p_ref[...]
    for k in range(1, n_outs):
        src = (o + n_outs - k) % n_outs
        pltpu.make_async_remote_copy(
            src_ref=p_ref,
            dst_ref=gbuf.at[src],
            send_sem=gsend.at[k],
            recv_sem=grecv.at[src],
            device_id=(r, src),
            device_id_type=MESH_ID,
        ).wait_recv()
    for copy in sends:
        copy.wait_send()
    acc = gbuf[0]
    for j in range(1, n_outs):
        acc = acc + gbuf[j]
    split = acc / targets
    split_ref[...] = split
    width = mbuf.shape[2]
    best = jnp.broadcast_to(jnp.max(split, axis=1, keepdims=True), (split.shape[0], width))
    base = 0
    for peers in row_stages(r, n_rows):
        mbuf[base] = best
        sends = []
        for j, peer in enumerate(peers):
            copy = pltpu.make_async_remote_copy(
                src_ref=mbuf.at[base],
                dst_ref=mbuf.at[base + 1 + j],
                send_sem=msend.at[base + 1 + j],
                recv_sem=mrecv.at[base + 1 + j],
                device_id=(peer, o),
                device_id_type=MESH_ID,
            )
            copy.start()
            sends.append(copy)
        for copy in sends:
            copy.wait_recv()
        for copy in sends:
            copy.wait_send()
        for j in range(len(peers)):
            best = jnp.maximum(best, mbuf[base + 1 + j])
        base += len(peers) + 1
    best_ref[...] = best


def exchange_gains(partial_gain, targets):
    nodes, span = partial_gain.shape
    n_rows = lax.axis_size("rows")
    n_outs = lax.axis_size("outs")
    width = 128
    return pl.pallas_call(
        functools.partial(exchange_kernel, targets=targets),
        out_shape=(
            jax.ShapeDtypeStruct((nodes, span), jnp.float32),
            jax.ShapeDtypeStruct((nodes, width), jnp.float32),
        ),
        in_specs=[pl.BlockSpec(memory_space=pltpu.VMEM)],
        out_specs=(pl.BlockSpec(memory_space=pltpu.VMEM), pl.BlockSpec(memory_space=pltpu.VMEM)),
        scratch_shapes=[
            pltpu.VMEM((n_outs, nodes, span), jnp.float32),
            pltpu.VMEM((n_rows, nodes, width), jnp.float32),
            pltpu.SemaphoreType.DMA((n_outs,)),
            pltpu.SemaphoreType.DMA((n_outs,)),
            pltpu.SemaphoreType.DMA((n_rows,)),
            pltpu.SemaphoreType.DMA((n_rows,)),
        ],
        compiler_params=pltpu.CompilerParams(collective_id=0, has_side_effects=True),
    )(partial_gain)


def block_hist(acc_ref, v, s, nodes):
    tl = v.shape[0] // 2
    half = s.shape[1]
    feats = s.shape[0] // 2
    one = jnp.ones((), jnp.bfloat16)
    zero = jnp.zeros((), jnp.bfloat16)
    bins = lax.broadcasted_iota(jnp.int32, (BINS, half), 0)
    for h in range(2):
        vh = v[:, h * half : (h + 1) * half]
        node = s[h : h + 1] >> 5
        onehot = jnp.concatenate(
            [jnp.where((s[2 * f + h : 2 * f + h + 1] & (BINS - 1)) == bins, one, zero) for f in range(feats)],
            axis=0,
        )
        blocks = []
        for c in range(2):
            vc = vh[c * tl : (c + 1) * tl]
            for n in range(nodes):
                blocks.append(jnp.where(node == n, vc, zero))
        vals = jnp.concatenate(blocks, axis=0)
        acc_ref[...] += lax.dot_general(
            vals, onehot, (((1,), (1,)), ((), ())), preferred_element_type=jnp.float32
        )


def gather_hist_kernel(seg_ref, v_ref, acc_ref, vbuf, sbuf, vsend, fsend, vrecv, ssend, srecv, *, nodes):
    n_rows = lax.axis_size("rows")
    chips = n_rows // 2
    r = lax.axis_index("rows")
    o = lax.axis_index("outs")
    core = r % 2
    chip = r // 2
    partner = chip * 2 + 1 - core
    barrier = pltpu.get_barrier_semaphore()

    def greet(k, carry):
        pl.semaphore_signal(barrier, 1, device_id=((r + k) % n_rows, o), device_id_type=MESH_ID)
        return carry

    lax.fori_loop(1, n_rows, greet, 0)
    pl.semaphore_wait(barrier, n_rows - 1)

    def s_copy(k, peer, slot):
        return pltpu.make_async_remote_copy(
            src_ref=seg_ref.at[peer], dst_ref=sbuf.at[slot], send_sem=ssend.at[k], recv_sem=srecv.at[slot],
            device_id=(peer, o), device_id_type=MESH_ID,
        )

    def v_copy(k, peer, slot):
        return pltpu.make_async_remote_copy(
            src_ref=v_ref, dst_ref=vbuf.at[slot], send_sem=vsend.at[k], recv_sem=vrecv.at[slot],
            device_id=(peer, o), device_id_type=MESH_ID,
        )

    def f_copy(k, slot):
        return pltpu.make_async_remote_copy(
            src_ref=vbuf.at[slot], dst_ref=vbuf.at[slot], send_sem=fsend.at[k], recv_sem=vrecv.at[slot],
            device_id=(partner, o), device_id_type=MESH_ID,
        )

    own = pltpu.make_async_remote_copy(
        src_ref=v_ref, dst_ref=vbuf.at[r], send_sem=fsend.at[0], recv_sem=vrecv.at[r],
        device_id=(partner, o), device_id_type=MESH_ID,
    )
    own.start()

    def send(k, carry):
        v_copy(k, ((chip + k) % chips) * 2 + core, r).start()
        return carry

    lax.fori_loop(1, chips, send, 0)

    def send_seg(k, carry):
        s_copy(k, (r + k) % n_rows, r).start()
        return carry

    lax.fori_loop(1, n_rows, send_seg, 0)
    acc_ref[...] = jnp.zeros_like(acc_ref)
    block_hist(acc_ref, v_ref[...], seg_ref[r].astype(jnp.int32), nodes)

    def take_direct(k, carry):
        src = ((chip + chips - k) % chips) * 2 + core
        v_copy(k, src, src).wait_recv()
        f_copy(k, src).start()
        s_copy(k, src, src).wait_recv()
        block_hist(acc_ref, vbuf[src], sbuf[src].astype(jnp.int32), nodes)
        return carry

    lax.fori_loop(1, chips, take_direct, 0)

    def take_forwarded(k, carry):
        src = ((chip + chips - k) % chips) * 2 + 1 - core
        f_copy(k, src).wait_recv()
        s_copy(k, src, src).wait_recv()
        block_hist(acc_ref, vbuf[src], sbuf[src].astype(jnp.int32), nodes)
        return carry

    lax.fori_loop(0, chips, take_forwarded, 0)

    def drain(k, carry):
        s_copy(k, (r + k) % n_rows, r).wait_send()
        return carry

    lax.fori_loop(1, n_rows, drain, 0)

    def drain_v(k, carry):
        v_copy(k, ((chip + k) % chips) * 2 + core, r).wait_send()
        return carry

    lax.fori_loop(1, chips, drain_v, 0)
    own.wait_send()

    def drain_f(k, carry):
        f_copy(k, ((chip + chips - k) % chips) * 2 + core).wait_send()
        return carry

    lax.fori_loop(1, chips, drain_f, 0)


def gather_hist(seg_p, v_loc, nodes):
    n_rows, width, half = seg_p.shape
    vw, rows = v_loc.shape
    feats = width // 2
    out_rows = vw * nodes
    cols = feats * BINS
    total = n_rows * rows
    return pl.pallas_call(
        functools.partial(gather_hist_kernel, nodes=nodes),
        out_shape=jax.ShapeDtypeStruct((out_rows, cols), jnp.float32),
        in_specs=[pl.BlockSpec(memory_space=pltpu.VMEM)] * 2,
        out_specs=pl.BlockSpec(memory_space=pltpu.VMEM),
        scratch_shapes=[
            pltpu.VMEM((n_rows, vw, rows), v_loc.dtype),
            pltpu.VMEM((n_rows, width, half), seg_p.dtype),
            pltpu.SemaphoreType.DMA((n_rows // 2,)),
            pltpu.SemaphoreType.DMA((n_rows // 2,)),
            pltpu.SemaphoreType.DMA((n_rows,)),
            pltpu.SemaphoreType.DMA((n_rows,)),
            pltpu.SemaphoreType.DMA((n_rows,)),
        ],
        compiler_params=pltpu.CompilerParams(collective_id=1, has_side_effects=True),
        cost_estimate=pl.CostEstimate(
            flops=2 * out_rows * cols * total,
            bytes_accessed=total * (vw * 2 + feats * 2) + out_rows * cols * 4,
            transcendentals=0,
        ),
    )(seg_p, v_loc)


def local(codes, node_of_row, grad, hess, small_side, evicted, parent_hist):
    pairs = small_side.shape[0]
    nodes = 2 * pairs
    local_targets = grad.shape[1]
    targets = local_targets * lax.axis_size("outs")
    n_rows = lax.axis_size("rows")
    count, features = codes.shape
    feats = features // n_rows
    half = count // 2
    seg = (node_of_row[:, None] * BINS + codes).astype(jnp.int16)
    seg_p = jnp.transpose(seg.reshape(2, half, n_rows, feats), (2, 3, 0, 1)).reshape(n_rows, 2 * feats, half)
    v_loc = jnp.concatenate([grad.T, hess.T], axis=0)
    span = feats * BINS
    built = gather_hist(seg_p, v_loc, nodes).reshape(2, nodes, local_targets, span)
    small = (small_side == 0)[None, :, None, None]
    pair_view = built.reshape(2, pairs, 2, local_targets, span)
    child = jnp.where(small, pair_view[:, :, 0], pair_view[:, :, 1])
    rebuilt = jnp.where(small, pair_view[:, :, 1], pair_view[:, :, 0])
    gone = (evicted == 1)[None, :, None, None]
    sibling = jnp.where(gone, rebuilt, parent_hist - child)
    first = jnp.where(small, child, sibling)
    second = jnp.where(small, sibling, child)
    node_hist = jnp.stack([first, second], axis=2).reshape(2, nodes, local_targets, span)
    partial_gain = gain_terms(node_hist)
    split_gain, best = exchange_gains(partial_gain, targets)
    best_gain = best[:, 0]
    return (node_hist, split_gain, best_gain)


def solution(mesh):
    return jax.shard_map(
        local,
        mesh=mesh,
        in_specs=(
            P("rows", None),
            P("rows"),
            P("rows", "outs"),
            P("rows", "outs"),
            P(),
            P(),
            P(None, None, "outs", "rows"),
        ),
        out_specs=(P(None, None, "outs", "rows"), P(None, "rows"), P()),
        check_vma=False,
    )
```

```python
import functools

import jax
import jax.numpy as jnp
import numpy as np
from jax import lax
from jax.experimental import pallas as pl
from jax.experimental.pallas import tpu as pltpu
from jax.sharding import PartitionSpec as P

BINS = 32


MESH_ID = pl.DeviceIdType.MESH


def row_stages(r, n_rows):
    chips = n_rows // 2
    nx = 4 if chips % 4 == 0 else chips
    ny = chips // nx
    chip = r // 2
    core = r % 2
    y = chip // nx
    x = chip % nx
    stages = [
        [chip * 2 + 1 - core],
        [(y * nx + (x + k) % nx) * 2 + core for k in range(1, nx)],
        [(((y + k) % ny) * nx + x) * 2 + core for k in range(1, ny)],
    ]
    return [stage for stage in stages if stage]


def row_peers(r, n_rows):
    return [peer for stage in row_stages(r, n_rows) for peer in stage]


def exchange(partial, split_ref, best_ref, gbuf, mbuf, gsend, grecv, msend, mrecv, targets):
    n_rows = lax.axis_size("rows")
    n_outs = lax.axis_size("outs")
    r = lax.axis_index("rows")
    o = lax.axis_index("outs")
    gbuf[o] = partial
    sends = []
    for k in range(1, n_outs):
        copy = pltpu.make_async_remote_copy(
            src_ref=gbuf.at[o],
            dst_ref=gbuf.at[o],
            send_sem=gsend.at[k],
            recv_sem=grecv.at[o],
            device_id=(r, (o + k) % n_outs),
            device_id_type=MESH_ID,
        )
        copy.start()
        sends.append(copy)
    for k in range(1, n_outs):
        src = (o + n_outs - k) % n_outs
        pltpu.make_async_remote_copy(
            src_ref=gbuf.at[o],
            dst_ref=gbuf.at[src],
            send_sem=gsend.at[k],
            recv_sem=grecv.at[src],
            device_id=(r, src),
            device_id_type=MESH_ID,
        ).wait_recv()
    for copy in sends:
        copy.wait_send()
    acc = gbuf[0]
    for j in range(1, n_outs):
        acc = acc + gbuf[j]
    split = acc / targets
    split_ref[...] = split
    width = mbuf.shape[2]
    best = jnp.broadcast_to(jnp.max(split, axis=1, keepdims=True), (split.shape[0], width))
    base = 0
    for peers in row_stages(r, n_rows):
        mbuf[base] = best
        sends = []
        for j, peer in enumerate(peers):
            copy = pltpu.make_async_remote_copy(
                src_ref=mbuf.at[base],
                dst_ref=mbuf.at[base + 1 + j],
                send_sem=msend.at[base + 1 + j],
                recv_sem=mrecv.at[base + 1 + j],
                device_id=(peer, o),
                device_id_type=MESH_ID,
            )
            copy.start()
            sends.append(copy)
        for copy in sends:
            copy.wait_recv()
        for copy in sends:
            copy.wait_send()
        for j in range(len(peers)):
            best = jnp.maximum(best, mbuf[base + 1 + j])
        base += len(peers) + 1
    best_ref[...] = best


def block_hist(acc_ref, v, s, nodes):
    tl = v.shape[0] // 2
    half = s.shape[1]
    feats = s.shape[0] // 2
    one = jnp.ones((), jnp.bfloat16)
    zero = jnp.zeros((), jnp.bfloat16)
    bins = lax.broadcasted_iota(jnp.int32, (BINS, half), 0)
    for h in range(2):
        vh = v[:, h * half : (h + 1) * half]
        node = s[h : h + 1] >> 5
        onehot = jnp.concatenate(
            [jnp.where((s[2 * f + h : 2 * f + h + 1] & (BINS - 1)) == bins, one, zero) for f in range(feats)],
            axis=0,
        )
        blocks = []
        for c in range(2):
            vc = vh[c * tl : (c + 1) * tl]
            for n in range(nodes):
                blocks.append(jnp.where(node == n, vc, zero))
        vals = jnp.concatenate(blocks, axis=0)
        acc_ref[...] += lax.dot_general(
            vals, onehot, (((1,), (1,)), ((), ())), preferred_element_type=jnp.float32
        )


def gather_hist_kernel(
    small_ref, evict_ref, seg_ref, v_ref, parent_ref, hist_ref, split_ref, best_ref,
    acc_ref, vbuf, sbuf, vsend, fsend, vrecv, ssend, srecv, gbuf, mbuf, gsend, grecv, msend, mrecv,
    *, nodes, targets,
):
    n_rows = lax.axis_size("rows")
    chips = n_rows // 2
    r = lax.axis_index("rows")
    o = lax.axis_index("outs")
    core = r % 2
    chip = r // 2
    partner = chip * 2 + 1 - core
    barrier = pltpu.get_barrier_semaphore()

    def greet(k, carry):
        pl.semaphore_signal(barrier, 1, device_id=((r + k) % n_rows, o), device_id_type=MESH_ID)
        return carry

    lax.fori_loop(1, n_rows, greet, 0)
    n_outs = lax.axis_size("outs")
    for k in range(1, n_outs):
        pl.semaphore_signal(barrier, 1, device_id=(r, (o + k) % n_outs), device_id_type=MESH_ID)
    pl.semaphore_wait(barrier, n_rows - 1 + n_outs - 1)

    def s_copy(k, peer, slot):
        return pltpu.make_async_remote_copy(
            src_ref=seg_ref.at[peer], dst_ref=sbuf.at[slot], send_sem=ssend.at[k], recv_sem=srecv.at[slot],
            device_id=(peer, o), device_id_type=MESH_ID,
        )

    def v_copy(k, peer, slot):
        return pltpu.make_async_remote_copy(
            src_ref=v_ref, dst_ref=vbuf.at[slot], send_sem=vsend.at[k], recv_sem=vrecv.at[slot],
            device_id=(peer, o), device_id_type=MESH_ID,
        )

    def f_copy(k, slot):
        return pltpu.make_async_remote_copy(
            src_ref=vbuf.at[slot], dst_ref=vbuf.at[slot], send_sem=fsend.at[k], recv_sem=vrecv.at[slot],
            device_id=(partner, o), device_id_type=MESH_ID,
        )

    own = pltpu.make_async_remote_copy(
        src_ref=v_ref, dst_ref=vbuf.at[r], send_sem=fsend.at[0], recv_sem=vrecv.at[r],
        device_id=(partner, o), device_id_type=MESH_ID,
    )
    own.start()

    def send(k, carry):
        v_copy(k, ((chip + k) % chips) * 2 + core, r).start()
        return carry

    lax.fori_loop(1, chips, send, 0)

    def send_seg(k, carry):
        s_copy(k, (r + k) % n_rows, r).start()
        return carry

    lax.fori_loop(1, n_rows, send_seg, 0)
    acc_ref[...] = jnp.zeros_like(acc_ref)
    block_hist(acc_ref, v_ref[...], seg_ref[r].astype(jnp.int32), nodes)

    def take_direct(k, carry):
        src = ((chip + chips - k) % chips) * 2 + core
        v_copy(k, src, src).wait_recv()
        f_copy(k, src).start()
        s_copy(k, src, src).wait_recv()
        block_hist(acc_ref, vbuf[src], sbuf[src].astype(jnp.int32), nodes)
        return carry

    lax.fori_loop(1, chips, take_direct, 0)

    def take_forwarded(k, carry):
        src = ((chip + chips - k) % chips) * 2 + 1 - core
        f_copy(k, src).wait_recv()
        s_copy(k, src, src).wait_recv()
        block_hist(acc_ref, vbuf[src], sbuf[src].astype(jnp.int32), nodes)
        return carry

    lax.fori_loop(0, chips, take_forwarded, 0)

    def drain(k, carry):
        s_copy(k, (r + k) % n_rows, r).wait_send()
        return carry

    lax.fori_loop(1, n_rows, drain, 0)

    def drain_v(k, carry):
        v_copy(k, ((chip + k) % chips) * 2 + core, r).wait_send()
        return carry

    lax.fori_loop(1, chips, drain_v, 0)
    own.wait_send()

    def drain_f(k, carry):
        f_copy(k, ((chip + chips - k) % chips) * 2 + core).wait_send()
        return carry

    lax.fori_loop(1, chips, drain_f, 0)

    node_hist(acc_ref, parent_ref, small_ref, evict_ref, hist_ref, nodes)
    partial = gain_terms(hist_ref, nodes)
    exchange(partial, split_ref, best_ref, gbuf, mbuf, gsend, grecv, msend, mrecv, targets)


def node_hist(acc_ref, parent_ref, small_ref, evict_ref, hist_ref, nodes):
    pairs = nodes // 2
    tl = acc_ref.shape[0] // (2 * nodes)
    for c in range(2):
        for p in range(pairs):
            lo = c * nodes * tl + 2 * p * tl
            a = acc_ref[lo : lo + tl]
            b = acc_ref[lo + tl : lo + 2 * tl]
            base = (c * pairs + p) * tl
            parent = parent_ref[base : base + tl]
            small = small_ref[p] == 0
            gone = evict_ref[p] == 1
            child = jnp.where(small, a, b)
            rebuilt = jnp.where(small, b, a)
            sibling = jnp.where(gone, rebuilt, parent - child)
            hist_ref[lo : lo + tl] = jnp.where(small, child, sibling)
            hist_ref[lo + tl : lo + 2 * tl] = jnp.where(small, sibling, child)


def group_scan(x, reverse):
    span = x.shape[1]
    lane = lax.broadcasted_iota(jnp.int32, x.shape, 1) % BINS
    shift = 1
    while shift < BINS:
        if reverse:
            moved = pltpu.roll(x, span - shift, 1)
            x = x + jnp.where(lane + shift < BINS, moved, 0.0)
        else:
            moved = pltpu.roll(x, shift, 1)
            x = x + jnp.where(lane >= shift, moved, 0.0)
        shift *= 2
    return x


def gain_terms(hist_ref, nodes):
    rows, span = hist_ref.shape
    half = rows // 2
    tl = half // nodes
    lane = lax.broadcasted_iota(jnp.int32, (half, span), 1) % BINS
    left_g = group_scan(hist_ref[0:half], False)
    left_h = group_scan(hist_ref[half:rows], False)
    total_g = group_scan(jnp.where(lane == BINS - 1, left_g, 0.0), True)
    total_h = group_scan(jnp.where(lane == BINS - 1, left_h, 0.0), True)

    def score(a, s):
        return a * a / (jnp.maximum(s, 0.0) + 1.0)

    gain = (
        score(left_g, left_h) + score(total_g - left_g, total_h - left_h) - score(total_g, total_h)
    )
    return jnp.sum(gain.reshape(nodes, tl, span), axis=1)


def gather_hist(small_side, evicted, seg_p, v_loc, parent, nodes, targets):
    n_rows, width, half = seg_p.shape
    n_outs = lax.axis_size("outs")
    vw, rows = v_loc.shape
    feats = width // 2
    out_rows = vw * nodes
    cols = feats * BINS
    total = n_rows * rows
    vmem = pl.BlockSpec(memory_space=pltpu.VMEM)
    smem = pl.BlockSpec(memory_space=pltpu.SMEM)
    return pl.pallas_call(
        functools.partial(gather_hist_kernel, nodes=nodes, targets=targets),
        out_shape=(
            jax.ShapeDtypeStruct((out_rows, cols), jnp.float32),
            jax.ShapeDtypeStruct((nodes, cols), jnp.float32),
            jax.ShapeDtypeStruct((nodes, 128), jnp.float32),
        ),
        in_specs=[smem, smem, vmem, vmem, vmem],
        out_specs=(vmem, vmem, vmem),
        scratch_shapes=[
            pltpu.VMEM((out_rows, cols), jnp.float32),
            pltpu.VMEM((n_rows, vw, rows), v_loc.dtype),
            pltpu.VMEM((n_rows, width, half), seg_p.dtype),
            pltpu.SemaphoreType.DMA((n_rows // 2,)),
            pltpu.SemaphoreType.DMA((n_rows // 2,)),
            pltpu.SemaphoreType.DMA((n_rows,)),
            pltpu.SemaphoreType.DMA((n_rows,)),
            pltpu.SemaphoreType.DMA((n_rows,)),
            pltpu.VMEM((n_outs, nodes, cols), jnp.float32),
            pltpu.VMEM((n_rows, nodes, 128), jnp.float32),
            pltpu.SemaphoreType.DMA((n_outs,)),
            pltpu.SemaphoreType.DMA((n_outs,)),
            pltpu.SemaphoreType.DMA((n_rows,)),
            pltpu.SemaphoreType.DMA((n_rows,)),
        ],
        compiler_params=pltpu.CompilerParams(collective_id=1, has_side_effects=True),
        cost_estimate=pl.CostEstimate(
            flops=2 * out_rows * cols * total,
            bytes_accessed=total * (vw * 2 + feats * 2) + out_rows * cols * 4,
            transcendentals=0,
        ),
    )(small_side, evicted, seg_p, v_loc, parent)


def local(codes, node_of_row, grad, hess, small_side, evicted, parent_hist):
    pairs = small_side.shape[0]
    nodes = 2 * pairs
    local_targets = grad.shape[1]
    targets = local_targets * lax.axis_size("outs")
    n_rows = lax.axis_size("rows")
    count, features = codes.shape
    feats = features // n_rows
    half = count // 2
    seg = (node_of_row[:, None] * BINS + codes).astype(jnp.int16)
    seg_p = jnp.transpose(seg.reshape(2, half, n_rows, feats), (2, 3, 0, 1)).reshape(n_rows, 2 * feats, half)
    v_loc = jnp.concatenate([grad.T, hess.T], axis=0)
    span = feats * BINS
    parent = parent_hist.reshape(2 * pairs * local_targets, span)
    hist, split_gain, best = gather_hist(small_side, evicted, seg_p, v_loc, parent, nodes, targets)
    node_hist = hist.reshape(2, nodes, local_targets, span)
    return (node_hist, split_gain, best[:, 0])


def solution(mesh):
    return jax.shard_map(
        local,
        mesh=mesh,
        in_specs=(
            P("rows", None),
            P("rows"),
            P("rows", "outs"),
            P("rows", "outs"),
            P(),
            P(),
            P(None, None, "outs", "rows"),
        ),
        out_specs=(P(None, None, "outs", "rows"), P(None, "rows"), P()),
        check_vma=False,
    )
```

```python
import functools

import jax
import jax.numpy as jnp
import numpy as np
from jax import lax
from jax.experimental import pallas as pl
from jax.experimental.pallas import tpu as pltpu
from jax.sharding import PartitionSpec as P

BINS = 32


MESH_ID = pl.DeviceIdType.MESH


def row_stages(r, n_rows):
    chips = n_rows // 2
    nx = 4 if chips % 4 == 0 else chips
    ny = chips // nx
    chip = r // 2
    core = r % 2
    y = chip // nx
    x = chip % nx
    row = 2 * nx
    stages = [
        [y * row + (r - y * row + k) % row for k in range(1, row)],
        [(((y + k) % ny) * nx + x) * 2 + core for k in range(1, ny)],
    ]
    return [stage for stage in stages if stage]


def row_peers(r, n_rows):
    return [peer for stage in row_stages(r, n_rows) for peer in stage]


def exchange(partial, split_ref, best_ref, gbuf, mbuf, gsend, grecv, msend, mrecv, targets):
    n_rows = lax.axis_size("rows")
    n_outs = lax.axis_size("outs")
    r = lax.axis_index("rows")
    o = lax.axis_index("outs")
    gbuf[o] = partial
    sends = []
    for k in range(1, n_outs):
        copy = pltpu.make_async_remote_copy(
            src_ref=gbuf.at[o],
            dst_ref=gbuf.at[o],
            send_sem=gsend.at[k],
            recv_sem=grecv.at[o],
            device_id=(r, (o + k) % n_outs),
            device_id_type=MESH_ID,
        )
        copy.start()
        sends.append(copy)
    for k in range(1, n_outs):
        src = (o + n_outs - k) % n_outs
        pltpu.make_async_remote_copy(
            src_ref=gbuf.at[o],
            dst_ref=gbuf.at[src],
            send_sem=gsend.at[k],
            recv_sem=grecv.at[src],
            device_id=(r, src),
            device_id_type=MESH_ID,
        ).wait_recv()
    for copy in sends:
        copy.wait_send()
    acc = gbuf[0]
    for j in range(1, n_outs):
        acc = acc + gbuf[j]
    split = acc / targets
    split_ref[...] = split
    width = mbuf.shape[2]
    best = jnp.broadcast_to(jnp.max(split, axis=1, keepdims=True), (split.shape[0], width))
    base = 0
    for peers in row_stages(r, n_rows):
        mbuf[base] = best
        sends = []
        for j, peer in enumerate(peers):
            copy = pltpu.make_async_remote_copy(
                src_ref=mbuf.at[base],
                dst_ref=mbuf.at[base + 1 + j],
                send_sem=msend.at[base + 1 + j],
                recv_sem=mrecv.at[base + 1 + j],
                device_id=(peer, o),
                device_id_type=MESH_ID,
            )
            copy.start()
            sends.append(copy)
        for copy in sends:
            copy.wait_recv()
        for copy in sends:
            copy.wait_send()
        for j in range(len(peers)):
            best = jnp.maximum(best, mbuf[base + 1 + j])
        base += len(peers) + 1
    best_ref[...] = best


def block_hist(acc_ref, v, s, nodes):
    tl = v.shape[0] // 2
    half = s.shape[1]
    feats = s.shape[0] // 2
    one = jnp.ones((), jnp.bfloat16)
    zero = jnp.zeros((), jnp.bfloat16)
    bins = lax.broadcasted_iota(jnp.int32, (BINS, half), 0)
    for h in range(2):
        vh = v[:, h * half : (h + 1) * half]
        node = s[h : h + 1] >> 5
        onehot = jnp.concatenate(
            [jnp.where((s[2 * f + h : 2 * f + h + 1] & (BINS - 1)) == bins, one, zero) for f in range(feats)],
            axis=0,
        )
        blocks = []
        for c in range(2):
            vc = vh[c * tl : (c + 1) * tl]
            for n in range(nodes):
                blocks.append(jnp.where(node == n, vc, zero))
        vals = jnp.concatenate(blocks, axis=0)
        acc_ref[...] += lax.dot_general(
            vals, onehot, (((1,), (1,)), ((), ())), preferred_element_type=jnp.float32
        )


def gather_hist_kernel(
    small_ref, evict_ref, seg_ref, v_ref, parent_ref, hist_ref, split_ref, best_ref,
    acc_ref, vbuf, sbuf, vsend, fsend, vrecv, ssend, srecv, gbuf, mbuf, gsend, grecv, msend, mrecv,
    *, nodes, targets,
):
    n_rows = lax.axis_size("rows")
    chips = n_rows // 2
    r = lax.axis_index("rows")
    o = lax.axis_index("outs")
    core = r % 2
    chip = r // 2
    partner = chip * 2 + 1 - core
    barrier = pltpu.get_barrier_semaphore()

    def greet(k, carry):
        pl.semaphore_signal(barrier, 1, device_id=((r + k) % n_rows, o), device_id_type=MESH_ID)
        return carry

    lax.fori_loop(1, n_rows, greet, 0)
    n_outs = lax.axis_size("outs")
    for k in range(1, n_outs):
        pl.semaphore_signal(barrier, 1, device_id=(r, (o + k) % n_outs), device_id_type=MESH_ID)
    acc_ref[...] = jnp.zeros_like(acc_ref)
    block_hist(acc_ref, v_ref[...], seg_ref[r].astype(jnp.int32), nodes)
    pl.semaphore_wait(barrier, n_rows - 1 + n_outs - 1)

    def s_copy(k, peer, slot):
        return pltpu.make_async_remote_copy(
            src_ref=seg_ref.at[peer], dst_ref=sbuf.at[slot], send_sem=ssend.at[k], recv_sem=srecv.at[slot],
            device_id=(peer, o), device_id_type=MESH_ID,
        )

    def v_copy(k, peer, slot):
        return pltpu.make_async_remote_copy(
            src_ref=v_ref, dst_ref=vbuf.at[slot], send_sem=vsend.at[k], recv_sem=vrecv.at[slot],
            device_id=(peer, o), device_id_type=MESH_ID,
        )

    def f_copy(k, slot):
        return pltpu.make_async_remote_copy(
            src_ref=vbuf.at[slot], dst_ref=vbuf.at[slot], send_sem=fsend.at[k], recv_sem=vrecv.at[slot],
            device_id=(partner, o), device_id_type=MESH_ID,
        )

    own = pltpu.make_async_remote_copy(
        src_ref=v_ref, dst_ref=vbuf.at[r], send_sem=fsend.at[0], recv_sem=vrecv.at[r],
        device_id=(partner, o), device_id_type=MESH_ID,
    )
    own.start()

    def send(k, carry):
        v_copy(k, ((chip + k) % chips) * 2 + core, r).start()
        return carry

    lax.fori_loop(1, chips, send, 0)

    def send_seg(k, carry):
        s_copy(k, (r + k) % n_rows, r).start()
        return carry

    lax.fori_loop(1, n_rows, send_seg, 0)

    def take_direct(k, carry):
        src = ((chip + chips - k) % chips) * 2 + core
        v_copy(k, src, src).wait_recv()
        f_copy(k, src).start()
        s_copy(k, src, src).wait_recv()
        block_hist(acc_ref, vbuf[src], sbuf[src].astype(jnp.int32), nodes)
        return carry

    lax.fori_loop(1, chips, take_direct, 0)

    def take_forwarded(k, carry):
        src = ((chip + chips - k) % chips) * 2 + 1 - core
        f_copy(k, src).wait_recv()
        s_copy(k, src, src).wait_recv()
        block_hist(acc_ref, vbuf[src], sbuf[src].astype(jnp.int32), nodes)
        return carry

    lax.fori_loop(0, chips, take_forwarded, 0)

    def drain(k, carry):
        s_copy(k, (r + k) % n_rows, r).wait_send()
        return carry

    lax.fori_loop(1, n_rows, drain, 0)

    def drain_v(k, carry):
        v_copy(k, ((chip + k) % chips) * 2 + core, r).wait_send()
        return carry

    lax.fori_loop(1, chips, drain_v, 0)
    own.wait_send()

    def drain_f(k, carry):
        f_copy(k, ((chip + chips - k) % chips) * 2 + core).wait_send()
        return carry

    lax.fori_loop(1, chips, drain_f, 0)

    node_hist(acc_ref, parent_ref, small_ref, evict_ref, hist_ref, nodes)
    partial = gain_terms(hist_ref, nodes)
    exchange(partial, split_ref, best_ref, gbuf, mbuf, gsend, grecv, msend, mrecv, targets)


def node_hist(acc_ref, parent_ref, small_ref, evict_ref, hist_ref, nodes):
    pairs = nodes // 2
    tl = acc_ref.shape[0] // (2 * nodes)
    for c in range(2):
        for p in range(pairs):
            lo = c * nodes * tl + 2 * p * tl
            a = acc_ref[lo : lo + tl]
            b = acc_ref[lo + tl : lo + 2 * tl]
            base = (c * pairs + p) * tl
            parent = parent_ref[base : base + tl]
            small = small_ref[p] == 0
            gone = evict_ref[p] == 1
            child = jnp.where(small, a, b)
            rebuilt = jnp.where(small, b, a)
            sibling = jnp.where(gone, rebuilt, parent - child)
            hist_ref[lo : lo + tl] = jnp.where(small, child, sibling)
            hist_ref[lo + tl : lo + 2 * tl] = jnp.where(small, sibling, child)


def group_scan(x, reverse):
    span = x.shape[1]
    lane = lax.broadcasted_iota(jnp.int32, x.shape, 1) % BINS
    shift = 1
    while shift < BINS:
        if reverse:
            moved = pltpu.roll(x, span - shift, 1)
            x = x + jnp.where(lane + shift < BINS, moved, 0.0)
        else:
            moved = pltpu.roll(x, shift, 1)
            x = x + jnp.where(lane >= shift, moved, 0.0)
        shift *= 2
    return x


def gain_terms(hist_ref, nodes):
    rows, span = hist_ref.shape
    half = rows // 2
    tl = half // nodes
    lane = lax.broadcasted_iota(jnp.int32, (half, span), 1) % BINS
    left_g = group_scan(hist_ref[0:half], False)
    left_h = group_scan(hist_ref[half:rows], False)
    total_g = group_scan(jnp.where(lane == BINS - 1, left_g, 0.0), True)
    total_h = group_scan(jnp.where(lane == BINS - 1, left_h, 0.0), True)

    def score(a, s):
        return a * a / (jnp.maximum(s, 0.0) + 1.0)

    gain = (
        score(left_g, left_h) + score(total_g - left_g, total_h - left_h) - score(total_g, total_h)
    )
    return jnp.sum(gain.reshape(nodes, tl, span), axis=1)


def gather_hist(small_side, evicted, seg_p, v_loc, parent, nodes, targets):
    n_rows, width, half = seg_p.shape
    n_outs = lax.axis_size("outs")
    vw, rows = v_loc.shape
    feats = width // 2
    out_rows = vw * nodes
    cols = feats * BINS
    total = n_rows * rows
    vmem = pl.BlockSpec(memory_space=pltpu.VMEM)
    smem = pl.BlockSpec(memory_space=pltpu.SMEM)
    return pl.pallas_call(
        functools.partial(gather_hist_kernel, nodes=nodes, targets=targets),
        out_shape=(
            jax.ShapeDtypeStruct((out_rows, cols), jnp.float32),
            jax.ShapeDtypeStruct((nodes, cols), jnp.float32),
            jax.ShapeDtypeStruct((nodes, 128), jnp.float32),
        ),
        in_specs=[smem, smem, vmem, vmem, vmem],
        out_specs=(vmem, vmem, vmem),
        scratch_shapes=[
            pltpu.VMEM((out_rows, cols), jnp.float32),
            pltpu.VMEM((n_rows, vw, rows), v_loc.dtype),
            pltpu.VMEM((n_rows, width, half), seg_p.dtype),
            pltpu.SemaphoreType.DMA((n_rows // 2,)),
            pltpu.SemaphoreType.DMA((n_rows // 2,)),
            pltpu.SemaphoreType.DMA((n_rows,)),
            pltpu.SemaphoreType.DMA((n_rows,)),
            pltpu.SemaphoreType.DMA((n_rows,)),
            pltpu.VMEM((n_outs, nodes, cols), jnp.float32),
            pltpu.VMEM((n_rows, nodes, 128), jnp.float32),
            pltpu.SemaphoreType.DMA((n_outs,)),
            pltpu.SemaphoreType.DMA((n_outs,)),
            pltpu.SemaphoreType.DMA((n_rows,)),
            pltpu.SemaphoreType.DMA((n_rows,)),
        ],
        compiler_params=pltpu.CompilerParams(collective_id=1, has_side_effects=True),
        cost_estimate=pl.CostEstimate(
            flops=2 * out_rows * cols * total,
            bytes_accessed=total * (vw * 2 + feats * 2) + out_rows * cols * 4,
            transcendentals=0,
        ),
    )(small_side, evicted, seg_p, v_loc, parent)


def local(codes, node_of_row, grad, hess, small_side, evicted, parent_hist):
    pairs = small_side.shape[0]
    nodes = 2 * pairs
    local_targets = grad.shape[1]
    targets = local_targets * lax.axis_size("outs")
    n_rows = lax.axis_size("rows")
    count, features = codes.shape
    feats = features // n_rows
    half = count // 2
    seg = (node_of_row[:, None] * BINS + codes).astype(jnp.int16)
    seg_p = jnp.transpose(seg.reshape(2, half, n_rows, feats), (2, 3, 0, 1)).reshape(n_rows, 2 * feats, half)
    v_loc = jnp.concatenate([grad.T, hess.T], axis=0)
    span = feats * BINS
    parent = parent_hist.reshape(2 * pairs * local_targets, span)
    hist, split_gain, best = gather_hist(small_side, evicted, seg_p, v_loc, parent, nodes, targets)
    node_hist = hist.reshape(2, nodes, local_targets, span)
    return (node_hist, split_gain, best[:, 0])


def solution(mesh):
    return jax.shard_map(
        local,
        mesh=mesh,
        in_specs=(
            P("rows", None),
            P("rows"),
            P("rows", "outs"),
            P("rows", "outs"),
            P(),
            P(),
            P(None, None, "outs", "rows"),
        ),
        out_specs=(P(None, None, "outs", "rows"), P(None, "rows"), P()),
        check_vma=False,
    )
```

```python
import functools

import jax
import jax.numpy as jnp
import numpy as np
from jax import lax
from jax.experimental import pallas as pl
from jax.experimental.pallas import tpu as pltpu
from jax.sharding import PartitionSpec as P

BINS = 32


MESH_ID = pl.DeviceIdType.MESH


def row_stages(r, n_rows):
    chips = n_rows // 2
    nx = 4 if chips % 4 == 0 else chips
    ny = chips // nx
    chip = r // 2
    core = r % 2
    y = chip // nx
    x = chip % nx
    row = 2 * nx
    stages = [
        [y * row + (r - y * row + k) % row for k in range(1, row)],
        [(((y + k) % ny) * nx + x) * 2 + core for k in range(1, ny)],
    ]
    return [stage for stage in stages if stage]


def row_peers(r, n_rows):
    return [peer for stage in row_stages(r, n_rows) for peer in stage]


def exchange(partial, split_ref, best_ref, gbuf, mbuf, gsend, grecv, msend, mrecv, targets):
    n_rows = lax.axis_size("rows")
    n_outs = lax.axis_size("outs")
    r = lax.axis_index("rows")
    o = lax.axis_index("outs")
    gbuf[o] = partial
    sends = []
    for k in range(1, n_outs):
        copy = pltpu.make_async_remote_copy(
            src_ref=gbuf.at[o],
            dst_ref=gbuf.at[o],
            send_sem=gsend.at[k],
            recv_sem=grecv.at[o],
            device_id=(r, (o + k) % n_outs),
            device_id_type=MESH_ID,
        )
        copy.start()
        sends.append(copy)
    for k in range(1, n_outs):
        src = (o + n_outs - k) % n_outs
        pltpu.make_async_remote_copy(
            src_ref=gbuf.at[o],
            dst_ref=gbuf.at[src],
            send_sem=gsend.at[k],
            recv_sem=grecv.at[src],
            device_id=(r, src),
            device_id_type=MESH_ID,
        ).wait_recv()
    for copy in sends:
        copy.wait_send()
    acc = gbuf[0]
    for j in range(1, n_outs):
        acc = acc + gbuf[j]
    split = acc / targets
    split_ref[...] = split
    width = mbuf.shape[2]
    best = jnp.broadcast_to(jnp.max(split, axis=1, keepdims=True), (split.shape[0], width))
    base = 0
    for peers in row_stages(r, n_rows):
        mbuf[base] = best
        sends = []
        for j, peer in enumerate(peers):
            copy = pltpu.make_async_remote_copy(
                src_ref=mbuf.at[base],
                dst_ref=mbuf.at[base + 1 + j],
                send_sem=msend.at[base + 1 + j],
                recv_sem=mrecv.at[base + 1 + j],
                device_id=(peer, o),
                device_id_type=MESH_ID,
            )
            copy.start()
            sends.append(copy)
        for copy in sends:
            copy.wait_recv()
        for copy in sends:
            copy.wait_send()
        for j in range(len(peers)):
            best = jnp.maximum(best, mbuf[base + 1 + j])
        base += len(peers) + 1
    best_ref[...] = best


def block_hist(acc_ref, v, s, nodes):
    tl = v.shape[0] // 2
    half = s.shape[1]
    feats = s.shape[0] // 2
    one = jnp.ones((), jnp.bfloat16)
    zero = jnp.zeros((), jnp.bfloat16)
    bins = lax.broadcasted_iota(jnp.int32, (BINS, half), 0)
    for h in range(2):
        vh = v[:, h * half : (h + 1) * half]
        node = s[h : h + 1] >> 5
        onehot = jnp.concatenate(
            [jnp.where((s[2 * f + h : 2 * f + h + 1] & (BINS - 1)) == bins, one, zero) for f in range(feats)],
            axis=0,
        )
        blocks = []
        for c in range(2):
            vc = vh[c * tl : (c + 1) * tl]
            for n in range(nodes):
                blocks.append(jnp.where(node == n, vc, zero))
        vals = jnp.concatenate(blocks, axis=0)
        acc_ref[...] += lax.dot_general(
            vals, onehot, (((1,), (1,)), ((), ())), preferred_element_type=jnp.float32
        )


def gather_hist_kernel(
    small_ref, evict_ref, seg_ref, v_ref, parent_ref, hist_ref, split_ref, best_ref,
    acc_ref, vbuf, sbuf, vsend, fsend, vrecv, ssend, srecv, gbuf, mbuf, gsend, grecv, msend, mrecv,
    *, nodes, targets,
):
    n_rows = lax.axis_size("rows")
    chips = n_rows // 2
    r = lax.axis_index("rows")
    o = lax.axis_index("outs")
    core = r % 2
    chip = r // 2
    partner = chip * 2 + 1 - core
    barrier = pltpu.get_barrier_semaphore()

    def greet(k, carry):
        pl.semaphore_signal(barrier, 1, device_id=((r + k) % n_rows, o), device_id_type=MESH_ID)
        return carry

    lax.fori_loop(1, n_rows, greet, 0)
    n_outs = lax.axis_size("outs")
    for k in range(1, n_outs):
        pl.semaphore_signal(barrier, 1, device_id=(r, (o + k) % n_outs), device_id_type=MESH_ID)
    acc_ref[...] = jnp.zeros_like(acc_ref)
    block_hist(acc_ref, v_ref[...], seg_ref[r].astype(jnp.int32), nodes)
    pl.semaphore_wait(barrier, n_rows - 1 + n_outs - 1)

    def s_copy(k, peer, slot):
        return pltpu.make_async_remote_copy(
            src_ref=seg_ref.at[peer], dst_ref=sbuf.at[slot], send_sem=ssend.at[k], recv_sem=srecv.at[slot],
            device_id=(peer, o), device_id_type=MESH_ID,
        )

    def v_copy(k, peer, slot):
        return pltpu.make_async_remote_copy(
            src_ref=v_ref, dst_ref=vbuf.at[slot], send_sem=vsend.at[k], recv_sem=vrecv.at[slot],
            device_id=(peer, o), device_id_type=MESH_ID,
        )

    def f_copy(k, slot):
        return pltpu.make_async_remote_copy(
            src_ref=vbuf.at[slot], dst_ref=vbuf.at[slot], send_sem=fsend.at[k], recv_sem=vrecv.at[slot],
            device_id=(partner, o), device_id_type=MESH_ID,
        )

    own = pltpu.make_async_remote_copy(
        src_ref=v_ref, dst_ref=vbuf.at[r], send_sem=fsend.at[0], recv_sem=vrecv.at[r],
        device_id=(partner, o), device_id_type=MESH_ID,
    )
    own.start()

    def send(k, carry):
        v_copy(k, ((chip + k) % chips) * 2 + core, r).start()
        return carry

    lax.fori_loop(1, chips, send, 0)

    def send_seg(k, carry):
        s_copy(k, (r + k) % n_rows, r).start()
        return carry

    lax.fori_loop(1, n_rows, send_seg, 0)

    def take_forwarded(k):
        src = ((chip + chips - k) % chips) * 2 + 1 - core
        f_copy(k, src).wait_recv()
        s_copy(k, src, src).wait_recv()
        block_hist(acc_ref, vbuf[src], sbuf[src].astype(jnp.int32), nodes)

    def take(k, carry):
        src = ((chip + chips - k) % chips) * 2 + core
        v_copy(k, src, src).wait_recv()
        f_copy(k, src).start()
        s_copy(k, src, src).wait_recv()
        block_hist(acc_ref, vbuf[src], sbuf[src].astype(jnp.int32), nodes)
        take_forwarded(k)
        return carry

    take_forwarded(0)
    lax.fori_loop(1, chips, take, 0)

    def drain(k, carry):
        s_copy(k, (r + k) % n_rows, r).wait_send()
        return carry

    lax.fori_loop(1, n_rows, drain, 0)

    def drain_v(k, carry):
        v_copy(k, ((chip + k) % chips) * 2 + core, r).wait_send()
        return carry

    lax.fori_loop(1, chips, drain_v, 0)
    own.wait_send()

    def drain_f(k, carry):
        f_copy(k, ((chip + chips - k) % chips) * 2 + core).wait_send()
        return carry

    lax.fori_loop(1, chips, drain_f, 0)

    node_hist(acc_ref, parent_ref, small_ref, evict_ref, hist_ref, nodes)
    partial = gain_terms(hist_ref, nodes)
    exchange(partial, split_ref, best_ref, gbuf, mbuf, gsend, grecv, msend, mrecv, targets)


def node_hist(acc_ref, parent_ref, small_ref, evict_ref, hist_ref, nodes):
    pairs = nodes // 2
    tl = acc_ref.shape[0] // (2 * nodes)
    for c in range(2):
        for p in range(pairs):
            lo = c * nodes * tl + 2 * p * tl
            a = acc_ref[lo : lo + tl]
            b = acc_ref[lo + tl : lo + 2 * tl]
            base = (c * pairs + p) * tl
            parent = parent_ref[base : base + tl]
            small = small_ref[p] == 0
            gone = evict_ref[p] == 1
            child = jnp.where(small, a, b)
            rebuilt = jnp.where(small, b, a)
            sibling = jnp.where(gone, rebuilt, parent - child)
            hist_ref[lo : lo + tl] = jnp.where(small, child, sibling)
            hist_ref[lo + tl : lo + 2 * tl] = jnp.where(small, sibling, child)


def group_scan(x, reverse):
    span = x.shape[1]
    lane = lax.broadcasted_iota(jnp.int32, x.shape, 1) % BINS
    shift = 1
    while shift < BINS:
        if reverse:
            moved = pltpu.roll(x, span - shift, 1)
            x = x + jnp.where(lane + shift < BINS, moved, 0.0)
        else:
            moved = pltpu.roll(x, shift, 1)
            x = x + jnp.where(lane >= shift, moved, 0.0)
        shift *= 2
    return x


def gain_terms(hist_ref, nodes):
    rows, span = hist_ref.shape
    half = rows // 2
    tl = half // nodes
    lane = lax.broadcasted_iota(jnp.int32, (half, span), 1) % BINS
    left_g = group_scan(hist_ref[0:half], False)
    left_h = group_scan(hist_ref[half:rows], False)
    total_g = group_scan(jnp.where(lane == BINS - 1, left_g, 0.0), True)
    total_h = group_scan(jnp.where(lane == BINS - 1, left_h, 0.0), True)

    def score(a, s):
        return a * a / (jnp.maximum(s, 0.0) + 1.0)

    gain = (
        score(left_g, left_h) + score(total_g - left_g, total_h - left_h) - score(total_g, total_h)
    )
    return jnp.sum(gain.reshape(nodes, tl, span), axis=1)


def gather_hist(small_side, evicted, seg_p, v_loc, parent, nodes, targets):
    n_rows, width, half = seg_p.shape
    n_outs = lax.axis_size("outs")
    vw, rows = v_loc.shape
    feats = width // 2
    out_rows = vw * nodes
    cols = feats * BINS
    total = n_rows * rows
    vmem = pl.BlockSpec(memory_space=pltpu.VMEM)
    smem = pl.BlockSpec(memory_space=pltpu.SMEM)
    return pl.pallas_call(
        functools.partial(gather_hist_kernel, nodes=nodes, targets=targets),
        out_shape=(
            jax.ShapeDtypeStruct((out_rows, cols), jnp.float32),
            jax.ShapeDtypeStruct((nodes, cols), jnp.float32),
            jax.ShapeDtypeStruct((nodes, 128), jnp.float32),
        ),
        in_specs=[smem, smem, vmem, vmem, vmem],
        out_specs=(vmem, vmem, vmem),
        scratch_shapes=[
            pltpu.VMEM((out_rows, cols), jnp.float32),
            pltpu.VMEM((n_rows, vw, rows), v_loc.dtype),
            pltpu.VMEM((n_rows, width, half), seg_p.dtype),
            pltpu.SemaphoreType.DMA((n_rows // 2,)),
            pltpu.SemaphoreType.DMA((n_rows // 2,)),
            pltpu.SemaphoreType.DMA((n_rows,)),
            pltpu.SemaphoreType.DMA((n_rows,)),
            pltpu.SemaphoreType.DMA((n_rows,)),
            pltpu.VMEM((n_outs, nodes, cols), jnp.float32),
            pltpu.VMEM((n_rows, nodes, 128), jnp.float32),
            pltpu.SemaphoreType.DMA((n_outs,)),
            pltpu.SemaphoreType.DMA((n_outs,)),
            pltpu.SemaphoreType.DMA((n_rows,)),
            pltpu.SemaphoreType.DMA((n_rows,)),
        ],
        compiler_params=pltpu.CompilerParams(collective_id=1, has_side_effects=True),
        cost_estimate=pl.CostEstimate(
            flops=2 * out_rows * cols * total,
            bytes_accessed=total * (vw * 2 + feats * 2) + out_rows * cols * 4,
            transcendentals=0,
        ),
    )(small_side, evicted, seg_p, v_loc, parent)


def local(codes, node_of_row, grad, hess, small_side, evicted, parent_hist):
    pairs = small_side.shape[0]
    nodes = 2 * pairs
    local_targets = grad.shape[1]
    targets = local_targets * lax.axis_size("outs")
    n_rows = lax.axis_size("rows")
    count, features = codes.shape
    feats = features // n_rows
    half = count // 2
    seg = (node_of_row[:, None] * BINS + codes).astype(jnp.int16)
    seg_p = jnp.transpose(seg.reshape(2, half, n_rows, feats), (2, 3, 0, 1)).reshape(n_rows, 2 * feats, half)
    v_loc = jnp.concatenate([grad.T, hess.T], axis=0)
    span = feats * BINS
    parent = parent_hist.reshape(2 * pairs * local_targets, span)
    hist, split_gain, best = gather_hist(small_side, evicted, seg_p, v_loc, parent, nodes, targets)
    node_hist = hist.reshape(2, nodes, local_targets, span)
    return (node_hist, split_gain, best[:, 0])


def solution(mesh):
    return jax.shard_map(
        local,
        mesh=mesh,
        in_specs=(
            P("rows", None),
            P("rows"),
            P("rows", "outs"),
            P("rows", "outs"),
            P(),
            P(),
            P(None, None, "outs", "rows"),
        ),
        out_specs=(P(None, None, "outs", "rows"), P(None, "rows"), P()),
        check_vma=False,
    )
```

```python
import functools

import jax
import jax.numpy as jnp
import numpy as np
from jax import lax
from jax.experimental import pallas as pl
from jax.experimental.pallas import tpu as pltpu
from jax.sharding import PartitionSpec as P

BINS = 32
LAG = 3


MESH_ID = pl.DeviceIdType.MESH


def row_stages(r, n_rows):
    chips = n_rows // 2
    nx = 4 if chips % 4 == 0 else chips
    ny = chips // nx
    chip = r // 2
    core = r % 2
    y = chip // nx
    x = chip % nx
    row = 2 * nx
    stages = [
        [y * row + (r - y * row + k) % row for k in range(1, row)],
        [(((y + k) % ny) * nx + x) * 2 + core for k in range(1, ny)],
    ]
    return [stage for stage in stages if stage]


def row_peers(r, n_rows):
    return [peer for stage in row_stages(r, n_rows) for peer in stage]


def exchange(partial, split_ref, best_ref, gbuf, mbuf, gsend, grecv, msend, mrecv, targets):
    n_rows = lax.axis_size("rows")
    n_outs = lax.axis_size("outs")
    r = lax.axis_index("rows")
    o = lax.axis_index("outs")
    gbuf[o] = partial
    sends = []
    for k in range(1, n_outs):
        copy = pltpu.make_async_remote_copy(
            src_ref=gbuf.at[o],
            dst_ref=gbuf.at[o],
            send_sem=gsend.at[k],
            recv_sem=grecv.at[o],
            device_id=(r, (o + k) % n_outs),
            device_id_type=MESH_ID,
        )
        copy.start()
        sends.append(copy)
    for k in range(1, n_outs):
        src = (o + n_outs - k) % n_outs
        pltpu.make_async_remote_copy(
            src_ref=gbuf.at[o],
            dst_ref=gbuf.at[src],
            send_sem=gsend.at[k],
            recv_sem=grecv.at[src],
            device_id=(r, src),
            device_id_type=MESH_ID,
        ).wait_recv()
    for copy in sends:
        copy.wait_send()
    acc = gbuf[0]
    for j in range(1, n_outs):
        acc = acc + gbuf[j]
    split = acc / targets
    split_ref[...] = split
    width = mbuf.shape[2]
    best = jnp.broadcast_to(jnp.max(split, axis=1, keepdims=True), (split.shape[0], width))
    base = 0
    for peers in row_stages(r, n_rows):
        mbuf[base] = best
        sends = []
        for j, peer in enumerate(peers):
            copy = pltpu.make_async_remote_copy(
                src_ref=mbuf.at[base],
                dst_ref=mbuf.at[base + 1 + j],
                send_sem=msend.at[base + 1 + j],
                recv_sem=mrecv.at[base + 1 + j],
                device_id=(peer, o),
                device_id_type=MESH_ID,
            )
            copy.start()
            sends.append(copy)
        for copy in sends:
            copy.wait_recv()
        for copy in sends:
            copy.wait_send()
        for j in range(len(peers)):
            best = jnp.maximum(best, mbuf[base + 1 + j])
        base += len(peers) + 1
    best_ref[...] = best


def block_hist(acc_ref, v, s, nodes):
    tl = v.shape[0] // 2
    half = s.shape[1]
    feats = s.shape[0] // 2
    one = jnp.ones((), jnp.bfloat16)
    zero = jnp.zeros((), jnp.bfloat16)
    bins = lax.broadcasted_iota(jnp.int32, (BINS, half), 0)
    for h in range(2):
        vh = v[:, h * half : (h + 1) * half]
        node = s[h : h + 1] >> 5
        onehot = jnp.concatenate(
            [jnp.where((s[2 * f + h : 2 * f + h + 1] & (BINS - 1)) == bins, one, zero) for f in range(feats)],
            axis=0,
        )
        blocks = []
        for c in range(2):
            vc = vh[c * tl : (c + 1) * tl]
            for n in range(nodes):
                blocks.append(jnp.where(node == n, vc, zero))
        vals = jnp.concatenate(blocks, axis=0)
        acc_ref[...] += lax.dot_general(
            vals, onehot, (((1,), (1,)), ((), ())), preferred_element_type=jnp.float32
        )


def gather_hist_kernel(
    small_ref, evict_ref, seg_ref, v_ref, parent_ref, hist_ref, split_ref, best_ref,
    acc_ref, vbuf, sbuf, vsend, fsend, vrecv, ssend, srecv, gbuf, mbuf, gsend, grecv, msend, mrecv,
    *, nodes, targets,
):
    n_rows = lax.axis_size("rows")
    chips = n_rows // 2
    r = lax.axis_index("rows")
    o = lax.axis_index("outs")
    core = r % 2
    chip = r // 2
    partner = chip * 2 + 1 - core
    barrier = pltpu.get_barrier_semaphore()

    def greet(k, carry):
        pl.semaphore_signal(barrier, 1, device_id=((r + k) % n_rows, o), device_id_type=MESH_ID)
        return carry

    lax.fori_loop(1, n_rows, greet, 0)
    n_outs = lax.axis_size("outs")
    for k in range(1, n_outs):
        pl.semaphore_signal(barrier, 1, device_id=(r, (o + k) % n_outs), device_id_type=MESH_ID)
    acc_ref[...] = jnp.zeros_like(acc_ref)
    block_hist(acc_ref, v_ref[...], seg_ref[r].astype(jnp.int32), nodes)
    pl.semaphore_wait(barrier, n_rows - 1 + n_outs - 1)

    def s_copy(k, peer, slot):
        return pltpu.make_async_remote_copy(
            src_ref=seg_ref.at[peer], dst_ref=sbuf.at[slot], send_sem=ssend.at[k], recv_sem=srecv.at[slot],
            device_id=(peer, o), device_id_type=MESH_ID,
        )

    def v_copy(k, peer, slot):
        return pltpu.make_async_remote_copy(
            src_ref=v_ref, dst_ref=vbuf.at[slot], send_sem=vsend.at[k], recv_sem=vrecv.at[slot],
            device_id=(peer, o), device_id_type=MESH_ID,
        )

    def f_copy(k, slot):
        return pltpu.make_async_remote_copy(
            src_ref=vbuf.at[slot], dst_ref=vbuf.at[slot], send_sem=fsend.at[k], recv_sem=vrecv.at[slot],
            device_id=(partner, o), device_id_type=MESH_ID,
        )

    own = pltpu.make_async_remote_copy(
        src_ref=v_ref, dst_ref=vbuf.at[r], send_sem=fsend.at[0], recv_sem=vrecv.at[r],
        device_id=(partner, o), device_id_type=MESH_ID,
    )
    own.start()

    def send(k, carry):
        v_copy(k, ((chip + k) % chips) * 2 + core, r).start()
        return carry

    lax.fori_loop(1, chips, send, 0)

    def send_seg(k, carry):
        s_copy(k, (r + k) % n_rows, r).start()
        return carry

    lax.fori_loop(1, n_rows, send_seg, 0)

    def take_forwarded(k):
        src = ((chip + chips - k) % chips) * 2 + 1 - core
        f_copy(k, src).wait_recv()
        s_copy(k, src, src).wait_recv()
        block_hist(acc_ref, vbuf[src], sbuf[src].astype(jnp.int32), nodes)

    def take_direct(k):
        src = ((chip + chips - k) % chips) * 2 + core
        v_copy(k, src, src).wait_recv()
        f_copy(k, src).start()
        s_copy(k, src, src).wait_recv()
        block_hist(acc_ref, vbuf[src], sbuf[src].astype(jnp.int32), nodes)

    def lead(k, carry):
        take_direct(k)
        return carry

    def take(k, carry):
        take_direct(k)
        take_forwarded(k - LAG)
        return carry

    def tail(k, carry):
        take_forwarded(k)
        return carry

    lag = min(LAG, chips)
    lax.fori_loop(1, lag, lead, 0)
    lax.fori_loop(lag, chips, take, 0)
    lax.fori_loop(chips - lag, chips, tail, 0)

    def drain(k, carry):
        s_copy(k, (r + k) % n_rows, r).wait_send()
        return carry

    lax.fori_loop(1, n_rows, drain, 0)

    def drain_v(k, carry):
        v_copy(k, ((chip + k) % chips) * 2 + core, r).wait_send()
        return carry

    lax.fori_loop(1, chips, drain_v, 0)
    own.wait_send()

    def drain_f(k, carry):
        f_copy(k, ((chip + chips - k) % chips) * 2 + core).wait_send()
        return carry

    lax.fori_loop(1, chips, drain_f, 0)

    node_hist(acc_ref, parent_ref, small_ref, evict_ref, hist_ref, nodes)
    partial = gain_terms(hist_ref, nodes)
    exchange(partial, split_ref, best_ref, gbuf, mbuf, gsend, grecv, msend, mrecv, targets)


def node_hist(acc_ref, parent_ref, small_ref, evict_ref, hist_ref, nodes):
    pairs = nodes // 2
    tl = acc_ref.shape[0] // (2 * nodes)
    for c in range(2):
        for p in range(pairs):
            lo = c * nodes * tl + 2 * p * tl
            a = acc_ref[lo : lo + tl]
            b = acc_ref[lo + tl : lo + 2 * tl]
            base = (c * pairs + p) * tl
            parent = parent_ref[base : base + tl]
            small = small_ref[p] == 0
            gone = evict_ref[p] == 1
            child = jnp.where(small, a, b)
            rebuilt = jnp.where(small, b, a)
            sibling = jnp.where(gone, rebuilt, parent - child)
            hist_ref[lo : lo + tl] = jnp.where(small, child, sibling)
            hist_ref[lo + tl : lo + 2 * tl] = jnp.where(small, sibling, child)


def group_scan(x, reverse):
    span = x.shape[1]
    lane = lax.broadcasted_iota(jnp.int32, x.shape, 1) % BINS
    shift = 1
    while shift < BINS:
        if reverse:
            moved = pltpu.roll(x, span - shift, 1)
            x = x + jnp.where(lane + shift < BINS, moved, 0.0)
        else:
            moved = pltpu.roll(x, shift, 1)
            x = x + jnp.where(lane >= shift, moved, 0.0)
        shift *= 2
    return x


def gain_terms(hist_ref, nodes):
    rows, span = hist_ref.shape
    half = rows // 2
    tl = half // nodes
    lane = lax.broadcasted_iota(jnp.int32, (half, span), 1) % BINS
    left_g = group_scan(hist_ref[0:half], False)
    left_h = group_scan(hist_ref[half:rows], False)
    total_g = group_scan(jnp.where(lane == BINS - 1, left_g, 0.0), True)
    total_h = group_scan(jnp.where(lane == BINS - 1, left_h, 0.0), True)

    def score(a, s):
        return a * a / (jnp.maximum(s, 0.0) + 1.0)

    gain = (
        score(left_g, left_h) + score(total_g - left_g, total_h - left_h) - score(total_g, total_h)
    )
    return jnp.sum(gain.reshape(nodes, tl, span), axis=1)


def gather_hist(small_side, evicted, seg_p, v_loc, parent, nodes, targets):
    n_rows, width, half = seg_p.shape
    n_outs = lax.axis_size("outs")
    vw, rows = v_loc.shape
    feats = width // 2
    out_rows = vw * nodes
    cols = feats * BINS
    total = n_rows * rows
    vmem = pl.BlockSpec(memory_space=pltpu.VMEM)
    smem = pl.BlockSpec(memory_space=pltpu.SMEM)
    return pl.pallas_call(
        functools.partial(gather_hist_kernel, nodes=nodes, targets=targets),
        out_shape=(
            jax.ShapeDtypeStruct((out_rows, cols), jnp.float32),
            jax.ShapeDtypeStruct((nodes, cols), jnp.float32),
            jax.ShapeDtypeStruct((nodes, 128), jnp.float32),
        ),
        in_specs=[smem, smem, vmem, vmem, vmem],
        out_specs=(vmem, vmem, vmem),
        scratch_shapes=[
            pltpu.VMEM((out_rows, cols), jnp.float32),
            pltpu.VMEM((n_rows, vw, rows), v_loc.dtype),
            pltpu.VMEM((n_rows, width, half), seg_p.dtype),
            pltpu.SemaphoreType.DMA((n_rows // 2,)),
            pltpu.SemaphoreType.DMA((n_rows // 2,)),
            pltpu.SemaphoreType.DMA((n_rows,)),
            pltpu.SemaphoreType.DMA((n_rows,)),
            pltpu.SemaphoreType.DMA((n_rows,)),
            pltpu.VMEM((n_outs, nodes, cols), jnp.float32),
            pltpu.VMEM((n_rows, nodes, 128), jnp.float32),
            pltpu.SemaphoreType.DMA((n_outs,)),
            pltpu.SemaphoreType.DMA((n_outs,)),
            pltpu.SemaphoreType.DMA((n_rows,)),
            pltpu.SemaphoreType.DMA((n_rows,)),
        ],
        compiler_params=pltpu.CompilerParams(collective_id=1, has_side_effects=True),
        cost_estimate=pl.CostEstimate(
            flops=2 * out_rows * cols * total,
            bytes_accessed=total * (vw * 2 + feats * 2) + out_rows * cols * 4,
            transcendentals=0,
        ),
    )(small_side, evicted, seg_p, v_loc, parent)


def local(codes, node_of_row, grad, hess, small_side, evicted, parent_hist):
    pairs = small_side.shape[0]
    nodes = 2 * pairs
    local_targets = grad.shape[1]
    targets = local_targets * lax.axis_size("outs")
    n_rows = lax.axis_size("rows")
    count, features = codes.shape
    feats = features // n_rows
    half = count // 2
    seg = (node_of_row[:, None] * BINS + codes).astype(jnp.int16)
    seg_p = jnp.transpose(seg.reshape(2, half, n_rows, feats), (2, 3, 0, 1)).reshape(n_rows, 2 * feats, half)
    v_loc = jnp.concatenate([grad.T, hess.T], axis=0)
    span = feats * BINS
    parent = parent_hist.reshape(2 * pairs * local_targets, span)
    hist, split_gain, best = gather_hist(small_side, evicted, seg_p, v_loc, parent, nodes, targets)
    node_hist = hist.reshape(2, nodes, local_targets, span)
    return (node_hist, split_gain, best[:, 0])


def solution(mesh):
    return jax.shard_map(
        local,
        mesh=mesh,
        in_specs=(
            P("rows", None),
            P("rows"),
            P("rows", "outs"),
            P("rows", "outs"),
            P(),
            P(),
            P(None, None, "outs", "rows"),
        ),
        out_specs=(P(None, None, "outs", "rows"), P(None, "rows"), P()),
        check_vma=False,
    )
```

```python
import functools

import jax
import jax.numpy as jnp
import numpy as np
from jax import lax
from jax.experimental import pallas as pl
from jax.experimental.pallas import tpu as pltpu
from jax.sharding import PartitionSpec as P

BINS = 32


MESH_ID = pl.DeviceIdType.MESH


def row_stages(r, n_rows):
    chips = n_rows // 2
    nx = 4 if chips % 4 == 0 else chips
    ny = chips // nx
    chip = r // 2
    core = r % 2
    y = chip // nx
    x = chip % nx
    row = 2 * nx
    stages = [
        [y * row + (r - y * row + k) % row for k in range(1, row)],
        [(((y + k) % ny) * nx + x) * 2 + core for k in range(1, ny)],
    ]
    return [stage for stage in stages if stage]


def row_peers(r, n_rows):
    return [peer for stage in row_stages(r, n_rows) for peer in stage]


def exchange(partial, split_ref, best_ref, gbuf, mbuf, gsend, grecv, msend, mrecv, targets):
    n_rows = lax.axis_size("rows")
    n_outs = lax.axis_size("outs")
    r = lax.axis_index("rows")
    o = lax.axis_index("outs")
    gbuf[o] = partial
    sends = []
    for k in range(1, n_outs):
        copy = pltpu.make_async_remote_copy(
            src_ref=gbuf.at[o],
            dst_ref=gbuf.at[o],
            send_sem=gsend.at[k],
            recv_sem=grecv.at[o],
            device_id=(r, (o + k) % n_outs),
            device_id_type=MESH_ID,
        )
        copy.start()
        sends.append(copy)
    for k in range(1, n_outs):
        src = (o + n_outs - k) % n_outs
        pltpu.make_async_remote_copy(
            src_ref=gbuf.at[o],
            dst_ref=gbuf.at[src],
            send_sem=gsend.at[k],
            recv_sem=grecv.at[src],
            device_id=(r, src),
            device_id_type=MESH_ID,
        ).wait_recv()
    for copy in sends:
        copy.wait_send()
    acc = gbuf[0]
    for j in range(1, n_outs):
        acc = acc + gbuf[j]
    split = acc / targets
    split_ref[...] = split
    width = mbuf.shape[2]
    best = jnp.broadcast_to(jnp.max(split, axis=1, keepdims=True), (split.shape[0], width))
    base = 0
    for peers in row_stages(r, n_rows):
        mbuf[base] = best
        sends = []
        for j, peer in enumerate(peers):
            copy = pltpu.make_async_remote_copy(
                src_ref=mbuf.at[base],
                dst_ref=mbuf.at[base + 1 + j],
                send_sem=msend.at[base + 1 + j],
                recv_sem=mrecv.at[base + 1 + j],
                device_id=(peer, o),
                device_id_type=MESH_ID,
            )
            copy.start()
            sends.append(copy)
        for copy in sends:
            copy.wait_recv()
        for copy in sends:
            copy.wait_send()
        for j in range(len(peers)):
            best = jnp.maximum(best, mbuf[base + 1 + j])
        base += len(peers) + 1
    best_ref[...] = best


def block_hist(acc_ref, v, s, nodes):
    tl = v.shape[0] // 2
    half = s.shape[1]
    feats = s.shape[0] // 2
    one = jnp.ones((), jnp.bfloat16)
    zero = jnp.zeros((), jnp.bfloat16)
    bins = lax.broadcasted_iota(jnp.int32, (BINS, half), 0)
    for h in range(2):
        vh = v[:, h * half : (h + 1) * half]
        node = s[h : h + 1] >> 5
        onehot = jnp.concatenate(
            [jnp.where((s[2 * f + h : 2 * f + h + 1] & (BINS - 1)) == bins, one, zero) for f in range(feats)],
            axis=0,
        )
        blocks = []
        for c in range(2):
            vc = vh[c * tl : (c + 1) * tl]
            for n in range(nodes):
                blocks.append(jnp.where(node == n, vc, zero))
        vals = jnp.concatenate(blocks, axis=0)
        acc_ref[...] += lax.dot_general(
            vals, onehot, (((1,), (1,)), ((), ())), preferred_element_type=jnp.float32
        )


def relay_gather(acc_ref, seg_ref, v_ref, vbuf, sbuf, vsend, fsend, vrecv, s_copy, send_seg, nodes):
    n_rows = lax.axis_size("rows")
    r = lax.axis_index("rows")
    o = lax.axis_index("outs")
    core = r % 2
    chip = r // 2
    y = chip // 4
    x = chip % 4
    a = x + core * (y - x)
    b = y + core * (x - y)
    partner = chip * 2 + 1 - core

    def dev(da, db):
        ap = (a + da + 4) % 4
        bp = (b + db + 4) % 4
        return ((1 - core) * (bp * 4 + ap) + core * (ap * 4 + bp)) * 2 + core

    def copy(src, sem, peer, slot):
        return pltpu.make_async_remote_copy(
            src_ref=src, dst_ref=vbuf.at[slot], send_sem=sem, recv_sem=vrecv.at[slot],
            device_id=(peer, o), device_id_type=MESH_ID,
        )

    def arrive(slot):
        copy(vbuf.at[slot], vsend.at[0], partner, slot).wait_recv()
        s_copy(0, slot, slot).wait_recv()

    def compute(slot):
        block_hist(acc_ref, vbuf[slot], sbuf[slot].astype(jnp.int32), nodes)

    started = []

    def start(src, sem, peer, slot):
        c = copy(src, sem, peer, slot)
        c.start()
        started.append(c)

    start(v_ref, fsend.at[0], partner, r)
    for j, (da, db) in enumerate([(1, 0), (-1, 0), (0, 1), (0, -1)]):
        start(v_ref, vsend.at[j], dev(da, db), r)
    lax.fori_loop(1, n_rows, send_seg, 0)

    sem = 4
    for j, da in enumerate([-1, 1, -2]):
        slot = dev(da, 0)
        arrive(slot)
        if da == -1:
            start(vbuf.at[slot], vsend.at[sem], dev(1, 0), slot)
            sem += 1
        start(vbuf.at[slot], vsend.at[sem], dev(0, 1), slot)
        start(vbuf.at[slot], vsend.at[sem + 1], dev(0, -1), slot)
        sem += 2
        start(vbuf.at[slot], fsend.at[1 + j], partner, slot)
        compute(slot)

    def row_step(db, relay, first):
        def body(i, carry):
            slot = dev((i * 3) % 4, db)
            arrive(slot)
            if relay:
                copy(vbuf.at[slot], vsend.at[11 + i], dev(0, 1), slot).start()
            copy(vbuf.at[slot], fsend.at[first + i], partner, slot).start()
            compute(slot)
            return carry

        return body

    def row_drain(db, relay, first):
        def body(i, carry):
            slot = dev((i * 3) % 4, db)
            if relay:
                copy(vbuf.at[slot], vsend.at[11 + i], dev(0, 1), slot).wait_send()
            copy(vbuf.at[slot], fsend.at[first + i], partner, slot).wait_send()
            return carry

        return body

    rows_plan = [(-1, True, 4), (1, False, 8), (-2, False, 12)]
    for db, relay, first in rows_plan:
        lax.fori_loop(0, 4, row_step(db, relay, first), 0)

    def take_partner(k, carry):
        slot = ((chip + 16 - k) % 16) * 2 + 1 - core
        arrive(slot)
        compute(slot)
        return carry

    lax.fori_loop(0, 16, take_partner, 0)
    for c in started:
        c.wait_send()
    for db, relay, first in rows_plan:
        lax.fori_loop(0, 4, row_drain(db, relay, first), 0)


def gather_hist_kernel(
    small_ref, evict_ref, seg_ref, v_ref, parent_ref, hist_ref, split_ref, best_ref,
    acc_ref, vbuf, sbuf, vsend, fsend, vrecv, ssend, srecv, gbuf, mbuf, gsend, grecv, msend, mrecv,
    *, nodes, targets,
):
    n_rows = lax.axis_size("rows")
    chips = n_rows // 2
    r = lax.axis_index("rows")
    o = lax.axis_index("outs")
    core = r % 2
    chip = r // 2
    partner = chip * 2 + 1 - core
    barrier = pltpu.get_barrier_semaphore()

    def greet(k, carry):
        pl.semaphore_signal(barrier, 1, device_id=((r + k) % n_rows, o), device_id_type=MESH_ID)
        return carry

    lax.fori_loop(1, n_rows, greet, 0)
    n_outs = lax.axis_size("outs")
    for k in range(1, n_outs):
        pl.semaphore_signal(barrier, 1, device_id=(r, (o + k) % n_outs), device_id_type=MESH_ID)
    acc_ref[...] = jnp.zeros_like(acc_ref)
    block_hist(acc_ref, v_ref[...], seg_ref[r].astype(jnp.int32), nodes)
    pl.semaphore_wait(barrier, n_rows - 1 + n_outs - 1)

    def s_copy(k, peer, slot):
        return pltpu.make_async_remote_copy(
            src_ref=seg_ref.at[peer], dst_ref=sbuf.at[slot], send_sem=ssend.at[k], recv_sem=srecv.at[slot],
            device_id=(peer, o), device_id_type=MESH_ID,
        )

    def v_copy(k, peer, slot):
        return pltpu.make_async_remote_copy(
            src_ref=v_ref, dst_ref=vbuf.at[slot], send_sem=vsend.at[k], recv_sem=vrecv.at[slot],
            device_id=(peer, o), device_id_type=MESH_ID,
        )

    def f_copy(k, slot):
        return pltpu.make_async_remote_copy(
            src_ref=vbuf.at[slot], dst_ref=vbuf.at[slot], send_sem=fsend.at[k], recv_sem=vrecv.at[slot],
            device_id=(partner, o), device_id_type=MESH_ID,
        )

    def send_seg(k, carry):
        s_copy(k, (r + k) % n_rows, r).start()
        return carry

    def drain(k, carry):
        s_copy(k, (r + k) % n_rows, r).wait_send()
        return carry

    if chips == 16:
        relay_gather(acc_ref, seg_ref, v_ref, vbuf, sbuf, vsend, fsend, vrecv, s_copy, send_seg, nodes)
        lax.fori_loop(1, n_rows, drain, 0)
    else:
        own = pltpu.make_async_remote_copy(
            src_ref=v_ref, dst_ref=vbuf.at[r], send_sem=fsend.at[0], recv_sem=vrecv.at[r],
            device_id=(partner, o), device_id_type=MESH_ID,
        )
        own.start()

        def send(k, carry):
            v_copy(k, ((chip + k) % chips) * 2 + core, r).start()
            return carry

        lax.fori_loop(1, chips, send, 0)

        lax.fori_loop(1, n_rows, send_seg, 0)

        def take_direct(k, carry):
            src = ((chip + chips - k) % chips) * 2 + core
            v_copy(k, src, src).wait_recv()
            f_copy(k, src).start()
            s_copy(k, src, src).wait_recv()
            block_hist(acc_ref, vbuf[src], sbuf[src].astype(jnp.int32), nodes)
            return carry

        lax.fori_loop(1, chips, take_direct, 0)

        def take_forwarded(k, carry):
            src = ((chip + chips - k) % chips) * 2 + 1 - core
            f_copy(k, src).wait_recv()
            s_copy(k, src, src).wait_recv()
            block_hist(acc_ref, vbuf[src], sbuf[src].astype(jnp.int32), nodes)
            return carry

        lax.fori_loop(0, chips, take_forwarded, 0)

        lax.fori_loop(1, n_rows, drain, 0)

        def drain_v(k, carry):
            v_copy(k, ((chip + k) % chips) * 2 + core, r).wait_send()
            return carry

        lax.fori_loop(1, chips, drain_v, 0)
        own.wait_send()

        def drain_f(k, carry):
            f_copy(k, ((chip + chips - k) % chips) * 2 + core).wait_send()
            return carry

        lax.fori_loop(1, chips, drain_f, 0)


    node_hist(acc_ref, parent_ref, small_ref, evict_ref, hist_ref, nodes)
    partial = gain_terms(hist_ref, nodes)
    exchange(partial, split_ref, best_ref, gbuf, mbuf, gsend, grecv, msend, mrecv, targets)


def node_hist(acc_ref, parent_ref, small_ref, evict_ref, hist_ref, nodes):
    pairs = nodes // 2
    tl = acc_ref.shape[0] // (2 * nodes)
    for c in range(2):
        for p in range(pairs):
            lo = c * nodes * tl + 2 * p * tl
            a = acc_ref[lo : lo + tl]
            b = acc_ref[lo + tl : lo + 2 * tl]
            base = (c * pairs + p) * tl
            parent = parent_ref[base : base + tl]
            small = small_ref[p] == 0
            gone = evict_ref[p] == 1
            child = jnp.where(small, a, b)
            rebuilt = jnp.where(small, b, a)
            sibling = jnp.where(gone, rebuilt, parent - child)
            hist_ref[lo : lo + tl] = jnp.where(small, child, sibling)
            hist_ref[lo + tl : lo + 2 * tl] = jnp.where(small, sibling, child)


def group_scan(x, reverse):
    span = x.shape[1]
    lane = lax.broadcasted_iota(jnp.int32, x.shape, 1) % BINS
    shift = 1
    while shift < BINS:
        if reverse:
            moved = pltpu.roll(x, span - shift, 1)
            x = x + jnp.where(lane + shift < BINS, moved, 0.0)
        else:
            moved = pltpu.roll(x, shift, 1)
            x = x + jnp.where(lane >= shift, moved, 0.0)
        shift *= 2
    return x


def gain_terms(hist_ref, nodes):
    rows, span = hist_ref.shape
    half = rows // 2
    tl = half // nodes
    lane = lax.broadcasted_iota(jnp.int32, (half, span), 1) % BINS
    left_g = group_scan(hist_ref[0:half], False)
    left_h = group_scan(hist_ref[half:rows], False)
    total_g = group_scan(jnp.where(lane == BINS - 1, left_g, 0.0), True)
    total_h = group_scan(jnp.where(lane == BINS - 1, left_h, 0.0), True)

    def score(a, s):
        return a * a / (jnp.maximum(s, 0.0) + 1.0)

    gain = (
        score(left_g, left_h) + score(total_g - left_g, total_h - left_h) - score(total_g, total_h)
    )
    return jnp.sum(gain.reshape(nodes, tl, span), axis=1)


def gather_hist(small_side, evicted, seg_p, v_loc, parent, nodes, targets):
    n_rows, width, half = seg_p.shape
    n_outs = lax.axis_size("outs")
    vw, rows = v_loc.shape
    feats = width // 2
    out_rows = vw * nodes
    cols = feats * BINS
    total = n_rows * rows
    vmem = pl.BlockSpec(memory_space=pltpu.VMEM)
    smem = pl.BlockSpec(memory_space=pltpu.SMEM)
    return pl.pallas_call(
        functools.partial(gather_hist_kernel, nodes=nodes, targets=targets),
        out_shape=(
            jax.ShapeDtypeStruct((out_rows, cols), jnp.float32),
            jax.ShapeDtypeStruct((nodes, cols), jnp.float32),
            jax.ShapeDtypeStruct((nodes, 128), jnp.float32),
        ),
        in_specs=[smem, smem, vmem, vmem, vmem],
        out_specs=(vmem, vmem, vmem),
        scratch_shapes=[
            pltpu.VMEM((out_rows, cols), jnp.float32),
            pltpu.VMEM((n_rows, vw, rows), v_loc.dtype),
            pltpu.VMEM((n_rows, width, half), seg_p.dtype),
            pltpu.SemaphoreType.DMA((n_rows // 2,)),
            pltpu.SemaphoreType.DMA((n_rows // 2,)),
            pltpu.SemaphoreType.DMA((n_rows,)),
            pltpu.SemaphoreType.DMA((n_rows,)),
            pltpu.SemaphoreType.DMA((n_rows,)),
            pltpu.VMEM((n_outs, nodes, cols), jnp.float32),
            pltpu.VMEM((n_rows, nodes, 128), jnp.float32),
            pltpu.SemaphoreType.DMA((n_outs,)),
            pltpu.SemaphoreType.DMA((n_outs,)),
            pltpu.SemaphoreType.DMA((n_rows,)),
            pltpu.SemaphoreType.DMA((n_rows,)),
        ],
        compiler_params=pltpu.CompilerParams(collective_id=1, has_side_effects=True),
        cost_estimate=pl.CostEstimate(
            flops=2 * out_rows * cols * total,
            bytes_accessed=total * (vw * 2 + feats * 2) + out_rows * cols * 4,
            transcendentals=0,
        ),
    )(small_side, evicted, seg_p, v_loc, parent)


def local(codes, node_of_row, grad, hess, small_side, evicted, parent_hist):
    pairs = small_side.shape[0]
    nodes = 2 * pairs
    local_targets = grad.shape[1]
    targets = local_targets * lax.axis_size("outs")
    n_rows = lax.axis_size("rows")
    count, features = codes.shape
    feats = features // n_rows
    half = count // 2
    seg = (node_of_row[:, None] * BINS + codes).astype(jnp.int16)
    seg_p = jnp.transpose(seg.reshape(2, half, n_rows, feats), (2, 3, 0, 1)).reshape(n_rows, 2 * feats, half)
    v_loc = jnp.concatenate([grad.T, hess.T], axis=0)
    span = feats * BINS
    parent = parent_hist.reshape(2 * pairs * local_targets, span)
    hist, split_gain, best = gather_hist(small_side, evicted, seg_p, v_loc, parent, nodes, targets)
    node_hist = hist.reshape(2, nodes, local_targets, span)
    return (node_hist, split_gain, best[:, 0])


def solution(mesh):
    return jax.shard_map(
        local,
        mesh=mesh,
        in_specs=(
            P("rows", None),
            P("rows"),
            P("rows", "outs"),
            P("rows", "outs"),
            P(),
            P(),
            P(None, None, "outs", "rows"),
        ),
        out_specs=(P(None, None, "outs", "rows"), P(None, "rows"), P()),
        check_vma=False,
    )
```

```python
import functools

import jax
import jax.numpy as jnp
import numpy as np
from jax import lax
from jax.experimental import pallas as pl
from jax.experimental.pallas import tpu as pltpu
from jax.sharding import PartitionSpec as P

BINS = 32


MESH_ID = pl.DeviceIdType.MESH


def row_stages(r, n_rows):
    chips = n_rows // 2
    nx = 4 if chips % 4 == 0 else chips
    ny = chips // nx
    chip = r // 2
    core = r % 2
    y = chip // nx
    x = chip % nx
    row = 2 * nx
    stages = [
        [y * row + (r - y * row + k) % row for k in range(1, row)],
        [(((y + k) % ny) * nx + x) * 2 + core for k in range(1, ny)],
    ]
    return [stage for stage in stages if stage]


def row_peers(r, n_rows):
    return [peer for stage in row_stages(r, n_rows) for peer in stage]


def exchange(partial, split_ref, best_ref, gbuf, mbuf, gsend, grecv, msend, mrecv, targets):
    n_rows = lax.axis_size("rows")
    n_outs = lax.axis_size("outs")
    r = lax.axis_index("rows")
    o = lax.axis_index("outs")
    gbuf[o] = partial
    sends = []
    for k in range(1, n_outs):
        copy = pltpu.make_async_remote_copy(
            src_ref=gbuf.at[o],
            dst_ref=gbuf.at[o],
            send_sem=gsend.at[k],
            recv_sem=grecv.at[o],
            device_id=(r, (o + k) % n_outs),
            device_id_type=MESH_ID,
        )
        copy.start()
        sends.append(copy)
    for k in range(1, n_outs):
        src = (o + n_outs - k) % n_outs
        pltpu.make_async_remote_copy(
            src_ref=gbuf.at[o],
            dst_ref=gbuf.at[src],
            send_sem=gsend.at[k],
            recv_sem=grecv.at[src],
            device_id=(r, src),
            device_id_type=MESH_ID,
        ).wait_recv()
    for copy in sends:
        copy.wait_send()
    acc = gbuf[0]
    for j in range(1, n_outs):
        acc = acc + gbuf[j]
    split = acc / targets
    split_ref[...] = split
    width = mbuf.shape[2]
    best = jnp.broadcast_to(jnp.max(split, axis=1, keepdims=True), (split.shape[0], width))
    base = 0
    for peers in row_stages(r, n_rows):
        mbuf[base] = best
        sends = []
        for j, peer in enumerate(peers):
            copy = pltpu.make_async_remote_copy(
                src_ref=mbuf.at[base],
                dst_ref=mbuf.at[base + 1 + j],
                send_sem=msend.at[base + 1 + j],
                recv_sem=mrecv.at[base + 1 + j],
                device_id=(peer, o),
                device_id_type=MESH_ID,
            )
            copy.start()
            sends.append(copy)
        for copy in sends:
            copy.wait_recv()
        for copy in sends:
            copy.wait_send()
        for j in range(len(peers)):
            best = jnp.maximum(best, mbuf[base + 1 + j])
        base += len(peers) + 1
    best_ref[...] = best


def block_hist(acc_ref, v, s, nodes):
    tl = v.shape[0] // 2
    half = s.shape[1]
    feats = s.shape[0] // 2
    one = jnp.ones((), jnp.bfloat16)
    zero = jnp.zeros((), jnp.bfloat16)
    bins = lax.broadcasted_iota(jnp.int32, (BINS, half), 0)
    for h in range(2):
        vh = v[:, h * half : (h + 1) * half]
        node = s[h : h + 1] >> 5
        onehot = jnp.concatenate(
            [jnp.where((s[2 * f + h : 2 * f + h + 1] & (BINS - 1)) == bins, one, zero) for f in range(feats)],
            axis=0,
        )
        blocks = []
        for c in range(2):
            vc = vh[c * tl : (c + 1) * tl]
            for n in range(nodes):
                blocks.append(jnp.where(node == n, vc, zero))
        vals = jnp.concatenate(blocks, axis=0)
        acc_ref[...] += lax.dot_general(
            vals, onehot, (((1,), (1,)), ((), ())), preferred_element_type=jnp.float32
        )


def relay_gather(acc_ref, seg_ref, v_ref, vbuf, sbuf, vsend, fsend, vrecv, s_copy, send_seg, nodes):
    n_rows = lax.axis_size("rows")
    r = lax.axis_index("rows")
    o = lax.axis_index("outs")
    core = r % 2
    chip = r // 2
    y = chip // 4
    x = chip % 4
    a = x + core * (y - x)
    b = y + core * (x - y)
    partner = chip * 2 + 1 - core

    def dev(da, db):
        ap = (a + da + 4) % 4
        bp = (b + db + 4) % 4
        return ((1 - core) * (bp * 4 + ap) + core * (ap * 4 + bp)) * 2 + core

    def copy(src, sem, peer, slot):
        return pltpu.make_async_remote_copy(
            src_ref=src, dst_ref=vbuf.at[slot], send_sem=sem, recv_sem=vrecv.at[slot],
            device_id=(peer, o), device_id_type=MESH_ID,
        )

    def arrive(slot):
        copy(vbuf.at[slot], vsend.at[0], partner, slot).wait_recv()
        s_copy(0, slot, slot).wait_recv()

    def compute(slot):
        block_hist(acc_ref, vbuf[slot], sbuf[slot].astype(jnp.int32), nodes)

    started = []

    def start(src, sem, peer, slot):
        c = copy(src, sem, peer, slot)
        c.start()
        started.append(c)

    start(v_ref, fsend.at[0], partner, r)
    for j, (da, db) in enumerate([(1, 0), (-1, 0), (0, 1), (0, -1)]):
        start(v_ref, vsend.at[j], dev(da, db), r)
    lax.fori_loop(1, n_rows, send_seg, 0)

    sem = 4
    for j, da in enumerate([-1, 1, -2]):
        slot = dev(da, 0)
        arrive(slot)
        if da == -1:
            start(vbuf.at[slot], vsend.at[sem], dev(1, 0), slot)
            sem += 1
        start(vbuf.at[slot], vsend.at[sem], dev(0, 1), slot)
        start(vbuf.at[slot], vsend.at[sem + 1], dev(0, -1), slot)
        sem += 2
        start(vbuf.at[slot], fsend.at[1 + j], partner, slot)
        compute(slot)

    def row_step(db, relay, first):
        def body(i, carry):
            slot = dev((i * 3) % 4, db)
            arrive(slot)
            if relay:
                copy(vbuf.at[slot], vsend.at[11 + i], dev(0, -db), slot).start()
            copy(vbuf.at[slot], fsend.at[first + i], partner, slot).start()
            compute(slot)
            return carry

        return body

    def row_drain(db, relay, first):
        def body(i, carry):
            slot = dev((i * 3) % 4, db)
            if relay:
                copy(vbuf.at[slot], vsend.at[11 + i], dev(0, -db), slot).wait_send()
            copy(vbuf.at[slot], fsend.at[first + i], partner, slot).wait_send()
            return carry

        return body

    rows_plan = [(-1, True, 4, 0, 2), (1, False, 8, 0, 2), (-1, False, 4, 2, 4), (1, True, 8, 2, 4), (2, False, 12, 0, 4)]
    for db, relay, first, lo, hi in rows_plan:
        lax.fori_loop(lo, hi, row_step(db, relay, first), 0)

    def take_partner(k, carry):
        slot = ((chip + 16 - k) % 16) * 2 + 1 - core
        arrive(slot)
        compute(slot)
        return carry

    lax.fori_loop(0, 16, take_partner, 0)
    for c in started:
        c.wait_send()
    for db, relay, first, lo, hi in rows_plan:
        lax.fori_loop(lo, hi, row_drain(db, relay, first), 0)


def gather_hist_kernel(
    small_ref, evict_ref, seg_ref, v_ref, parent_ref, hist_ref, split_ref, best_ref,
    acc_ref, vbuf, sbuf, vsend, fsend, vrecv, ssend, srecv, gbuf, mbuf, gsend, grecv, msend, mrecv,
    *, nodes, targets,
):
    n_rows = lax.axis_size("rows")
    chips = n_rows // 2
    r = lax.axis_index("rows")
    o = lax.axis_index("outs")
    core = r % 2
    chip = r // 2
    partner = chip * 2 + 1 - core
    barrier = pltpu.get_barrier_semaphore()

    def greet(k, carry):
        pl.semaphore_signal(barrier, 1, device_id=((r + k) % n_rows, o), device_id_type=MESH_ID)
        return carry

    lax.fori_loop(1, n_rows, greet, 0)
    n_outs = lax.axis_size("outs")
    for k in range(1, n_outs):
        pl.semaphore_signal(barrier, 1, device_id=(r, (o + k) % n_outs), device_id_type=MESH_ID)
    acc_ref[...] = jnp.zeros_like(acc_ref)
    block_hist(acc_ref, v_ref[...], seg_ref[r].astype(jnp.int32), nodes)
    pl.semaphore_wait(barrier, n_rows - 1 + n_outs - 1)

    def s_copy(k, peer, slot):
        return pltpu.make_async_remote_copy(
            src_ref=seg_ref.at[peer], dst_ref=sbuf.at[slot], send_sem=ssend.at[k], recv_sem=srecv.at[slot],
            device_id=(peer, o), device_id_type=MESH_ID,
        )

    def v_copy(k, peer, slot):
        return pltpu.make_async_remote_copy(
            src_ref=v_ref, dst_ref=vbuf.at[slot], send_sem=vsend.at[k], recv_sem=vrecv.at[slot],
            device_id=(peer, o), device_id_type=MESH_ID,
        )

    def f_copy(k, slot):
        return pltpu.make_async_remote_copy(
            src_ref=vbuf.at[slot], dst_ref=vbuf.at[slot], send_sem=fsend.at[k], recv_sem=vrecv.at[slot],
            device_id=(partner, o), device_id_type=MESH_ID,
        )

    def send_seg(k, carry):
        s_copy(k, (r + k) % n_rows, r).start()
        return carry

    def drain(k, carry):
        s_copy(k, (r + k) % n_rows, r).wait_send()
        return carry

    if chips == 16:
        relay_gather(acc_ref, seg_ref, v_ref, vbuf, sbuf, vsend, fsend, vrecv, s_copy, send_seg, nodes)
        lax.fori_loop(1, n_rows, drain, 0)
    else:
        own = pltpu.make_async_remote_copy(
            src_ref=v_ref, dst_ref=vbuf.at[r], send_sem=fsend.at[0], recv_sem=vrecv.at[r],
            device_id=(partner, o), device_id_type=MESH_ID,
        )
        own.start()

        def send(k, carry):
            v_copy(k, ((chip + k) % chips) * 2 + core, r).start()
            return carry

        lax.fori_loop(1, chips, send, 0)

        lax.fori_loop(1, n_rows, send_seg, 0)

        def take_direct(k, carry):
            src = ((chip + chips - k) % chips) * 2 + core
            v_copy(k, src, src).wait_recv()
            f_copy(k, src).start()
            s_copy(k, src, src).wait_recv()
            block_hist(acc_ref, vbuf[src], sbuf[src].astype(jnp.int32), nodes)
            return carry

        lax.fori_loop(1, chips, take_direct, 0)

        def take_forwarded(k, carry):
            src = ((chip + chips - k) % chips) * 2 + 1 - core
            f_copy(k, src).wait_recv()
            s_copy(k, src, src).wait_recv()
            block_hist(acc_ref, vbuf[src], sbuf[src].astype(jnp.int32), nodes)
            return carry

        lax.fori_loop(0, chips, take_forwarded, 0)

        lax.fori_loop(1, n_rows, drain, 0)

        def drain_v(k, carry):
            v_copy(k, ((chip + k) % chips) * 2 + core, r).wait_send()
            return carry

        lax.fori_loop(1, chips, drain_v, 0)
        own.wait_send()

        def drain_f(k, carry):
            f_copy(k, ((chip + chips - k) % chips) * 2 + core).wait_send()
            return carry

        lax.fori_loop(1, chips, drain_f, 0)


    node_hist(acc_ref, parent_ref, small_ref, evict_ref, hist_ref, nodes)
    partial = gain_terms(hist_ref, nodes)
    exchange(partial, split_ref, best_ref, gbuf, mbuf, gsend, grecv, msend, mrecv, targets)


def node_hist(acc_ref, parent_ref, small_ref, evict_ref, hist_ref, nodes):
    pairs = nodes // 2
    tl = acc_ref.shape[0] // (2 * nodes)
    for c in range(2):
        for p in range(pairs):
            lo = c * nodes * tl + 2 * p * tl
            a = acc_ref[lo : lo + tl]
            b = acc_ref[lo + tl : lo + 2 * tl]
            base = (c * pairs + p) * tl
            parent = parent_ref[base : base + tl]
            small = small_ref[p] == 0
            gone = evict_ref[p] == 1
            child = jnp.where(small, a, b)
            rebuilt = jnp.where(small, b, a)
            sibling = jnp.where(gone, rebuilt, parent - child)
            hist_ref[lo : lo + tl] = jnp.where(small, child, sibling)
            hist_ref[lo + tl : lo + 2 * tl] = jnp.where(small, sibling, child)


def group_scan(x, reverse):
    span = x.shape[1]
    lane = lax.broadcasted_iota(jnp.int32, x.shape, 1) % BINS
    shift = 1
    while shift < BINS:
        if reverse:
            moved = pltpu.roll(x, span - shift, 1)
            x = x + jnp.where(lane + shift < BINS, moved, 0.0)
        else:
            moved = pltpu.roll(x, shift, 1)
            x = x + jnp.where(lane >= shift, moved, 0.0)
        shift *= 2
    return x


def gain_terms(hist_ref, nodes):
    rows, span = hist_ref.shape
    half = rows // 2
    tl = half // nodes
    lane = lax.broadcasted_iota(jnp.int32, (half, span), 1) % BINS
    left_g = group_scan(hist_ref[0:half], False)
    left_h = group_scan(hist_ref[half:rows], False)
    total_g = group_scan(jnp.where(lane == BINS - 1, left_g, 0.0), True)
    total_h = group_scan(jnp.where(lane == BINS - 1, left_h, 0.0), True)

    def score(a, s):
        return a * a / (jnp.maximum(s, 0.0) + 1.0)

    gain = (
        score(left_g, left_h) + score(total_g - left_g, total_h - left_h) - score(total_g, total_h)
    )
    return jnp.sum(gain.reshape(nodes, tl, span), axis=1)


def gather_hist(small_side, evicted, seg_p, v_loc, parent, nodes, targets):
    n_rows, width, half = seg_p.shape
    n_outs = lax.axis_size("outs")
    vw, rows = v_loc.shape
    feats = width // 2
    out_rows = vw * nodes
    cols = feats * BINS
    total = n_rows * rows
    vmem = pl.BlockSpec(memory_space=pltpu.VMEM)
    smem = pl.BlockSpec(memory_space=pltpu.SMEM)
    return pl.pallas_call(
        functools.partial(gather_hist_kernel, nodes=nodes, targets=targets),
        out_shape=(
            jax.ShapeDtypeStruct((out_rows, cols), jnp.float32),
            jax.ShapeDtypeStruct((nodes, cols), jnp.float32),
            jax.ShapeDtypeStruct((nodes, 128), jnp.float32),
        ),
        in_specs=[smem, smem, vmem, vmem, vmem],
        out_specs=(vmem, vmem, vmem),
        scratch_shapes=[
            pltpu.VMEM((out_rows, cols), jnp.float32),
            pltpu.VMEM((n_rows, vw, rows), v_loc.dtype),
            pltpu.VMEM((n_rows, width, half), seg_p.dtype),
            pltpu.SemaphoreType.DMA((n_rows // 2,)),
            pltpu.SemaphoreType.DMA((n_rows // 2,)),
            pltpu.SemaphoreType.DMA((n_rows,)),
            pltpu.SemaphoreType.DMA((n_rows,)),
            pltpu.SemaphoreType.DMA((n_rows,)),
            pltpu.VMEM((n_outs, nodes, cols), jnp.float32),
            pltpu.VMEM((n_rows, nodes, 128), jnp.float32),
            pltpu.SemaphoreType.DMA((n_outs,)),
            pltpu.SemaphoreType.DMA((n_outs,)),
            pltpu.SemaphoreType.DMA((n_rows,)),
            pltpu.SemaphoreType.DMA((n_rows,)),
        ],
        compiler_params=pltpu.CompilerParams(collective_id=1, has_side_effects=True),
        cost_estimate=pl.CostEstimate(
            flops=2 * out_rows * cols * total,
            bytes_accessed=total * (vw * 2 + feats * 2) + out_rows * cols * 4,
            transcendentals=0,
        ),
    )(small_side, evicted, seg_p, v_loc, parent)


def local(codes, node_of_row, grad, hess, small_side, evicted, parent_hist):
    pairs = small_side.shape[0]
    nodes = 2 * pairs
    local_targets = grad.shape[1]
    targets = local_targets * lax.axis_size("outs")
    n_rows = lax.axis_size("rows")
    count, features = codes.shape
    feats = features // n_rows
    half = count // 2
    seg = (node_of_row[:, None] * BINS + codes).astype(jnp.int16)
    seg_p = jnp.transpose(seg.reshape(2, half, n_rows, feats), (2, 3, 0, 1)).reshape(n_rows, 2 * feats, half)
    v_loc = jnp.concatenate([grad.T, hess.T], axis=0)
    span = feats * BINS
    parent = parent_hist.reshape(2 * pairs * local_targets, span)
    hist, split_gain, best = gather_hist(small_side, evicted, seg_p, v_loc, parent, nodes, targets)
    node_hist = hist.reshape(2, nodes, local_targets, span)
    return (node_hist, split_gain, best[:, 0])


def solution(mesh):
    return jax.shard_map(
        local,
        mesh=mesh,
        in_specs=(
            P("rows", None),
            P("rows"),
            P("rows", "outs"),
            P("rows", "outs"),
            P(),
            P(),
            P(None, None, "outs", "rows"),
        ),
        out_specs=(P(None, None, "outs", "rows"), P(None, "rows"), P()),
        check_vma=False,
    )
```

```python
import functools

import jax
import jax.numpy as jnp
import numpy as np
from jax import lax
from jax.experimental import pallas as pl
from jax.experimental.pallas import tpu as pltpu
from jax.sharding import PartitionSpec as P

BINS = 32


MESH_ID = pl.DeviceIdType.MESH


def row_stages(r, n_rows):
    chips = n_rows // 2
    nx = 4 if chips % 4 == 0 else chips
    ny = chips // nx
    chip = r // 2
    core = r % 2
    y = chip // nx
    x = chip % nx
    row = 2 * nx
    stages = [
        [y * row + (r - y * row + k) % row for k in range(1, row)],
        [(((y + k) % ny) * nx + x) * 2 + core for k in range(1, ny)],
    ]
    return [stage for stage in stages if stage]


def row_peers(r, n_rows):
    return [peer for stage in row_stages(r, n_rows) for peer in stage]


def exchange(partial, split_ref, best_ref, gbuf, mbuf, gsend, grecv, msend, mrecv, targets):
    n_rows = lax.axis_size("rows")
    n_outs = lax.axis_size("outs")
    r = lax.axis_index("rows")
    o = lax.axis_index("outs")
    gbuf[o] = partial
    sends = []
    for k in range(1, n_outs):
        copy = pltpu.make_async_remote_copy(
            src_ref=gbuf.at[o],
            dst_ref=gbuf.at[o],
            send_sem=gsend.at[k],
            recv_sem=grecv.at[o],
            device_id=(r, (o + k) % n_outs),
            device_id_type=MESH_ID,
        )
        copy.start()
        sends.append(copy)
    for k in range(1, n_outs):
        src = (o + n_outs - k) % n_outs
        pltpu.make_async_remote_copy(
            src_ref=gbuf.at[o],
            dst_ref=gbuf.at[src],
            send_sem=gsend.at[k],
            recv_sem=grecv.at[src],
            device_id=(r, src),
            device_id_type=MESH_ID,
        ).wait_recv()
    for copy in sends:
        copy.wait_send()
    acc = gbuf[0]
    for j in range(1, n_outs):
        acc = acc + gbuf[j]
    split = acc / targets
    split_ref[...] = split
    width = mbuf.shape[2]
    best = jnp.broadcast_to(jnp.max(split, axis=1, keepdims=True), (split.shape[0], width))
    base = 0
    for peers in row_stages(r, n_rows):
        mbuf[base] = best
        sends = []
        for j, peer in enumerate(peers):
            copy = pltpu.make_async_remote_copy(
                src_ref=mbuf.at[base],
                dst_ref=mbuf.at[base + 1 + j],
                send_sem=msend.at[base + 1 + j],
                recv_sem=mrecv.at[base + 1 + j],
                device_id=(peer, o),
                device_id_type=MESH_ID,
            )
            copy.start()
            sends.append(copy)
        for copy in sends:
            copy.wait_recv()
        for copy in sends:
            copy.wait_send()
        for j in range(len(peers)):
            best = jnp.maximum(best, mbuf[base + 1 + j])
        base += len(peers) + 1
    best_ref[...] = best


def block_hist(acc_ref, v, s, nodes):
    tl = v.shape[0] // 2
    half = s.shape[1]
    feats = s.shape[0] // 2
    one = jnp.ones((), jnp.bfloat16)
    zero = jnp.zeros((), jnp.bfloat16)
    bins = lax.broadcasted_iota(jnp.int32, (BINS, half), 0)
    for h in range(2):
        vh = v[:, h * half : (h + 1) * half]
        node = s[h : h + 1] >> 5
        onehot = jnp.concatenate(
            [jnp.where((s[2 * f + h : 2 * f + h + 1] & (BINS - 1)) == bins, one, zero) for f in range(feats)],
            axis=0,
        )
        blocks = []
        for c in range(2):
            vc = vh[c * tl : (c + 1) * tl]
            for n in range(nodes):
                blocks.append(jnp.where(node == n, vc, zero))
        vals = jnp.concatenate(blocks, axis=0)
        acc_ref[...] += lax.dot_general(
            vals, onehot, (((1,), (1,)), ((), ())), preferred_element_type=jnp.float32
        )


def relay_gather(acc_ref, seg_ref, v_ref, vbuf, sbuf, vsend, fsend, vrecv, s_copy, send_seg, nodes):
    n_rows = lax.axis_size("rows")
    r = lax.axis_index("rows")
    o = lax.axis_index("outs")
    core = r % 2
    chip = r // 2
    y = chip // 4
    x = chip % 4
    a = x + core * (y - x)
    b = y + core * (x - y)
    partner = chip * 2 + 1 - core

    def dev(da, db):
        ap = (a + da + 4) % 4
        bp = (b + db + 4) % 4
        return ((1 - core) * (bp * 4 + ap) + core * (ap * 4 + bp)) * 2 + core

    def copy(src, sem, peer, slot):
        return pltpu.make_async_remote_copy(
            src_ref=src, dst_ref=vbuf.at[slot], send_sem=sem, recv_sem=vrecv.at[slot],
            device_id=(peer, o), device_id_type=MESH_ID,
        )

    def arrive(slot):
        copy(vbuf.at[slot], vsend.at[0], partner, slot).wait_recv()
        s_copy(0, slot, slot).wait_recv()

    def compute(slot):
        block_hist(acc_ref, vbuf[slot], sbuf[slot].astype(jnp.int32), nodes)

    started = []

    def start(src, sem, peer, slot):
        c = copy(src, sem, peer, slot)
        c.start()
        started.append(c)

    start(v_ref, fsend.at[0], partner, r)
    for j, (da, db) in enumerate([(1, 0), (-1, 0), (0, 1), (0, -1)]):
        start(v_ref, vsend.at[j], dev(da, db), r)
    lax.fori_loop(1, n_rows, send_seg, 0)

    sem = 4
    for j, da in enumerate([-1, 1, -2]):
        slot = dev(da, 0)
        arrive(slot)
        if da == -1:
            start(vbuf.at[slot], vsend.at[sem], dev(1, 0), slot)
            sem += 1
        start(vbuf.at[slot], vsend.at[sem], dev(0, 1), slot)
        start(vbuf.at[slot], vsend.at[sem + 1], dev(0, -1), slot)
        sem += 2
        start(vbuf.at[slot], fsend.at[1 + j], partner, slot)
        compute(slot)

    def row_step(db, relay, first):
        def body(i, carry):
            slot = dev((i * 3) % 4, db)
            arrive(slot)
            if relay:
                copy(vbuf.at[slot], vsend.at[11 + i], dev(0, -db), slot).start()
            copy(vbuf.at[slot], fsend.at[first + i], partner, slot).start()
            compute(slot)
            return carry

        return body

    def row_drain(db, relay, first):
        def body(i, carry):
            slot = dev((i * 3) % 4, db)
            if relay:
                copy(vbuf.at[slot], vsend.at[11 + i], dev(0, -db), slot).wait_send()
            copy(vbuf.at[slot], fsend.at[first + i], partner, slot).wait_send()
            return carry

        return body

    rows_plan = [(-1, True, 4, 0, 2), (1, False, 8, 0, 2), (-1, False, 4, 2, 4), (1, True, 8, 2, 4), (2, False, 12, 0, 4)]
    for db, relay, first, lo, hi in rows_plan:
        lax.fori_loop(lo, hi, row_step(db, relay, first), 0)

    def take_partner(k, carry):
        slot = ((chip + 16 - k) % 16) * 2 + 1 - core
        arrive(slot)
        compute(slot)
        return carry

    lax.fori_loop(0, 16, take_partner, 0)
    for c in started:
        c.wait_send()
    for db, relay, first, lo, hi in rows_plan:
        lax.fori_loop(lo, hi, row_drain(db, relay, first), 0)


def gather_hist_kernel(
    small_ref, evict_ref, seg_ref, v_ref, parent_ref, hist_ref, split_ref, best_ref,
    acc_ref, vbuf, sbuf, vsend, fsend, vrecv, ssend, srecv, gbuf, mbuf, gsend, grecv, msend, mrecv,
    *, nodes, targets,
):
    n_rows = lax.axis_size("rows")
    chips = n_rows // 2
    r = lax.axis_index("rows")
    o = lax.axis_index("outs")
    core = r % 2
    chip = r // 2
    partner = chip * 2 + 1 - core
    barrier = pltpu.get_barrier_semaphore()

    def greet(k, carry):
        pl.semaphore_signal(barrier, 1, device_id=((r + k) % n_rows, o), device_id_type=MESH_ID)
        return carry

    lax.fori_loop(1, n_rows, greet, 0)
    n_outs = lax.axis_size("outs")
    for k in range(1, n_outs):
        pl.semaphore_signal(barrier, 1, device_id=(r, (o + k) % n_outs), device_id_type=MESH_ID)
    acc_ref[...] = jnp.zeros_like(acc_ref)
    block_hist(acc_ref, v_ref[...], seg_ref[r].astype(jnp.int32), nodes)
    pl.semaphore_wait(barrier, n_rows - 1 + n_outs - 1)

    def s_copy(k, peer, slot):
        return pltpu.make_async_remote_copy(
            src_ref=seg_ref.at[peer], dst_ref=sbuf.at[slot], send_sem=ssend.at[k], recv_sem=srecv.at[slot],
            device_id=(peer, o), device_id_type=MESH_ID,
        )

    def v_copy(k, peer, slot):
        return pltpu.make_async_remote_copy(
            src_ref=v_ref, dst_ref=vbuf.at[slot], send_sem=vsend.at[k], recv_sem=vrecv.at[slot],
            device_id=(peer, o), device_id_type=MESH_ID,
        )

    def f_copy(k, slot):
        return pltpu.make_async_remote_copy(
            src_ref=vbuf.at[slot], dst_ref=vbuf.at[slot], send_sem=fsend.at[k], recv_sem=vrecv.at[slot],
            device_id=(partner, o), device_id_type=MESH_ID,
        )

    def send_seg(k, carry):
        s_copy(k, (r + k) % n_rows, r).start()
        return carry

    def drain(k, carry):
        s_copy(k, (r + k) % n_rows, r).wait_send()
        return carry

    if chips == 16:
        relay_gather(acc_ref, seg_ref, v_ref, vbuf, sbuf, vsend, fsend, vrecv, s_copy, send_seg, nodes)
        lax.fori_loop(1, n_rows, drain, 0)
    else:
        own = pltpu.make_async_remote_copy(
            src_ref=v_ref, dst_ref=vbuf.at[r], send_sem=fsend.at[0], recv_sem=vrecv.at[r],
            device_id=(partner, o), device_id_type=MESH_ID,
        )
        own.start()

        def send(k, carry):
            v_copy(k, ((chip + k) % chips) * 2 + core, r).start()
            return carry

        lax.fori_loop(1, chips, send, 0)

        lax.fori_loop(1, n_rows, send_seg, 0)

        def take_direct(k, carry):
            src = ((chip + chips - k) % chips) * 2 + core
            v_copy(k, src, src).wait_recv()
            f_copy(k, src).start()
            s_copy(k, src, src).wait_recv()
            block_hist(acc_ref, vbuf[src], sbuf[src].astype(jnp.int32), nodes)
            return carry

        lax.fori_loop(1, chips, take_direct, 0)

        def take_forwarded(k, carry):
            src = ((chip + chips - k) % chips) * 2 + 1 - core
            f_copy(k, src).wait_recv()
            s_copy(k, src, src).wait_recv()
            block_hist(acc_ref, vbuf[src], sbuf[src].astype(jnp.int32), nodes)
            return carry

        lax.fori_loop(0, chips, take_forwarded, 0)

        lax.fori_loop(1, n_rows, drain, 0)

        def drain_v(k, carry):
            v_copy(k, ((chip + k) % chips) * 2 + core, r).wait_send()
            return carry

        lax.fori_loop(1, chips, drain_v, 0)
        own.wait_send()

        def drain_f(k, carry):
            f_copy(k, ((chip + chips - k) % chips) * 2 + core).wait_send()
            return carry

        lax.fori_loop(1, chips, drain_f, 0)


    node_hist(acc_ref, parent_ref, small_ref, evict_ref, hist_ref, nodes)
    partial = gain_terms(hist_ref, nodes)
    exchange(partial, split_ref, best_ref, gbuf, mbuf, gsend, grecv, msend, mrecv, targets)


def node_hist(acc_ref, parent_ref, small_ref, evict_ref, hist_ref, nodes):
    pairs = nodes // 2
    tl = acc_ref.shape[0] // (2 * nodes)
    for c in range(2):
        for p in range(pairs):
            lo = c * nodes * tl + 2 * p * tl
            a = acc_ref[lo : lo + tl]
            b = acc_ref[lo + tl : lo + 2 * tl]
            base = (c * pairs + p) * tl
            parent = parent_ref[base : base + tl]
            small = small_ref[p] == 0
            gone = evict_ref[p] == 1
            child = jnp.where(small, a, b)
            rebuilt = jnp.where(small, b, a)
            sibling = jnp.where(gone, rebuilt, parent - child)
            hist_ref[lo : lo + tl] = jnp.where(small, child, sibling)
            hist_ref[lo + tl : lo + 2 * tl] = jnp.where(small, sibling, child)


def group_scan(x, reverse):
    span = x.shape[1]
    lane = lax.broadcasted_iota(jnp.int32, x.shape, 1) % BINS
    shift = 1
    while shift < BINS:
        if reverse:
            moved = pltpu.roll(x, span - shift, 1)
            x = x + jnp.where(lane + shift < BINS, moved, 0.0)
        else:
            moved = pltpu.roll(x, shift, 1)
            x = x + jnp.where(lane >= shift, moved, 0.0)
        shift *= 2
    return x


def gain_terms(hist_ref, nodes):
    rows, span = hist_ref.shape
    half = rows // 2
    tl = half // nodes
    lane = lax.broadcasted_iota(jnp.int32, (half, span), 1) % BINS
    left_g = group_scan(hist_ref[0:half], False)
    left_h = group_scan(hist_ref[half:rows], False)
    total_g = group_scan(jnp.where(lane == BINS - 1, left_g, 0.0), True)
    total_h = group_scan(jnp.where(lane == BINS - 1, left_h, 0.0), True)

    def score(a, s):
        return a * a / (jnp.maximum(s, 0.0) + 1.0)

    gain = (
        score(left_g, left_h) + score(total_g - left_g, total_h - left_h) - score(total_g, total_h)
    )
    return jnp.sum(gain.reshape(nodes, tl, span), axis=1)


def gather_hist(small_side, evicted, seg_p, v_loc, parent, nodes, targets):
    n_rows, width, half = seg_p.shape
    n_outs = lax.axis_size("outs")
    vw, rows = v_loc.shape
    feats = width // 2
    out_rows = vw * nodes
    cols = feats * BINS
    total = n_rows * rows
    vmem = pl.BlockSpec(memory_space=pltpu.VMEM)
    smem = pl.BlockSpec(memory_space=pltpu.SMEM)
    return pl.pallas_call(
        functools.partial(gather_hist_kernel, nodes=nodes, targets=targets),
        out_shape=(
            jax.ShapeDtypeStruct((out_rows, cols), jnp.float32),
            jax.ShapeDtypeStruct((nodes, cols), jnp.float32),
            jax.ShapeDtypeStruct((nodes, 128), jnp.float32),
        ),
        in_specs=[smem, smem, vmem, vmem, vmem],
        out_specs=(vmem, vmem, vmem),
        scratch_shapes=[
            pltpu.VMEM((out_rows, cols), jnp.float32),
            pltpu.VMEM((n_rows, vw, rows), v_loc.dtype),
            pltpu.VMEM((n_rows, width, half), seg_p.dtype),
            pltpu.SemaphoreType.DMA((n_rows // 2,)),
            pltpu.SemaphoreType.DMA((n_rows // 2,)),
            pltpu.SemaphoreType.DMA((n_rows,)),
            pltpu.SemaphoreType.DMA((n_rows,)),
            pltpu.SemaphoreType.DMA((n_rows,)),
            pltpu.VMEM((n_outs, nodes, cols), jnp.float32),
            pltpu.VMEM((n_rows, nodes, 128), jnp.float32),
            pltpu.SemaphoreType.DMA((n_outs,)),
            pltpu.SemaphoreType.DMA((n_outs,)),
            pltpu.SemaphoreType.DMA((n_rows,)),
            pltpu.SemaphoreType.DMA((n_rows,)),
        ],
        compiler_params=pltpu.CompilerParams(collective_id=1, has_side_effects=True),
        cost_estimate=pl.CostEstimate(
            flops=2 * out_rows * cols * total,
            bytes_accessed=total * (vw * 2 + feats * 2) + out_rows * cols * 4,
            transcendentals=0,
        ),
    )(small_side, evicted, seg_p, v_loc, parent)


def pair_split_kernel(
    small_ref, evict_ref, seg_ref, v_ref, parent_ref, hist_ref, split_ref, best_ref,
    acc_ref, vbuf, sbuf, pbuf, vsend, vrecv, ssend, srecv, psend, precv, gbuf, mbuf, gsend, grecv, msend, mrecv,
    *, nodes, targets,
):
    n_rows = lax.axis_size("rows")
    n_outs = lax.axis_size("outs")
    r = lax.axis_index("rows")
    o = lax.axis_index("outs")
    core = r % 2
    chip = r // 2
    y = chip // 4
    x = chip % 4
    a = x + core * (y - x)
    b = y + core * (x - y)
    partner = chip * 2 + 1 - core
    barrier = pltpu.get_barrier_semaphore()

    def greet(k, carry):
        pl.semaphore_signal(barrier, 1, device_id=((r + k) % n_rows, o), device_id_type=MESH_ID)
        return carry

    lax.fori_loop(1, n_rows, greet, 0)
    for k in range(1, n_outs):
        pl.semaphore_signal(barrier, 1, device_id=(r, (o + k) % n_outs), device_id_type=MESH_ID)
    acc_ref[...] = jnp.zeros_like(acc_ref)
    block_hist(acc_ref, v_ref[...], seg_ref[chip].astype(jnp.int32), nodes)
    pl.semaphore_wait(barrier, n_rows - 1 + n_outs - 1)

    def dev(da, db):
        ap = (a + da + 4) % 4
        bp = (b + db + 4) % 4
        return ((1 - core) * (bp * 4 + ap) + core * (ap * 4 + bp)) * 2 + core

    def copy(src, sem, peer, slot):
        return pltpu.make_async_remote_copy(
            src_ref=src, dst_ref=vbuf.at[slot], send_sem=sem, recv_sem=vrecv.at[slot],
            device_id=(peer, o), device_id_type=MESH_ID,
        )

    def s_copy(k, peer, slot):
        return pltpu.make_async_remote_copy(
            src_ref=seg_ref.at[peer // 2], dst_ref=sbuf.at[slot], send_sem=ssend.at[k], recv_sem=srecv.at[slot],
            device_id=(peer, o), device_id_type=MESH_ID,
        )

    def seg_peer(k):
        return ((chip + k) % 16) * 2 + core

    def arrive(slot):
        copy(vbuf.at[slot], vsend.at[0], partner, slot).wait_recv()
        s_copy(0, slot, slot).wait_recv()

    def compute(slot):
        block_hist(acc_ref, vbuf[slot], sbuf[slot].astype(jnp.int32), nodes)

    started = []

    def start(src, sem, peer, slot):
        c = copy(src, sem, peer, slot)
        c.start()
        started.append(c)

    for j, (da, db) in enumerate([(1, 0), (-1, 0), (0, 1), (0, -1)]):
        start(v_ref, vsend.at[j], dev(da, db), r)

    def send_seg(k, carry):
        s_copy(k, seg_peer(k), r).start()
        return carry

    lax.fori_loop(1, 16, send_seg, 0)

    sem = 4
    for da in [-1, 1, -2]:
        slot = dev(da, 0)
        arrive(slot)
        if da == -1:
            start(vbuf.at[slot], vsend.at[sem], dev(1, 0), slot)
            sem += 1
        start(vbuf.at[slot], vsend.at[sem], dev(0, 1), slot)
        start(vbuf.at[slot], vsend.at[sem + 1], dev(0, -1), slot)
        sem += 2
        compute(slot)

    def row_step(db, relay):
        def body(i, carry):
            slot = dev((i * 3) % 4, db)
            arrive(slot)
            if relay:
                copy(vbuf.at[slot], vsend.at[11 + i], dev(0, 1), slot).start()
            compute(slot)
            return carry

        return body

    for db, relay in [(-1, True), (1, False), (-2, False)]:
        lax.fori_loop(0, 4, row_step(db, relay), 0)

    span = hist_ref.shape[1]
    mine = pl.ds(pl.multiple_of(core * span, span), span)
    theirs = pl.ds(pl.multiple_of((1 - core) * span, span), span)
    swap = pltpu.make_async_remote_copy(
        src_ref=acc_ref.at[:, theirs], dst_ref=pbuf, send_sem=psend, recv_sem=precv,
        device_id=(partner, o), device_id_type=MESH_ID,
    )
    swap.start()
    swap.wait_recv()
    hist_ref[...] = acc_ref[:, mine] + pbuf[...]
    swap.wait_send()
    for c in started:
        c.wait_send()

    def relay_drain(i, carry):
        slot = dev((i * 3) % 4, -1)
        copy(vbuf.at[slot], vsend.at[11 + i], dev(0, 1), slot).wait_send()
        return carry

    lax.fori_loop(0, 4, relay_drain, 0)

    def drain(k, carry):
        s_copy(k, seg_peer(k), r).wait_send()
        return carry

    lax.fori_loop(1, 16, drain, 0)

    node_hist(hist_ref, parent_ref, small_ref, evict_ref, hist_ref, nodes)
    partial = gain_terms(hist_ref, nodes)
    exchange(partial, split_ref, best_ref, gbuf, mbuf, gsend, grecv, msend, mrecv, targets)


def pair_split(small_side, evicted, seg_c, v_loc, parent, nodes, targets):
    chips, width, half = seg_c.shape
    n_rows = 2 * chips
    n_outs = lax.axis_size("outs")
    vw, rows = v_loc.shape
    cols = width // 2 * BINS
    span = cols // 2
    out_rows = vw * nodes
    total = n_rows * rows
    vmem = pl.BlockSpec(memory_space=pltpu.VMEM)
    smem = pl.BlockSpec(memory_space=pltpu.SMEM)
    return pl.pallas_call(
        functools.partial(pair_split_kernel, nodes=nodes, targets=targets),
        out_shape=(
            jax.ShapeDtypeStruct((out_rows, span), jnp.float32),
            jax.ShapeDtypeStruct((nodes, span), jnp.float32),
            jax.ShapeDtypeStruct((nodes, 128), jnp.float32),
        ),
        in_specs=[smem, smem, vmem, vmem, vmem],
        out_specs=(vmem, vmem, vmem),
        scratch_shapes=[
            pltpu.VMEM((out_rows, cols), jnp.float32),
            pltpu.VMEM((n_rows, vw, rows), v_loc.dtype),
            pltpu.VMEM((n_rows, width, half), seg_c.dtype),
            pltpu.VMEM((out_rows, span), jnp.float32),
            pltpu.SemaphoreType.DMA((chips,)),
            pltpu.SemaphoreType.DMA((n_rows,)),
            pltpu.SemaphoreType.DMA((chips,)),
            pltpu.SemaphoreType.DMA((n_rows,)),
            pltpu.SemaphoreType.DMA(()),
            pltpu.SemaphoreType.DMA(()),
            pltpu.VMEM((n_outs, nodes, span), jnp.float32),
            pltpu.VMEM((n_rows, nodes, 128), jnp.float32),
            pltpu.SemaphoreType.DMA((n_outs,)),
            pltpu.SemaphoreType.DMA((n_outs,)),
            pltpu.SemaphoreType.DMA((n_rows,)),
            pltpu.SemaphoreType.DMA((n_rows,)),
        ],
        compiler_params=pltpu.CompilerParams(collective_id=2, has_side_effects=True),
        cost_estimate=pl.CostEstimate(
            flops=2 * out_rows * cols * total // 2,
            bytes_accessed=total * (vw * 2 + width) + out_rows * cols * 4,
            transcendentals=0,
        ),
    )(small_side, evicted, seg_c, v_loc, parent)


def local(codes, node_of_row, grad, hess, small_side, evicted, parent_hist):
    pairs = small_side.shape[0]
    nodes = 2 * pairs
    local_targets = grad.shape[1]
    targets = local_targets * lax.axis_size("outs")
    n_rows = lax.axis_size("rows")
    count, features = codes.shape
    feats = features // n_rows
    half = count // 2
    seg = (node_of_row[:, None] * BINS + codes).astype(jnp.int16)
    seg_p = jnp.transpose(seg.reshape(2, half, n_rows, feats), (2, 3, 0, 1)).reshape(n_rows, 2 * feats, half)
    v_loc = jnp.concatenate([grad.T, hess.T], axis=0)
    span = feats * BINS
    parent = parent_hist.reshape(2 * pairs * local_targets, span)
    if n_rows == 32:
        seg_c = jnp.transpose(seg.reshape(2, half, n_rows // 2, 2 * feats), (2, 3, 0, 1)).reshape(
            n_rows // 2, 4 * feats, half
        )
        hist, split_gain, best = pair_split(small_side, evicted, seg_c, v_loc, parent, nodes, targets)
    else:
        hist, split_gain, best = gather_hist(small_side, evicted, seg_p, v_loc, parent, nodes, targets)
    node_hist = hist.reshape(2, nodes, local_targets, span)
    return (node_hist, split_gain, best[:, 0])


def solution(mesh):
    return jax.shard_map(
        local,
        mesh=mesh,
        in_specs=(
            P("rows", None),
            P("rows"),
            P("rows", "outs"),
            P("rows", "outs"),
            P(),
            P(),
            P(None, None, "outs", "rows"),
        ),
        out_specs=(P(None, None, "outs", "rows"), P(None, "rows"), P()),
        check_vma=False,
    )
```

```python
import functools

import jax
import jax.numpy as jnp
import numpy as np
from jax import lax
from jax.experimental import pallas as pl
from jax.experimental.pallas import tpu as pltpu
from jax.sharding import PartitionSpec as P

BINS = 32


MESH_ID = pl.DeviceIdType.MESH


def row_stages(r, n_rows):
    chips = n_rows // 2
    nx = 4 if chips % 4 == 0 else chips
    ny = chips // nx
    chip = r // 2
    core = r % 2
    y = chip // nx
    x = chip % nx
    row = 2 * nx
    stages = [
        [y * row + (r - y * row + k) % row for k in range(1, row)],
        [(((y + k) % ny) * nx + x) * 2 + core for k in range(1, ny)],
    ]
    return [stage for stage in stages if stage]


def row_peers(r, n_rows):
    return [peer for stage in row_stages(r, n_rows) for peer in stage]


def exchange(partial, split_ref, best_ref, gbuf, mbuf, gsend, grecv, msend, mrecv, targets):
    n_rows = lax.axis_size("rows")
    n_outs = lax.axis_size("outs")
    r = lax.axis_index("rows")
    o = lax.axis_index("outs")
    gbuf[o] = partial
    sends = []
    for k in range(1, n_outs):
        copy = pltpu.make_async_remote_copy(
            src_ref=gbuf.at[o],
            dst_ref=gbuf.at[o],
            send_sem=gsend.at[k],
            recv_sem=grecv.at[o],
            device_id=(r, (o + k) % n_outs),
            device_id_type=MESH_ID,
        )
        copy.start()
        sends.append(copy)
    for k in range(1, n_outs):
        src = (o + n_outs - k) % n_outs
        pltpu.make_async_remote_copy(
            src_ref=gbuf.at[o],
            dst_ref=gbuf.at[src],
            send_sem=gsend.at[k],
            recv_sem=grecv.at[src],
            device_id=(r, src),
            device_id_type=MESH_ID,
        ).wait_recv()
    for copy in sends:
        copy.wait_send()
    acc = gbuf[0]
    for j in range(1, n_outs):
        acc = acc + gbuf[j]
    split = acc / targets
    split_ref[...] = split
    width = mbuf.shape[2]
    best = jnp.broadcast_to(jnp.max(split, axis=1, keepdims=True), (split.shape[0], width))
    base = 0
    for peers in row_stages(r, n_rows):
        mbuf[base] = best
        sends = []
        for j, peer in enumerate(peers):
            copy = pltpu.make_async_remote_copy(
                src_ref=mbuf.at[base],
                dst_ref=mbuf.at[base + 1 + j],
                send_sem=msend.at[base + 1 + j],
                recv_sem=mrecv.at[base + 1 + j],
                device_id=(peer, o),
                device_id_type=MESH_ID,
            )
            copy.start()
            sends.append(copy)
        for copy in sends:
            copy.wait_recv()
        for copy in sends:
            copy.wait_send()
        for j in range(len(peers)):
            best = jnp.maximum(best, mbuf[base + 1 + j])
        base += len(peers) + 1
    best_ref[...] = best


def block_hist(acc_ref, v, s, nodes):
    tl = v.shape[0] // 2
    half = s.shape[1]
    feats = s.shape[0] // 2
    one = jnp.ones((), jnp.bfloat16)
    zero = jnp.zeros((), jnp.bfloat16)
    bins = lax.broadcasted_iota(jnp.int32, (BINS, half), 0)
    for h in range(2):
        vh = v[:, h * half : (h + 1) * half]
        node = s[h : h + 1] >> 5
        onehot = jnp.concatenate(
            [jnp.where((s[2 * f + h : 2 * f + h + 1] & (BINS - 1)) == bins, one, zero) for f in range(feats)],
            axis=0,
        )
        blocks = []
        for c in range(2):
            vc = vh[c * tl : (c + 1) * tl]
            for n in range(nodes):
                blocks.append(jnp.where(node == n, vc, zero))
        vals = jnp.concatenate(blocks, axis=0)
        acc_ref[...] += lax.dot_general(
            vals, onehot, (((1,), (1,)), ((), ())), preferred_element_type=jnp.float32
        )


def relay_gather(acc_ref, seg_ref, v_ref, vbuf, sbuf, vsend, fsend, vrecv, s_copy, send_seg, nodes):
    n_rows = lax.axis_size("rows")
    r = lax.axis_index("rows")
    o = lax.axis_index("outs")
    core = r % 2
    chip = r // 2
    y = chip // 4
    x = chip % 4
    a = x + core * (y - x)
    b = y + core * (x - y)
    partner = chip * 2 + 1 - core

    def dev(da, db):
        ap = (a + da + 4) % 4
        bp = (b + db + 4) % 4
        return ((1 - core) * (bp * 4 + ap) + core * (ap * 4 + bp)) * 2 + core

    def copy(src, sem, peer, slot):
        return pltpu.make_async_remote_copy(
            src_ref=src, dst_ref=vbuf.at[slot], send_sem=sem, recv_sem=vrecv.at[slot],
            device_id=(peer, o), device_id_type=MESH_ID,
        )

    def arrive(slot):
        copy(vbuf.at[slot], vsend.at[0], partner, slot).wait_recv()
        s_copy(0, slot, slot).wait_recv()

    def compute(slot):
        block_hist(acc_ref, vbuf[slot], sbuf[slot].astype(jnp.int32), nodes)

    started = []

    def start(src, sem, peer, slot):
        c = copy(src, sem, peer, slot)
        c.start()
        started.append(c)

    start(v_ref, fsend.at[0], partner, r)
    for j, (da, db) in enumerate([(1, 0), (-1, 0), (0, 1), (0, -1)]):
        start(v_ref, vsend.at[j], dev(da, db), r)
    lax.fori_loop(1, n_rows, send_seg, 0)

    sem = 4
    for j, da in enumerate([-1, 1, -2]):
        slot = dev(da, 0)
        arrive(slot)
        if da == -1:
            start(vbuf.at[slot], vsend.at[sem], dev(1, 0), slot)
            sem += 1
        start(vbuf.at[slot], vsend.at[sem], dev(0, 1), slot)
        start(vbuf.at[slot], vsend.at[sem + 1], dev(0, -1), slot)
        sem += 2
        start(vbuf.at[slot], fsend.at[1 + j], partner, slot)
        compute(slot)

    def row_step(db, relay, first):
        def body(i, carry):
            slot = dev((i * 3) % 4, db)
            arrive(slot)
            if relay:
                copy(vbuf.at[slot], vsend.at[11 + i], dev(0, -db), slot).start()
            copy(vbuf.at[slot], fsend.at[first + i], partner, slot).start()
            compute(slot)
            return carry

        return body

    def row_drain(db, relay, first):
        def body(i, carry):
            slot = dev((i * 3) % 4, db)
            if relay:
                copy(vbuf.at[slot], vsend.at[11 + i], dev(0, -db), slot).wait_send()
            copy(vbuf.at[slot], fsend.at[first + i], partner, slot).wait_send()
            return carry

        return body

    rows_plan = [(-1, True, 4, 0, 2), (1, False, 8, 0, 2), (-1, False, 4, 2, 4), (1, True, 8, 2, 4), (2, False, 12, 0, 4)]
    for db, relay, first, lo, hi in rows_plan:
        lax.fori_loop(lo, hi, row_step(db, relay, first), 0)

    def take_partner(k, carry):
        slot = ((chip + 16 - k) % 16) * 2 + 1 - core
        arrive(slot)
        compute(slot)
        return carry

    lax.fori_loop(0, 16, take_partner, 0)
    for c in started:
        c.wait_send()
    for db, relay, first, lo, hi in rows_plan:
        lax.fori_loop(lo, hi, row_drain(db, relay, first), 0)


def gather_hist_kernel(
    small_ref, evict_ref, seg_ref, v_ref, parent_ref, hist_ref, split_ref, best_ref,
    acc_ref, vbuf, sbuf, vsend, fsend, vrecv, ssend, srecv, gbuf, mbuf, gsend, grecv, msend, mrecv,
    *, nodes, targets,
):
    n_rows = lax.axis_size("rows")
    chips = n_rows // 2
    r = lax.axis_index("rows")
    o = lax.axis_index("outs")
    core = r % 2
    chip = r // 2
    partner = chip * 2 + 1 - core
    barrier = pltpu.get_barrier_semaphore()

    def greet(k, carry):
        pl.semaphore_signal(barrier, 1, device_id=((r + k) % n_rows, o), device_id_type=MESH_ID)
        return carry

    lax.fori_loop(1, n_rows, greet, 0)
    n_outs = lax.axis_size("outs")
    for k in range(1, n_outs):
        pl.semaphore_signal(barrier, 1, device_id=(r, (o + k) % n_outs), device_id_type=MESH_ID)
    acc_ref[...] = jnp.zeros_like(acc_ref)
    block_hist(acc_ref, v_ref[...], seg_ref[r].astype(jnp.int32), nodes)
    pl.semaphore_wait(barrier, n_rows - 1 + n_outs - 1)

    def s_copy(k, peer, slot):
        return pltpu.make_async_remote_copy(
            src_ref=seg_ref.at[peer], dst_ref=sbuf.at[slot], send_sem=ssend.at[k], recv_sem=srecv.at[slot],
            device_id=(peer, o), device_id_type=MESH_ID,
        )

    def v_copy(k, peer, slot):
        return pltpu.make_async_remote_copy(
            src_ref=v_ref, dst_ref=vbuf.at[slot], send_sem=vsend.at[k], recv_sem=vrecv.at[slot],
            device_id=(peer, o), device_id_type=MESH_ID,
        )

    def f_copy(k, slot):
        return pltpu.make_async_remote_copy(
            src_ref=vbuf.at[slot], dst_ref=vbuf.at[slot], send_sem=fsend.at[k], recv_sem=vrecv.at[slot],
            device_id=(partner, o), device_id_type=MESH_ID,
        )

    def send_seg(k, carry):
        s_copy(k, (r + k) % n_rows, r).start()
        return carry

    def drain(k, carry):
        s_copy(k, (r + k) % n_rows, r).wait_send()
        return carry

    if chips == 16:
        relay_gather(acc_ref, seg_ref, v_ref, vbuf, sbuf, vsend, fsend, vrecv, s_copy, send_seg, nodes)
        lax.fori_loop(1, n_rows, drain, 0)
    else:
        own = pltpu.make_async_remote_copy(
            src_ref=v_ref, dst_ref=vbuf.at[r], send_sem=fsend.at[0], recv_sem=vrecv.at[r],
            device_id=(partner, o), device_id_type=MESH_ID,
        )
        own.start()

        def send(k, carry):
            v_copy(k, ((chip + k) % chips) * 2 + core, r).start()
            return carry

        lax.fori_loop(1, chips, send, 0)

        lax.fori_loop(1, n_rows, send_seg, 0)

        def take_direct(k, carry):
            src = ((chip + chips - k) % chips) * 2 + core
            v_copy(k, src, src).wait_recv()
            f_copy(k, src).start()
            s_copy(k, src, src).wait_recv()
            block_hist(acc_ref, vbuf[src], sbuf[src].astype(jnp.int32), nodes)
            return carry

        lax.fori_loop(1, chips, take_direct, 0)

        def take_forwarded(k, carry):
            src = ((chip + chips - k) % chips) * 2 + 1 - core
            f_copy(k, src).wait_recv()
            s_copy(k, src, src).wait_recv()
            block_hist(acc_ref, vbuf[src], sbuf[src].astype(jnp.int32), nodes)
            return carry

        lax.fori_loop(0, chips, take_forwarded, 0)

        lax.fori_loop(1, n_rows, drain, 0)

        def drain_v(k, carry):
            v_copy(k, ((chip + k) % chips) * 2 + core, r).wait_send()
            return carry

        lax.fori_loop(1, chips, drain_v, 0)
        own.wait_send()

        def drain_f(k, carry):
            f_copy(k, ((chip + chips - k) % chips) * 2 + core).wait_send()
            return carry

        lax.fori_loop(1, chips, drain_f, 0)


    node_hist(acc_ref, parent_ref, small_ref, evict_ref, hist_ref, nodes)
    partial = gain_terms(hist_ref, nodes)
    exchange(partial, split_ref, best_ref, gbuf, mbuf, gsend, grecv, msend, mrecv, targets)


def node_hist(acc_ref, parent_ref, small_ref, evict_ref, hist_ref, nodes):
    pairs = nodes // 2
    tl = acc_ref.shape[0] // (2 * nodes)
    for c in range(2):
        for p in range(pairs):
            lo = c * nodes * tl + 2 * p * tl
            a = acc_ref[lo : lo + tl]
            b = acc_ref[lo + tl : lo + 2 * tl]
            base = (c * pairs + p) * tl
            parent = parent_ref[base : base + tl]
            small = small_ref[p] == 0
            gone = evict_ref[p] == 1
            child = jnp.where(small, a, b)
            rebuilt = jnp.where(small, b, a)
            sibling = jnp.where(gone, rebuilt, parent - child)
            hist_ref[lo : lo + tl] = jnp.where(small, child, sibling)
            hist_ref[lo + tl : lo + 2 * tl] = jnp.where(small, sibling, child)


def group_scan(x, reverse):
    span = x.shape[1]
    lane = lax.broadcasted_iota(jnp.int32, x.shape, 1) % BINS
    shift = 1
    while shift < BINS:
        if reverse:
            moved = pltpu.roll(x, span - shift, 1)
            x = x + jnp.where(lane + shift < BINS, moved, 0.0)
        else:
            moved = pltpu.roll(x, shift, 1)
            x = x + jnp.where(lane >= shift, moved, 0.0)
        shift *= 2
    return x


def gain_terms(hist_ref, nodes):
    rows, span = hist_ref.shape
    half = rows // 2
    tl = half // nodes
    lane = lax.broadcasted_iota(jnp.int32, (half, span), 1) % BINS
    left_g = group_scan(hist_ref[0:half], False)
    left_h = group_scan(hist_ref[half:rows], False)
    total_g = group_scan(jnp.where(lane == BINS - 1, left_g, 0.0), True)
    total_h = group_scan(jnp.where(lane == BINS - 1, left_h, 0.0), True)

    def score(a, s):
        return a * a / (jnp.maximum(s, 0.0) + 1.0)

    gain = (
        score(left_g, left_h) + score(total_g - left_g, total_h - left_h) - score(total_g, total_h)
    )
    return jnp.sum(gain.reshape(nodes, tl, span), axis=1)


def gather_hist(small_side, evicted, seg_p, v_loc, parent, nodes, targets):
    n_rows, width, half = seg_p.shape
    n_outs = lax.axis_size("outs")
    vw, rows = v_loc.shape
    feats = width // 2
    out_rows = vw * nodes
    cols = feats * BINS
    total = n_rows * rows
    vmem = pl.BlockSpec(memory_space=pltpu.VMEM)
    smem = pl.BlockSpec(memory_space=pltpu.SMEM)
    return pl.pallas_call(
        functools.partial(gather_hist_kernel, nodes=nodes, targets=targets),
        out_shape=(
            jax.ShapeDtypeStruct((out_rows, cols), jnp.float32),
            jax.ShapeDtypeStruct((nodes, cols), jnp.float32),
            jax.ShapeDtypeStruct((nodes, 128), jnp.float32),
        ),
        in_specs=[smem, smem, vmem, vmem, vmem],
        out_specs=(vmem, vmem, vmem),
        scratch_shapes=[
            pltpu.VMEM((out_rows, cols), jnp.float32),
            pltpu.VMEM((n_rows, vw, rows), v_loc.dtype),
            pltpu.VMEM((n_rows, width, half), seg_p.dtype),
            pltpu.SemaphoreType.DMA((n_rows // 2,)),
            pltpu.SemaphoreType.DMA((n_rows // 2,)),
            pltpu.SemaphoreType.DMA((n_rows,)),
            pltpu.SemaphoreType.DMA((n_rows,)),
            pltpu.SemaphoreType.DMA((n_rows,)),
            pltpu.VMEM((n_outs, nodes, cols), jnp.float32),
            pltpu.VMEM((n_rows, nodes, 128), jnp.float32),
            pltpu.SemaphoreType.DMA((n_outs,)),
            pltpu.SemaphoreType.DMA((n_outs,)),
            pltpu.SemaphoreType.DMA((n_rows,)),
            pltpu.SemaphoreType.DMA((n_rows,)),
        ],
        compiler_params=pltpu.CompilerParams(collective_id=1, has_side_effects=True),
        cost_estimate=pl.CostEstimate(
            flops=2 * out_rows * cols * total,
            bytes_accessed=total * (vw * 2 + feats * 2) + out_rows * cols * 4,
            transcendentals=0,
        ),
    )(small_side, evicted, seg_p, v_loc, parent)


def pair_split_kernel(
    small_ref, evict_ref, seg_ref, v_ref, parent_ref, hist_ref, split_ref, best_ref,
    acc_ref, vbuf, sbuf, pbuf, vsend, vrecv, ssend, srecv, psend, precv, gbuf, mbuf, gsend, grecv, msend, mrecv,
    *, nodes, targets,
):
    n_rows = lax.axis_size("rows")
    n_outs = lax.axis_size("outs")
    r = lax.axis_index("rows")
    o = lax.axis_index("outs")
    core = r % 2
    chip = r // 2
    y = chip // 4
    x = chip % 4
    a = x + core * (y - x)
    b = y + core * (x - y)
    partner = chip * 2 + 1 - core
    barrier = pltpu.get_barrier_semaphore()

    def greet(k, carry):
        pl.semaphore_signal(barrier, 1, device_id=((r + k) % n_rows, o), device_id_type=MESH_ID)
        return carry

    lax.fori_loop(1, n_rows, greet, 0)
    for k in range(1, n_outs):
        pl.semaphore_signal(barrier, 1, device_id=(r, (o + k) % n_outs), device_id_type=MESH_ID)
    acc_ref[...] = jnp.zeros_like(acc_ref)
    block_hist(acc_ref, v_ref[...], seg_ref[chip].astype(jnp.int32), nodes)
    pl.semaphore_wait(barrier, n_rows - 1 + n_outs - 1)

    def dev(da, db):
        ap = (a + da + 4) % 4
        bp = (b + db + 4) % 4
        return ((1 - core) * (bp * 4 + ap) + core * (ap * 4 + bp)) * 2 + core

    def copy(src, sem, peer, slot):
        return pltpu.make_async_remote_copy(
            src_ref=src, dst_ref=vbuf.at[slot], send_sem=sem, recv_sem=vrecv.at[slot],
            device_id=(peer, o), device_id_type=MESH_ID,
        )

    def s_copy(k, peer, slot):
        return pltpu.make_async_remote_copy(
            src_ref=seg_ref.at[peer // 2], dst_ref=sbuf.at[slot], send_sem=ssend.at[k], recv_sem=srecv.at[slot],
            device_id=(peer, o), device_id_type=MESH_ID,
        )

    def seg_peer(k):
        return ((chip + k) % 16) * 2 + core

    def arrive(slot):
        copy(vbuf.at[slot], vsend.at[0], partner, slot).wait_recv()
        s_copy(0, slot, slot).wait_recv()

    def compute(slot):
        block_hist(acc_ref, vbuf[slot], sbuf[slot].astype(jnp.int32), nodes)

    started = []

    def start(src, sem, peer, slot):
        c = copy(src, sem, peer, slot)
        c.start()
        started.append(c)

    for j, (da, db) in enumerate([(1, 0), (-1, 0), (0, 1), (0, -1)]):
        start(v_ref, vsend.at[j], dev(da, db), r)

    def send_seg(k, carry):
        s_copy(k, seg_peer(k), r).start()
        return carry

    lax.fori_loop(1, 16, send_seg, 0)

    sem = 4
    for da in [-1, 1, -2]:
        slot = dev(da, 0)
        arrive(slot)
        if da == -1:
            start(vbuf.at[slot], vsend.at[sem], dev(1, 0), slot)
            sem += 1
        start(vbuf.at[slot], vsend.at[sem], dev(0, 1), slot)
        start(vbuf.at[slot], vsend.at[sem + 1], dev(0, -1), slot)
        sem += 2
        compute(slot)

    def row_step(db, relay):
        def body(i, carry):
            slot = dev((i * 3) % 4, db)
            arrive(slot)
            if relay:
                copy(vbuf.at[slot], vsend.at[11 + i], dev(0, 1), slot).start()
            compute(slot)
            return carry

        return body

    for db, relay in [(-1, True), (1, False), (-2, False)]:
        lax.fori_loop(0, 4, row_step(db, relay), 0)

    span = hist_ref.shape[1]
    mine = pl.ds(pl.multiple_of(core * span, span), span)
    theirs = pl.ds(pl.multiple_of((1 - core) * span, span), span)
    swap = pltpu.make_async_remote_copy(
        src_ref=acc_ref.at[:, theirs], dst_ref=pbuf, send_sem=psend, recv_sem=precv,
        device_id=(partner, o), device_id_type=MESH_ID,
    )
    swap.start()
    swap.wait_recv()
    hist_ref[...] = acc_ref[:, mine] + pbuf[...]
    swap.wait_send()
    for c in started:
        c.wait_send()

    def relay_drain(i, carry):
        slot = dev((i * 3) % 4, -1)
        copy(vbuf.at[slot], vsend.at[11 + i], dev(0, 1), slot).wait_send()
        return carry

    lax.fori_loop(0, 4, relay_drain, 0)

    def drain(k, carry):
        s_copy(k, seg_peer(k), r).wait_send()
        return carry

    lax.fori_loop(1, 16, drain, 0)

    node_hist(hist_ref, parent_ref, small_ref, evict_ref, hist_ref, nodes)
    partial = gain_terms(hist_ref, nodes)
    exchange(partial, split_ref, best_ref, gbuf, mbuf, gsend, grecv, msend, mrecv, targets)


def pair_split(small_side, evicted, seg_c, v_loc, parent, nodes, targets):
    chips, width, half = seg_c.shape
    n_rows = 2 * chips
    n_outs = lax.axis_size("outs")
    vw, rows = v_loc.shape
    cols = width // 2 * BINS
    span = cols // 2
    out_rows = vw * nodes
    total = n_rows * rows
    vmem = pl.BlockSpec(memory_space=pltpu.VMEM)
    smem = pl.BlockSpec(memory_space=pltpu.SMEM)
    return pl.pallas_call(
        functools.partial(pair_split_kernel, nodes=nodes, targets=targets),
        out_shape=(
            jax.ShapeDtypeStruct((out_rows, span), jnp.float32),
            jax.ShapeDtypeStruct((nodes, span), jnp.float32),
            jax.ShapeDtypeStruct((nodes, 128), jnp.float32),
        ),
        in_specs=[smem, smem, vmem, vmem, vmem],
        out_specs=(vmem, vmem, vmem),
        scratch_shapes=[
            pltpu.VMEM((out_rows, cols), jnp.float32),
            pltpu.VMEM((n_rows, vw, rows), v_loc.dtype),
            pltpu.VMEM((n_rows, width, half), seg_c.dtype),
            pltpu.VMEM((out_rows, span), jnp.float32),
            pltpu.SemaphoreType.DMA((chips,)),
            pltpu.SemaphoreType.DMA((n_rows,)),
            pltpu.SemaphoreType.DMA((chips,)),
            pltpu.SemaphoreType.DMA((n_rows,)),
            pltpu.SemaphoreType.DMA(()),
            pltpu.SemaphoreType.DMA(()),
            pltpu.VMEM((n_outs, nodes, span), jnp.float32),
            pltpu.VMEM((n_rows, nodes, 128), jnp.float32),
            pltpu.SemaphoreType.DMA((n_outs,)),
            pltpu.SemaphoreType.DMA((n_outs,)),
            pltpu.SemaphoreType.DMA((n_rows,)),
            pltpu.SemaphoreType.DMA((n_rows,)),
        ],
        compiler_params=pltpu.CompilerParams(collective_id=2, has_side_effects=True),
        cost_estimate=pl.CostEstimate(
            flops=2 * out_rows * cols * total // 2,
            bytes_accessed=total * (vw * 2 + width) + out_rows * cols * 4,
            transcendentals=0,
        ),
    )(small_side, evicted, seg_c, v_loc, parent)


def local(codes, node_of_row, grad, hess, small_side, evicted, parent_hist):
    pairs = small_side.shape[0]
    nodes = 2 * pairs
    local_targets = grad.shape[1]
    targets = local_targets * lax.axis_size("outs")
    n_rows = lax.axis_size("rows")
    count, features = codes.shape
    feats = features // n_rows
    half = count // 2
    seg = (node_of_row[:, None] * BINS + codes).astype(jnp.int16)
    seg_p = jnp.transpose(seg.reshape(2, half, n_rows, feats), (2, 3, 0, 1)).reshape(n_rows, 2 * feats, half)
    v_loc = jnp.concatenate([grad.T, hess.T], axis=0)
    span = feats * BINS
    parent = parent_hist.reshape(2 * pairs * local_targets, span)
    if n_rows == 32:
        seg_t = (codes.T + node_of_row[None, :] * BINS).astype(jnp.int16)
        seg_c = seg_t.reshape(n_rows // 2, 2 * feats, 2, half).reshape(n_rows // 2, 4 * feats, half)
        hist, split_gain, best = pair_split(small_side, evicted, seg_c, v_loc, parent, nodes, targets)
    else:
        hist, split_gain, best = gather_hist(small_side, evicted, seg_p, v_loc, parent, nodes, targets)
    node_hist = hist.reshape(2, nodes, local_targets, span)
    return (node_hist, split_gain, best[:, 0])


def solution(mesh):
    return jax.shard_map(
        local,
        mesh=mesh,
        in_specs=(
            P("rows", None),
            P("rows"),
            P("rows", "outs"),
            P("rows", "outs"),
            P(),
            P(),
            P(None, None, "outs", "rows"),
        ),
        out_specs=(P(None, None, "outs", "rows"), P(None, "rows"), P()),
        check_vma=False,
    )
```

```python
import functools

import jax
import jax.numpy as jnp
import numpy as np
from jax import lax
from jax.experimental import pallas as pl
from jax.experimental.pallas import tpu as pltpu
from jax.sharding import PartitionSpec as P

BINS = 32


MESH_ID = pl.DeviceIdType.MESH


def row_stages(r, n_rows):
    chips = n_rows // 2
    nx = 4 if chips % 4 == 0 else chips
    ny = chips // nx
    chip = r // 2
    core = r % 2
    y = chip // nx
    x = chip % nx
    row = 2 * nx
    stages = [
        [y * row + (r - y * row + k) % row for k in range(1, row)],
        [(((y + k) % ny) * nx + x) * 2 + core for k in range(1, ny)],
    ]
    return [stage for stage in stages if stage]


def row_peers(r, n_rows):
    return [peer for stage in row_stages(r, n_rows) for peer in stage]


def exchange(part_fn, split_ref, best_ref, gbuf, mbuf, gsend, grecv, msend, mrecv, targets):
    n_rows = lax.axis_size("rows")
    n_outs = lax.axis_size("outs")
    r = lax.axis_index("rows")
    o = lax.axis_index("outs")
    nodes = gbuf.shape[1]
    halves = [(0, nodes // 2), (nodes // 2, nodes)]

    def part_copy(h, k, dst, slot):
        lo, hi = halves[h]
        return pltpu.make_async_remote_copy(
            src_ref=gbuf.at[o, pl.ds(lo, hi - lo)],
            dst_ref=gbuf.at[slot, pl.ds(lo, hi - lo)],
            send_sem=gsend.at[h, k],
            recv_sem=grecv.at[h, slot],
            device_id=(r, dst),
            device_id_type=MESH_ID,
        )

    sends = []
    for h, (lo, hi) in enumerate(halves):
        gbuf[o, lo:hi] = part_fn(lo, hi)
        for k in range(1, n_outs):
            copy = part_copy(h, k, (o + k) % n_outs, o)
            copy.start()
            sends.append(copy)
    for h in range(2):
        for k in range(1, n_outs):
            src = (o + n_outs - k) % n_outs
            part_copy(h, k, src, src).wait_recv()
    for copy in sends:
        copy.wait_send()
    acc = gbuf[0]
    for j in range(1, n_outs):
        acc = acc + gbuf[j]
    split = acc / targets
    split_ref[...] = split
    width = mbuf.shape[2]
    best = jnp.broadcast_to(jnp.max(split, axis=1, keepdims=True), (split.shape[0], width))
    base = 0
    for peers in row_stages(r, n_rows):
        mbuf[base] = best
        sends = []
        for j, peer in enumerate(peers):
            copy = pltpu.make_async_remote_copy(
                src_ref=mbuf.at[base],
                dst_ref=mbuf.at[base + 1 + j],
                send_sem=msend.at[base + 1 + j],
                recv_sem=mrecv.at[base + 1 + j],
                device_id=(peer, o),
                device_id_type=MESH_ID,
            )
            copy.start()
            sends.append(copy)
        for copy in sends:
            copy.wait_recv()
        for copy in sends:
            copy.wait_send()
        for j in range(len(peers)):
            best = jnp.maximum(best, mbuf[base + 1 + j])
        base += len(peers) + 1
    best_ref[...] = best


def block_hist(acc_ref, v, s, nodes):
    tl = v.shape[0] // 2
    half = s.shape[1]
    feats = s.shape[0] // 2
    one = jnp.ones((), jnp.bfloat16)
    zero = jnp.zeros((), jnp.bfloat16)
    bins = lax.broadcasted_iota(jnp.int32, (BINS, half), 0)
    for h in range(2):
        vh = v[:, h * half : (h + 1) * half]
        node = s[h : h + 1] >> 5
        onehot = jnp.concatenate(
            [jnp.where((s[2 * f + h : 2 * f + h + 1] & (BINS - 1)) == bins, one, zero) for f in range(feats)],
            axis=0,
        )
        blocks = []
        for c in range(2):
            vc = vh[c * tl : (c + 1) * tl]
            for n in range(nodes):
                blocks.append(jnp.where(node == n, vc, zero))
        vals = jnp.concatenate(blocks, axis=0)
        acc_ref[...] += lax.dot_general(
            vals, onehot, (((1,), (1,)), ((), ())), preferred_element_type=jnp.float32
        )


def relay_gather(acc_ref, seg_ref, v_ref, vbuf, sbuf, vsend, fsend, vrecv, s_copy, send_seg, nodes):
    n_rows = lax.axis_size("rows")
    r = lax.axis_index("rows")
    o = lax.axis_index("outs")
    core = r % 2
    chip = r // 2
    y = chip // 4
    x = chip % 4
    a = x + core * (y - x)
    b = y + core * (x - y)
    partner = chip * 2 + 1 - core

    def dev(da, db):
        ap = (a + da + 4) % 4
        bp = (b + db + 4) % 4
        return ((1 - core) * (bp * 4 + ap) + core * (ap * 4 + bp)) * 2 + core

    def copy(src, sem, peer, slot):
        return pltpu.make_async_remote_copy(
            src_ref=src, dst_ref=vbuf.at[slot], send_sem=sem, recv_sem=vrecv.at[slot],
            device_id=(peer, o), device_id_type=MESH_ID,
        )

    def arrive(slot):
        copy(vbuf.at[slot], vsend.at[0], partner, slot).wait_recv()
        s_copy(0, slot, slot).wait_recv()

    def compute(slot):
        block_hist(acc_ref, vbuf[slot], sbuf[slot].astype(jnp.int32), nodes)

    started = []

    def start(src, sem, peer, slot):
        c = copy(src, sem, peer, slot)
        c.start()
        started.append(c)

    start(v_ref, fsend.at[0], partner, r)
    for j, (da, db) in enumerate([(1, 0), (-1, 0), (0, 1), (0, -1)]):
        start(v_ref, vsend.at[j], dev(da, db), r)
    lax.fori_loop(1, n_rows, send_seg, 0)

    sem = 4
    for j, da in enumerate([-1, 1, -2]):
        slot = dev(da, 0)
        arrive(slot)
        if da == -1:
            start(vbuf.at[slot], vsend.at[sem], dev(1, 0), slot)
            sem += 1
        start(vbuf.at[slot], vsend.at[sem], dev(0, 1), slot)
        start(vbuf.at[slot], vsend.at[sem + 1], dev(0, -1), slot)
        sem += 2
        start(vbuf.at[slot], fsend.at[1 + j], partner, slot)
        compute(slot)

    def row_step(db, relay, first):
        def body(i, carry):
            slot = dev((i * 3) % 4, db)
            arrive(slot)
            if relay:
                copy(vbuf.at[slot], vsend.at[11 + i], dev(0, -db), slot).start()
            copy(vbuf.at[slot], fsend.at[first + i], partner, slot).start()
            compute(slot)
            return carry

        return body

    def row_drain(db, relay, first):
        def body(i, carry):
            slot = dev((i * 3) % 4, db)
            if relay:
                copy(vbuf.at[slot], vsend.at[11 + i], dev(0, -db), slot).wait_send()
            copy(vbuf.at[slot], fsend.at[first + i], partner, slot).wait_send()
            return carry

        return body

    rows_plan = [(-1, True, 4, 0, 2), (1, False, 8, 0, 2), (-1, False, 4, 2, 4), (1, True, 8, 2, 4), (2, False, 12, 0, 4)]
    for db, relay, first, lo, hi in rows_plan:
        lax.fori_loop(lo, hi, row_step(db, relay, first), 0)

    def take_partner(k, carry):
        slot = ((chip + 16 - k) % 16) * 2 + 1 - core
        arrive(slot)
        compute(slot)
        return carry

    lax.fori_loop(0, 16, take_partner, 0)
    for c in started:
        c.wait_send()
    for db, relay, first, lo, hi in rows_plan:
        lax.fori_loop(lo, hi, row_drain(db, relay, first), 0)


def gather_hist_kernel(
    small_ref, evict_ref, seg_ref, v_ref, parent_ref, hist_ref, split_ref, best_ref,
    acc_ref, vbuf, sbuf, vsend, fsend, vrecv, ssend, srecv, gbuf, mbuf, gsend, grecv, msend, mrecv,
    *, nodes, targets,
):
    n_rows = lax.axis_size("rows")
    chips = n_rows // 2
    r = lax.axis_index("rows")
    o = lax.axis_index("outs")
    core = r % 2
    chip = r // 2
    partner = chip * 2 + 1 - core
    barrier = pltpu.get_barrier_semaphore()

    def greet(k, carry):
        pl.semaphore_signal(barrier, 1, device_id=((r + k) % n_rows, o), device_id_type=MESH_ID)
        return carry

    lax.fori_loop(1, n_rows, greet, 0)
    n_outs = lax.axis_size("outs")
    for k in range(1, n_outs):
        pl.semaphore_signal(barrier, 1, device_id=(r, (o + k) % n_outs), device_id_type=MESH_ID)
    acc_ref[...] = jnp.zeros_like(acc_ref)
    block_hist(acc_ref, v_ref[...], seg_ref[r].astype(jnp.int32), nodes)
    pl.semaphore_wait(barrier, n_rows - 1 + n_outs - 1)

    def s_copy(k, peer, slot):
        return pltpu.make_async_remote_copy(
            src_ref=seg_ref.at[peer], dst_ref=sbuf.at[slot], send_sem=ssend.at[k], recv_sem=srecv.at[slot],
            device_id=(peer, o), device_id_type=MESH_ID,
        )

    def v_copy(k, peer, slot):
        return pltpu.make_async_remote_copy(
            src_ref=v_ref, dst_ref=vbuf.at[slot], send_sem=vsend.at[k], recv_sem=vrecv.at[slot],
            device_id=(peer, o), device_id_type=MESH_ID,
        )

    def f_copy(k, slot):
        return pltpu.make_async_remote_copy(
            src_ref=vbuf.at[slot], dst_ref=vbuf.at[slot], send_sem=fsend.at[k], recv_sem=vrecv.at[slot],
            device_id=(partner, o), device_id_type=MESH_ID,
        )

    def send_seg(k, carry):
        s_copy(k, (r + k) % n_rows, r).start()
        return carry

    def drain(k, carry):
        s_copy(k, (r + k) % n_rows, r).wait_send()
        return carry

    if chips == 16:
        relay_gather(acc_ref, seg_ref, v_ref, vbuf, sbuf, vsend, fsend, vrecv, s_copy, send_seg, nodes)
        lax.fori_loop(1, n_rows, drain, 0)
    else:
        own = pltpu.make_async_remote_copy(
            src_ref=v_ref, dst_ref=vbuf.at[r], send_sem=fsend.at[0], recv_sem=vrecv.at[r],
            device_id=(partner, o), device_id_type=MESH_ID,
        )
        own.start()

        def send(k, carry):
            v_copy(k, ((chip + k) % chips) * 2 + core, r).start()
            return carry

        lax.fori_loop(1, chips, send, 0)

        lax.fori_loop(1, n_rows, send_seg, 0)

        def take_direct(k, carry):
            src = ((chip + chips - k) % chips) * 2 + core
            v_copy(k, src, src).wait_recv()
            f_copy(k, src).start()
            s_copy(k, src, src).wait_recv()
            block_hist(acc_ref, vbuf[src], sbuf[src].astype(jnp.int32), nodes)
            return carry

        lax.fori_loop(1, chips, take_direct, 0)

        def take_forwarded(k, carry):
            src = ((chip + chips - k) % chips) * 2 + 1 - core
            f_copy(k, src).wait_recv()
            s_copy(k, src, src).wait_recv()
            block_hist(acc_ref, vbuf[src], sbuf[src].astype(jnp.int32), nodes)
            return carry

        lax.fori_loop(0, chips, take_forwarded, 0)

        lax.fori_loop(1, n_rows, drain, 0)

        def drain_v(k, carry):
            v_copy(k, ((chip + k) % chips) * 2 + core, r).wait_send()
            return carry

        lax.fori_loop(1, chips, drain_v, 0)
        own.wait_send()

        def drain_f(k, carry):
            f_copy(k, ((chip + chips - k) % chips) * 2 + core).wait_send()
            return carry

        lax.fori_loop(1, chips, drain_f, 0)


    node_hist(acc_ref, parent_ref, small_ref, evict_ref, hist_ref, nodes)
    exchange(functools.partial(gain_terms, hist_ref, nodes), split_ref, best_ref, gbuf, mbuf, gsend, grecv, msend, mrecv, targets)


def node_hist(acc_ref, parent_ref, small_ref, evict_ref, hist_ref, nodes):
    pairs = nodes // 2
    tl = acc_ref.shape[0] // (2 * nodes)
    for c in range(2):
        for p in range(pairs):
            lo = c * nodes * tl + 2 * p * tl
            a = acc_ref[lo : lo + tl]
            b = acc_ref[lo + tl : lo + 2 * tl]
            base = (c * pairs + p) * tl
            parent = parent_ref[base : base + tl]
            small = small_ref[p] == 0
            gone = evict_ref[p] == 1
            child = jnp.where(small, a, b)
            rebuilt = jnp.where(small, b, a)
            sibling = jnp.where(gone, rebuilt, parent - child)
            hist_ref[lo : lo + tl] = jnp.where(small, child, sibling)
            hist_ref[lo + tl : lo + 2 * tl] = jnp.where(small, sibling, child)


def group_scan(x, reverse):
    span = x.shape[1]
    lane = lax.broadcasted_iota(jnp.int32, x.shape, 1) % BINS
    shift = 1
    while shift < BINS:
        if reverse:
            moved = pltpu.roll(x, span - shift, 1)
            x = x + jnp.where(lane + shift < BINS, moved, 0.0)
        else:
            moved = pltpu.roll(x, shift, 1)
            x = x + jnp.where(lane >= shift, moved, 0.0)
        shift *= 2
    return x


def gain_terms(hist_ref, nodes, lo, hi):
    rows, span = hist_ref.shape
    half = rows // 2
    tl = half // nodes
    count = (hi - lo) * tl
    lane = lax.broadcasted_iota(jnp.int32, (count, span), 1) % BINS
    left_g = group_scan(hist_ref[lo * tl : hi * tl], False)
    left_h = group_scan(hist_ref[half + lo * tl : half + hi * tl], False)
    total_g = group_scan(jnp.where(lane == BINS - 1, left_g, 0.0), True)
    total_h = group_scan(jnp.where(lane == BINS - 1, left_h, 0.0), True)

    def score(a, s):
        return a * a / (jnp.maximum(s, 0.0) + 1.0)

    gain = (
        score(left_g, left_h) + score(total_g - left_g, total_h - left_h) - score(total_g, total_h)
    )
    return jnp.sum(gain.reshape(hi - lo, tl, span), axis=1)


def gather_hist(small_side, evicted, seg_p, v_loc, parent, nodes, targets):
    n_rows, width, half = seg_p.shape
    n_outs = lax.axis_size("outs")
    vw, rows = v_loc.shape
    feats = width // 2
    out_rows = vw * nodes
    cols = feats * BINS
    total = n_rows * rows
    vmem = pl.BlockSpec(memory_space=pltpu.VMEM)
    smem = pl.BlockSpec(memory_space=pltpu.SMEM)
    return pl.pallas_call(
        functools.partial(gather_hist_kernel, nodes=nodes, targets=targets),
        out_shape=(
            jax.ShapeDtypeStruct((out_rows, cols), jnp.float32),
            jax.ShapeDtypeStruct((nodes, cols), jnp.float32),
            jax.ShapeDtypeStruct((nodes, 128), jnp.float32),
        ),
        in_specs=[smem, smem, vmem, vmem, vmem],
        out_specs=(vmem, vmem, vmem),
        scratch_shapes=[
            pltpu.VMEM((out_rows, cols), jnp.float32),
            pltpu.VMEM((n_rows, vw, rows), v_loc.dtype),
            pltpu.VMEM((n_rows, width, half), seg_p.dtype),
            pltpu.SemaphoreType.DMA((n_rows // 2,)),
            pltpu.SemaphoreType.DMA((n_rows // 2,)),
            pltpu.SemaphoreType.DMA((n_rows,)),
            pltpu.SemaphoreType.DMA((n_rows,)),
            pltpu.SemaphoreType.DMA((n_rows,)),
            pltpu.VMEM((n_outs, nodes, cols), jnp.float32),
            pltpu.VMEM((n_rows, nodes, 128), jnp.float32),
            pltpu.SemaphoreType.DMA((2, n_outs)),
            pltpu.SemaphoreType.DMA((2, n_outs)),
            pltpu.SemaphoreType.DMA((n_rows,)),
            pltpu.SemaphoreType.DMA((n_rows,)),
        ],
        compiler_params=pltpu.CompilerParams(collective_id=1, has_side_effects=True),
        cost_estimate=pl.CostEstimate(
            flops=2 * out_rows * cols * total,
            bytes_accessed=total * (vw * 2 + feats * 2) + out_rows * cols * 4,
            transcendentals=0,
        ),
    )(small_side, evicted, seg_p, v_loc, parent)


def pair_split_kernel(
    small_ref, evict_ref, seg_ref, v_ref, parent_ref, hist_ref, split_ref, best_ref,
    acc_ref, vbuf, sbuf, pbuf, vsend, vrecv, ssend, srecv, psend, precv, gbuf, mbuf, gsend, grecv, msend, mrecv,
    *, nodes, targets,
):
    n_rows = lax.axis_size("rows")
    n_outs = lax.axis_size("outs")
    r = lax.axis_index("rows")
    o = lax.axis_index("outs")
    core = r % 2
    chip = r // 2
    y = chip // 4
    x = chip % 4
    a = x + core * (y - x)
    b = y + core * (x - y)
    partner = chip * 2 + 1 - core
    barrier = pltpu.get_barrier_semaphore()

    def greet(k, carry):
        pl.semaphore_signal(barrier, 1, device_id=((r + k) % n_rows, o), device_id_type=MESH_ID)
        return carry

    lax.fori_loop(1, n_rows, greet, 0)
    for k in range(1, n_outs):
        pl.semaphore_signal(barrier, 1, device_id=(r, (o + k) % n_outs), device_id_type=MESH_ID)
    acc_ref[...] = jnp.zeros_like(acc_ref)
    block_hist(acc_ref, v_ref[...], seg_ref[chip].astype(jnp.int32), nodes)
    pl.semaphore_wait(barrier, n_rows - 1 + n_outs - 1)

    def dev(da, db):
        ap = (a + da + 4) % 4
        bp = (b + db + 4) % 4
        return ((1 - core) * (bp * 4 + ap) + core * (ap * 4 + bp)) * 2 + core

    def copy(src, sem, peer, slot):
        return pltpu.make_async_remote_copy(
            src_ref=src, dst_ref=vbuf.at[slot], send_sem=sem, recv_sem=vrecv.at[slot],
            device_id=(peer, o), device_id_type=MESH_ID,
        )

    def s_copy(k, peer, slot):
        return pltpu.make_async_remote_copy(
            src_ref=seg_ref.at[peer // 2], dst_ref=sbuf.at[slot], send_sem=ssend.at[k], recv_sem=srecv.at[slot],
            device_id=(peer, o), device_id_type=MESH_ID,
        )

    def seg_peer(k):
        return ((chip + k) % 16) * 2 + core

    def arrive(slot):
        copy(vbuf.at[slot], vsend.at[0], partner, slot).wait_recv()
        s_copy(0, slot, slot).wait_recv()

    def compute(slot):
        block_hist(acc_ref, vbuf[slot], sbuf[slot].astype(jnp.int32), nodes)

    started = []

    def start(src, sem, peer, slot):
        c = copy(src, sem, peer, slot)
        c.start()
        started.append(c)

    for j, (da, db) in enumerate([(1, 0), (-1, 0), (0, 1), (0, -1)]):
        start(v_ref, vsend.at[j], dev(da, db), r)

    def send_seg(k, carry):
        s_copy(k, seg_peer(k), r).start()
        return carry

    lax.fori_loop(1, 16, send_seg, 0)

    sem = 4
    for da in [-1, 1, -2]:
        slot = dev(da, 0)
        arrive(slot)
        if da == -1:
            start(vbuf.at[slot], vsend.at[sem], dev(1, 0), slot)
            sem += 1
        start(vbuf.at[slot], vsend.at[sem], dev(0, 1), slot)
        start(vbuf.at[slot], vsend.at[sem + 1], dev(0, -1), slot)
        sem += 2
        compute(slot)

    def row_step(db, relay):
        def body(i, carry):
            slot = dev((i * 3) % 4, db)
            arrive(slot)
            if relay:
                copy(vbuf.at[slot], vsend.at[11 + i], dev(0, 1), slot).start()
            compute(slot)
            return carry

        return body

    for db, relay in [(-1, True), (1, False), (-2, False)]:
        lax.fori_loop(0, 4, row_step(db, relay), 0)

    span = hist_ref.shape[1]
    mine = pl.ds(pl.multiple_of(core * span, span), span)
    theirs = pl.ds(pl.multiple_of((1 - core) * span, span), span)
    swap = pltpu.make_async_remote_copy(
        src_ref=acc_ref.at[:, theirs], dst_ref=pbuf, send_sem=psend, recv_sem=precv,
        device_id=(partner, o), device_id_type=MESH_ID,
    )
    swap.start()
    swap.wait_recv()
    hist_ref[...] = acc_ref[:, mine] + pbuf[...]
    swap.wait_send()
    for c in started:
        c.wait_send()

    def relay_drain(i, carry):
        slot = dev((i * 3) % 4, -1)
        copy(vbuf.at[slot], vsend.at[11 + i], dev(0, 1), slot).wait_send()
        return carry

    lax.fori_loop(0, 4, relay_drain, 0)

    def drain(k, carry):
        s_copy(k, seg_peer(k), r).wait_send()
        return carry

    lax.fori_loop(1, 16, drain, 0)

    node_hist(hist_ref, parent_ref, small_ref, evict_ref, hist_ref, nodes)
    exchange(functools.partial(gain_terms, hist_ref, nodes), split_ref, best_ref, gbuf, mbuf, gsend, grecv, msend, mrecv, targets)


def pair_split(small_side, evicted, seg_c, v_loc, parent, nodes, targets):
    chips, width, half = seg_c.shape
    n_rows = 2 * chips
    n_outs = lax.axis_size("outs")
    vw, rows = v_loc.shape
    cols = width // 2 * BINS
    span = cols // 2
    out_rows = vw * nodes
    total = n_rows * rows
    vmem = pl.BlockSpec(memory_space=pltpu.VMEM)
    smem = pl.BlockSpec(memory_space=pltpu.SMEM)
    return pl.pallas_call(
        functools.partial(pair_split_kernel, nodes=nodes, targets=targets),
        out_shape=(
            jax.ShapeDtypeStruct((out_rows, span), jnp.float32),
            jax.ShapeDtypeStruct((nodes, span), jnp.float32),
            jax.ShapeDtypeStruct((nodes, 128), jnp.float32),
        ),
        in_specs=[smem, smem, vmem, vmem, vmem],
        out_specs=(vmem, vmem, vmem),
        scratch_shapes=[
            pltpu.VMEM((out_rows, cols), jnp.float32),
            pltpu.VMEM((n_rows, vw, rows), v_loc.dtype),
            pltpu.VMEM((n_rows, width, half), seg_c.dtype),
            pltpu.VMEM((out_rows, span), jnp.float32),
            pltpu.SemaphoreType.DMA((chips,)),
            pltpu.SemaphoreType.DMA((n_rows,)),
            pltpu.SemaphoreType.DMA((chips,)),
            pltpu.SemaphoreType.DMA((n_rows,)),
            pltpu.SemaphoreType.DMA(()),
            pltpu.SemaphoreType.DMA(()),
            pltpu.VMEM((n_outs, nodes, span), jnp.float32),
            pltpu.VMEM((n_rows, nodes, 128), jnp.float32),
            pltpu.SemaphoreType.DMA((2, n_outs)),
            pltpu.SemaphoreType.DMA((2, n_outs)),
            pltpu.SemaphoreType.DMA((n_rows,)),
            pltpu.SemaphoreType.DMA((n_rows,)),
        ],
        compiler_params=pltpu.CompilerParams(collective_id=2, has_side_effects=True),
        cost_estimate=pl.CostEstimate(
            flops=2 * out_rows * cols * total // 2,
            bytes_accessed=total * (vw * 2 + width) + out_rows * cols * 4,
            transcendentals=0,
        ),
    )(small_side, evicted, seg_c, v_loc, parent)


def local(codes, node_of_row, grad, hess, small_side, evicted, parent_hist):
    pairs = small_side.shape[0]
    nodes = 2 * pairs
    local_targets = grad.shape[1]
    targets = local_targets * lax.axis_size("outs")
    n_rows = lax.axis_size("rows")
    count, features = codes.shape
    feats = features // n_rows
    half = count // 2
    seg = (node_of_row[:, None] * BINS + codes).astype(jnp.int16)
    seg_p = jnp.transpose(seg.reshape(2, half, n_rows, feats), (2, 3, 0, 1)).reshape(n_rows, 2 * feats, half)
    v_loc = jnp.concatenate([grad.T, hess.T], axis=0)
    span = feats * BINS
    parent = parent_hist.reshape(2 * pairs * local_targets, span)
    if n_rows == 32:
        seg_t = (codes.T + node_of_row[None, :] * BINS).astype(jnp.int16)
        seg_c = seg_t.reshape(n_rows // 2, 2 * feats, 2, half).reshape(n_rows // 2, 4 * feats, half)
        hist, split_gain, best = pair_split(small_side, evicted, seg_c, v_loc, parent, nodes, targets)
    else:
        hist, split_gain, best = gather_hist(small_side, evicted, seg_p, v_loc, parent, nodes, targets)
    node_hist = hist.reshape(2, nodes, local_targets, span)
    return (node_hist, split_gain, best[:, 0])


def solution(mesh):
    return jax.shard_map(
        local,
        mesh=mesh,
        in_specs=(
            P("rows", None),
            P("rows"),
            P("rows", "outs"),
            P("rows", "outs"),
            P(),
            P(),
            P(None, None, "outs", "rows"),
        ),
        out_specs=(P(None, None, "outs", "rows"), P(None, "rows"), P()),
        check_vma=False,
    )
```

```python
import functools

import jax
import jax.numpy as jnp
import numpy as np
from jax import lax
from jax.experimental import pallas as pl
from jax.experimental.pallas import tpu as pltpu
from jax.sharding import PartitionSpec as P

BINS = 32


MESH_ID = pl.DeviceIdType.MESH


def row_stages(r, n_rows):
    chips = n_rows // 2
    nx = 4 if chips % 4 == 0 else chips
    ny = chips // nx
    chip = r // 2
    core = r % 2
    y = chip // nx
    x = chip % nx
    row = 2 * nx
    stages = [
        [y * row + (r - y * row + k) % row for k in range(1, row)],
        [(((y + k) % ny) * nx + x) * 2 + core for k in range(1, ny)],
    ]
    return [stage for stage in stages if stage]


def row_peers(r, n_rows):
    return [peer for stage in row_stages(r, n_rows) for peer in stage]


def exchange(part_fn, split_ref, best_ref, gbuf, mbuf, gsend, grecv, msend, mrecv, targets):
    n_rows = lax.axis_size("rows")
    n_outs = lax.axis_size("outs")
    r = lax.axis_index("rows")
    o = lax.axis_index("outs")
    nodes = gbuf.shape[1]
    halves = [(0, nodes // 2), (nodes // 2, nodes)]

    def part_copy(h, k, dst, slot):
        lo, hi = halves[h]
        return pltpu.make_async_remote_copy(
            src_ref=gbuf.at[o, pl.ds(lo, hi - lo)],
            dst_ref=gbuf.at[slot, pl.ds(lo, hi - lo)],
            send_sem=gsend.at[h, k],
            recv_sem=grecv.at[h, slot],
            device_id=(r, dst),
            device_id_type=MESH_ID,
        )

    sends = []
    for h, (lo, hi) in enumerate(halves):
        gbuf[o, lo:hi] = part_fn(lo, hi)
        for k in range(1, n_outs):
            copy = part_copy(h, k, (o + k) % n_outs, o)
            copy.start()
            sends.append(copy)
    for h in range(2):
        for k in range(1, n_outs):
            src = (o + n_outs - k) % n_outs
            part_copy(h, k, src, src).wait_recv()
    for copy in sends:
        copy.wait_send()
    acc = gbuf[0]
    for j in range(1, n_outs):
        acc = acc + gbuf[j]
    split = acc / targets
    split_ref[...] = split
    width = mbuf.shape[2]
    best = jnp.broadcast_to(jnp.max(split, axis=1, keepdims=True), (split.shape[0], width))
    base = 0
    for peers in row_stages(r, n_rows):
        mbuf[base] = best
        sends = []
        for j, peer in enumerate(peers):
            copy = pltpu.make_async_remote_copy(
                src_ref=mbuf.at[base],
                dst_ref=mbuf.at[base + 1 + j],
                send_sem=msend.at[base + 1 + j],
                recv_sem=mrecv.at[base + 1 + j],
                device_id=(peer, o),
                device_id_type=MESH_ID,
            )
            copy.start()
            sends.append(copy)
        for copy in sends:
            copy.wait_recv()
        for copy in sends:
            copy.wait_send()
        for j in range(len(peers)):
            best = jnp.maximum(best, mbuf[base + 1 + j])
        base += len(peers) + 1
    best_ref[...] = best


def block_hist(acc_ref, v, s, nodes):
    tl = v.shape[0] // 2
    half = s.shape[1]
    feats = s.shape[0] // 2
    one = jnp.ones((), jnp.bfloat16)
    zero = jnp.zeros((), jnp.bfloat16)
    bins = lax.broadcasted_iota(jnp.int32, (BINS, half), 0)
    for h in range(2):
        vh = v[:, h * half : (h + 1) * half]
        node = s[h : h + 1] >> 5
        onehot = jnp.concatenate(
            [jnp.where((s[2 * f + h : 2 * f + h + 1] & (BINS - 1)) == bins, one, zero) for f in range(feats)],
            axis=0,
        )
        blocks = []
        for c in range(2):
            vc = vh[c * tl : (c + 1) * tl]
            for n in range(nodes):
                blocks.append(jnp.where(node == n, vc, zero))
        vals = jnp.concatenate(blocks, axis=0)
        acc_ref[...] += lax.dot_general(
            vals, onehot, (((1,), (1,)), ((), ())), preferred_element_type=jnp.float32
        )


def relay_gather(acc_ref, seg_ref, v_ref, vbuf, sbuf, vsend, fsend, vrecv, s_copy, send_seg, nodes):
    n_rows = lax.axis_size("rows")
    r = lax.axis_index("rows")
    o = lax.axis_index("outs")
    core = r % 2
    chip = r // 2
    y = chip // 4
    x = chip % 4
    a = x + core * (y - x)
    b = y + core * (x - y)
    partner = chip * 2 + 1 - core

    def dev(da, db):
        ap = (a + da + 4) % 4
        bp = (b + db + 4) % 4
        return ((1 - core) * (bp * 4 + ap) + core * (ap * 4 + bp)) * 2 + core

    def copy(src, sem, peer, slot):
        return pltpu.make_async_remote_copy(
            src_ref=src, dst_ref=vbuf.at[slot], send_sem=sem, recv_sem=vrecv.at[slot],
            device_id=(peer, o), device_id_type=MESH_ID,
        )

    def arrive(slot):
        copy(vbuf.at[slot], vsend.at[0], partner, slot).wait_recv()
        s_copy(0, slot, slot).wait_recv()

    def compute(slot):
        block_hist(acc_ref, vbuf[slot], sbuf[slot].astype(jnp.int32), nodes)

    started = []

    def start(src, sem, peer, slot):
        c = copy(src, sem, peer, slot)
        c.start()
        started.append(c)

    start(v_ref, fsend.at[0], partner, r)
    for j, (da, db) in enumerate([(1, 0), (-1, 0), (0, 1), (0, -1)]):
        start(v_ref, vsend.at[j], dev(da, db), r)
    lax.fori_loop(1, n_rows, send_seg, 0)

    sem = 4
    for j, da in enumerate([-1, 1, -2]):
        slot = dev(da, 0)
        arrive(slot)
        if da == -1:
            start(vbuf.at[slot], vsend.at[sem], dev(1, 0), slot)
            sem += 1
        start(vbuf.at[slot], vsend.at[sem], dev(0, 1), slot)
        start(vbuf.at[slot], vsend.at[sem + 1], dev(0, -1), slot)
        sem += 2
        start(vbuf.at[slot], fsend.at[1 + j], partner, slot)
        compute(slot)

    def row_step(db, relay, first):
        def body(i, carry):
            slot = dev((i * 3) % 4, db)
            arrive(slot)
            if relay:
                copy(vbuf.at[slot], vsend.at[11 + i], dev(0, -db), slot).start()
            copy(vbuf.at[slot], fsend.at[first + i], partner, slot).start()
            compute(slot)
            return carry

        return body

    def row_drain(db, relay, first):
        def body(i, carry):
            slot = dev((i * 3) % 4, db)
            if relay:
                copy(vbuf.at[slot], vsend.at[11 + i], dev(0, -db), slot).wait_send()
            copy(vbuf.at[slot], fsend.at[first + i], partner, slot).wait_send()
            return carry

        return body

    rows_plan = [(-1, True, 4, 0, 2), (1, False, 8, 0, 2), (-1, False, 4, 2, 4), (1, True, 8, 2, 4), (2, False, 12, 0, 4)]
    for db, relay, first, lo, hi in rows_plan:
        lax.fori_loop(lo, hi, row_step(db, relay, first), 0)

    def take_partner(k, carry):
        slot = ((chip + 16 - k) % 16) * 2 + 1 - core
        arrive(slot)
        compute(slot)
        return carry

    lax.fori_loop(0, 16, take_partner, 0)
    for c in started:
        c.wait_send()
    for db, relay, first, lo, hi in rows_plan:
        lax.fori_loop(lo, hi, row_drain(db, relay, first), 0)


def gather_hist_kernel(
    small_ref, evict_ref, seg_ref, v_ref, parent_ref, hist_ref, split_ref, best_ref,
    acc_ref, vbuf, sbuf, vsend, fsend, vrecv, ssend, srecv, gbuf, mbuf, gsend, grecv, msend, mrecv,
    *, nodes, targets,
):
    n_rows = lax.axis_size("rows")
    chips = n_rows // 2
    r = lax.axis_index("rows")
    o = lax.axis_index("outs")
    core = r % 2
    chip = r // 2
    partner = chip * 2 + 1 - core
    barrier = pltpu.get_barrier_semaphore()

    def greet(k, carry):
        pl.semaphore_signal(barrier, 1, device_id=((r + k) % n_rows, o), device_id_type=MESH_ID)
        return carry

    lax.fori_loop(1, n_rows, greet, 0)
    n_outs = lax.axis_size("outs")
    for k in range(1, n_outs):
        pl.semaphore_signal(barrier, 1, device_id=(r, (o + k) % n_outs), device_id_type=MESH_ID)
    acc_ref[...] = jnp.zeros_like(acc_ref)
    block_hist(acc_ref, v_ref[...], seg_ref[r].astype(jnp.int32), nodes)
    pl.semaphore_wait(barrier, n_rows - 1 + n_outs - 1)

    def s_copy(k, peer, slot):
        return pltpu.make_async_remote_copy(
            src_ref=seg_ref.at[peer], dst_ref=sbuf.at[slot], send_sem=ssend.at[k], recv_sem=srecv.at[slot],
            device_id=(peer, o), device_id_type=MESH_ID,
        )

    def v_copy(k, peer, slot):
        return pltpu.make_async_remote_copy(
            src_ref=v_ref, dst_ref=vbuf.at[slot], send_sem=vsend.at[k], recv_sem=vrecv.at[slot],
            device_id=(peer, o), device_id_type=MESH_ID,
        )

    def f_copy(k, slot):
        return pltpu.make_async_remote_copy(
            src_ref=vbuf.at[slot], dst_ref=vbuf.at[slot], send_sem=fsend.at[k], recv_sem=vrecv.at[slot],
            device_id=(partner, o), device_id_type=MESH_ID,
        )

    def send_seg(k, carry):
        s_copy(k, (r + k) % n_rows, r).start()
        return carry

    def drain(k, carry):
        s_copy(k, (r + k) % n_rows, r).wait_send()
        return carry

    if chips == 16:
        relay_gather(acc_ref, seg_ref, v_ref, vbuf, sbuf, vsend, fsend, vrecv, s_copy, send_seg, nodes)
        lax.fori_loop(1, n_rows, drain, 0)
    else:
        own = pltpu.make_async_remote_copy(
            src_ref=v_ref, dst_ref=vbuf.at[r], send_sem=fsend.at[0], recv_sem=vrecv.at[r],
            device_id=(partner, o), device_id_type=MESH_ID,
        )
        own.start()

        def send(k, carry):
            v_copy(k, ((chip + k) % chips) * 2 + core, r).start()
            return carry

        lax.fori_loop(1, chips, send, 0)

        lax.fori_loop(1, n_rows, send_seg, 0)

        def take_direct(k, carry):
            src = ((chip + chips - k) % chips) * 2 + core
            v_copy(k, src, src).wait_recv()
            f_copy(k, src).start()
            s_copy(k, src, src).wait_recv()
            block_hist(acc_ref, vbuf[src], sbuf[src].astype(jnp.int32), nodes)
            return carry

        lax.fori_loop(1, chips, take_direct, 0)

        def take_forwarded(k, carry):
            src = ((chip + chips - k) % chips) * 2 + 1 - core
            f_copy(k, src).wait_recv()
            s_copy(k, src, src).wait_recv()
            block_hist(acc_ref, vbuf[src], sbuf[src].astype(jnp.int32), nodes)
            return carry

        lax.fori_loop(0, chips, take_forwarded, 0)

        lax.fori_loop(1, n_rows, drain, 0)

        def drain_v(k, carry):
            v_copy(k, ((chip + k) % chips) * 2 + core, r).wait_send()
            return carry

        lax.fori_loop(1, chips, drain_v, 0)
        own.wait_send()

        def drain_f(k, carry):
            f_copy(k, ((chip + chips - k) % chips) * 2 + core).wait_send()
            return carry

        lax.fori_loop(1, chips, drain_f, 0)


    node_hist(acc_ref, parent_ref, small_ref, evict_ref, hist_ref, nodes)
    exchange(functools.partial(gain_terms, hist_ref, nodes), split_ref, best_ref, gbuf, mbuf, gsend, grecv, msend, mrecv, targets)


def node_hist(acc_ref, parent_ref, small_ref, evict_ref, hist_ref, nodes):
    pairs = nodes // 2
    tl = acc_ref.shape[0] // (2 * nodes)
    for c in range(2):
        for p in range(pairs):
            lo = c * nodes * tl + 2 * p * tl
            a = acc_ref[lo : lo + tl]
            b = acc_ref[lo + tl : lo + 2 * tl]
            base = (c * pairs + p) * tl
            parent = parent_ref[base : base + tl]
            small = small_ref[p] == 0
            gone = evict_ref[p] == 1
            child = jnp.where(small, a, b)
            rebuilt = jnp.where(small, b, a)
            sibling = jnp.where(gone, rebuilt, parent - child)
            hist_ref[lo : lo + tl] = jnp.where(small, child, sibling)
            hist_ref[lo + tl : lo + 2 * tl] = jnp.where(small, sibling, child)


def group_scan(x, reverse):
    span = x.shape[1]
    lane = lax.broadcasted_iota(jnp.int32, x.shape, 1) % BINS
    shift = 1
    while shift < BINS:
        if reverse:
            moved = pltpu.roll(x, span - shift, 1)
            x = x + jnp.where(lane + shift < BINS, moved, 0.0)
        else:
            moved = pltpu.roll(x, shift, 1)
            x = x + jnp.where(lane >= shift, moved, 0.0)
        shift *= 2
    return x


def gain_terms(hist_ref, nodes, lo, hi):
    rows, span = hist_ref.shape
    half = rows // 2
    tl = half // nodes
    count = (hi - lo) * tl
    lane = lax.broadcasted_iota(jnp.int32, (count, span), 1) % BINS
    left_g = group_scan(hist_ref[lo * tl : hi * tl], False)
    left_h = group_scan(hist_ref[half + lo * tl : half + hi * tl], False)
    total_g = group_scan(jnp.where(lane == BINS - 1, left_g, 0.0), True)
    total_h = group_scan(jnp.where(lane == BINS - 1, left_h, 0.0), True)

    def score(a, s):
        return a * a / (jnp.maximum(s, 0.0) + 1.0)

    gain = (
        score(left_g, left_h) + score(total_g - left_g, total_h - left_h) - score(total_g, total_h)
    )
    return jnp.sum(gain.reshape(hi - lo, tl, span), axis=1)


def gather_hist(small_side, evicted, seg_p, v_loc, parent, nodes, targets):
    n_rows, width, half = seg_p.shape
    n_outs = lax.axis_size("outs")
    vw, rows = v_loc.shape
    feats = width // 2
    out_rows = vw * nodes
    cols = feats * BINS
    total = n_rows * rows
    vmem = pl.BlockSpec(memory_space=pltpu.VMEM)
    smem = pl.BlockSpec(memory_space=pltpu.SMEM)
    return pl.pallas_call(
        functools.partial(gather_hist_kernel, nodes=nodes, targets=targets),
        out_shape=(
            jax.ShapeDtypeStruct((out_rows, cols), jnp.float32),
            jax.ShapeDtypeStruct((nodes, cols), jnp.float32),
            jax.ShapeDtypeStruct((nodes, 128), jnp.float32),
        ),
        in_specs=[smem, smem, vmem, vmem, vmem],
        out_specs=(vmem, vmem, vmem),
        scratch_shapes=[
            pltpu.VMEM((out_rows, cols), jnp.float32),
            pltpu.VMEM((n_rows, vw, rows), v_loc.dtype),
            pltpu.VMEM((n_rows, width, half), seg_p.dtype),
            pltpu.SemaphoreType.DMA((n_rows // 2,)),
            pltpu.SemaphoreType.DMA((n_rows // 2,)),
            pltpu.SemaphoreType.DMA((n_rows,)),
            pltpu.SemaphoreType.DMA((n_rows,)),
            pltpu.SemaphoreType.DMA((n_rows,)),
            pltpu.VMEM((n_outs, nodes, cols), jnp.float32),
            pltpu.VMEM((n_rows, nodes, 128), jnp.float32),
            pltpu.SemaphoreType.DMA((2, n_outs)),
            pltpu.SemaphoreType.DMA((2, n_outs)),
            pltpu.SemaphoreType.DMA((n_rows,)),
            pltpu.SemaphoreType.DMA((n_rows,)),
        ],
        compiler_params=pltpu.CompilerParams(collective_id=1, has_side_effects=True),
        cost_estimate=pl.CostEstimate(
            flops=2 * out_rows * cols * total,
            bytes_accessed=total * (vw * 2 + feats * 2) + out_rows * cols * 4,
            transcendentals=0,
        ),
    )(small_side, evicted, seg_p, v_loc, parent)


def pair_split_kernel(
    small_ref, evict_ref, seg_ref, v_ref, parent_ref, hist_ref, split_ref, best_ref,
    acc_ref, vbuf, sbuf, pbuf, vsend, vrecv, ssend, srecv, psend, precv, gbuf, mbuf, gsend, grecv, msend, mrecv,
    *, nodes, targets,
):
    n_rows = lax.axis_size("rows")
    n_outs = lax.axis_size("outs")
    r = lax.axis_index("rows")
    o = lax.axis_index("outs")
    core = r % 2
    chip = r // 2
    y = chip // 4
    x = chip % 4
    a = x + core * (y - x)
    b = y + core * (x - y)
    partner = chip * 2 + 1 - core
    barrier = pltpu.get_barrier_semaphore()

    def greet(k, carry):
        pl.semaphore_signal(barrier, 1, device_id=((r + k) % n_rows, o), device_id_type=MESH_ID)
        return carry

    lax.fori_loop(1, n_rows, greet, 0)
    for k in range(1, n_outs):
        pl.semaphore_signal(barrier, 1, device_id=(r, (o + k) % n_outs), device_id_type=MESH_ID)
    acc_ref[...] = jnp.zeros_like(acc_ref)
    block_hist(acc_ref, v_ref[...], seg_ref[chip].astype(jnp.int32), nodes)
    pl.semaphore_wait(barrier, n_rows - 1 + n_outs - 1)

    def dev(da, db):
        ap = (a + da + 4) % 4
        bp = (b + db + 4) % 4
        return ((1 - core) * (bp * 4 + ap) + core * (ap * 4 + bp)) * 2 + core

    def copy(src, sem, peer, slot):
        return pltpu.make_async_remote_copy(
            src_ref=src, dst_ref=vbuf.at[slot], send_sem=sem, recv_sem=vrecv.at[slot],
            device_id=(peer, o), device_id_type=MESH_ID,
        )

    def s_copy(k, peer, slot):
        return pltpu.make_async_remote_copy(
            src_ref=seg_ref.at[peer // 2], dst_ref=sbuf.at[slot], send_sem=ssend.at[k], recv_sem=srecv.at[slot],
            device_id=(peer, o), device_id_type=MESH_ID,
        )

    def seg_peer(k):
        return ((chip + k) % 16) * 2 + core

    def arrive(slot):
        copy(vbuf.at[slot], vsend.at[0], partner, slot).wait_recv()
        s_copy(0, slot, slot).wait_recv()

    def compute(slot):
        block_hist(acc_ref, vbuf[slot], sbuf[slot].astype(jnp.int32), nodes)

    started = []

    def start(src, sem, peer, slot):
        c = copy(src, sem, peer, slot)
        c.start()
        started.append(c)

    for j, (da, db) in enumerate([(1, 0), (-1, 0), (0, 1), (0, -1)]):
        start(v_ref, vsend.at[j], dev(da, db), r)

    def send_seg(k, carry):
        s_copy(k, seg_peer(k), r).start()
        return carry

    lax.fori_loop(1, 16, send_seg, 0)

    def row_step(db, relay):
        def body(i, carry):
            slot = dev((i * 3) % 4, db)
            arrive(slot)
            if relay:
                copy(vbuf.at[slot], vsend.at[11 + i], dev(0, 1), slot).start()
            compute(slot)
            return carry

        return body

    sem = 4
    for da in [-1, 1, None, -2]:
        if da is None:
            for db, relay in [(-1, True), (1, False)]:
                lax.fori_loop(0, 1, row_step(db, relay), 0)
            continue
        slot = dev(da, 0)
        arrive(slot)
        if da == -1:
            start(vbuf.at[slot], vsend.at[sem], dev(1, 0), slot)
            sem += 1
        start(vbuf.at[slot], vsend.at[sem], dev(0, 1), slot)
        start(vbuf.at[slot], vsend.at[sem + 1], dev(0, -1), slot)
        sem += 2
        compute(slot)
    for db, relay, lo in [(-1, True, 1), (1, False, 1), (-2, False, 0)]:
        lax.fori_loop(lo, 4, row_step(db, relay), 0)

    span = hist_ref.shape[1]
    mine = pl.ds(pl.multiple_of(core * span, span), span)
    theirs = pl.ds(pl.multiple_of((1 - core) * span, span), span)
    swap = pltpu.make_async_remote_copy(
        src_ref=acc_ref.at[:, theirs], dst_ref=pbuf, send_sem=psend, recv_sem=precv,
        device_id=(partner, o), device_id_type=MESH_ID,
    )
    swap.start()
    swap.wait_recv()
    hist_ref[...] = acc_ref[:, mine] + pbuf[...]
    swap.wait_send()
    for c in started:
        c.wait_send()

    def relay_drain(i, carry):
        slot = dev((i * 3) % 4, -1)
        copy(vbuf.at[slot], vsend.at[11 + i], dev(0, 1), slot).wait_send()
        return carry

    lax.fori_loop(0, 4, relay_drain, 0)

    def drain(k, carry):
        s_copy(k, seg_peer(k), r).wait_send()
        return carry

    lax.fori_loop(1, 16, drain, 0)

    node_hist(hist_ref, parent_ref, small_ref, evict_ref, hist_ref, nodes)
    exchange(functools.partial(gain_terms, hist_ref, nodes), split_ref, best_ref, gbuf, mbuf, gsend, grecv, msend, mrecv, targets)


def pair_split(small_side, evicted, seg_c, v_loc, parent, nodes, targets):
    chips, width, half = seg_c.shape
    n_rows = 2 * chips
    n_outs = lax.axis_size("outs")
    vw, rows = v_loc.shape
    cols = width // 2 * BINS
    span = cols // 2
    out_rows = vw * nodes
    total = n_rows * rows
    vmem = pl.BlockSpec(memory_space=pltpu.VMEM)
    smem = pl.BlockSpec(memory_space=pltpu.SMEM)
    return pl.pallas_call(
        functools.partial(pair_split_kernel, nodes=nodes, targets=targets),
        out_shape=(
            jax.ShapeDtypeStruct((out_rows, span), jnp.float32),
            jax.ShapeDtypeStruct((nodes, span), jnp.float32),
            jax.ShapeDtypeStruct((nodes, 128), jnp.float32),
        ),
        in_specs=[smem, smem, vmem, vmem, vmem],
        out_specs=(vmem, vmem, vmem),
        scratch_shapes=[
            pltpu.VMEM((out_rows, cols), jnp.float32),
            pltpu.VMEM((n_rows, vw, rows), v_loc.dtype),
            pltpu.VMEM((n_rows, width, half), seg_c.dtype),
            pltpu.VMEM((out_rows, span), jnp.float32),
            pltpu.SemaphoreType.DMA((chips,)),
            pltpu.SemaphoreType.DMA((n_rows,)),
            pltpu.SemaphoreType.DMA((chips,)),
            pltpu.SemaphoreType.DMA((n_rows,)),
            pltpu.SemaphoreType.DMA(()),
            pltpu.SemaphoreType.DMA(()),
            pltpu.VMEM((n_outs, nodes, span), jnp.float32),
            pltpu.VMEM((n_rows, nodes, 128), jnp.float32),
            pltpu.SemaphoreType.DMA((2, n_outs)),
            pltpu.SemaphoreType.DMA((2, n_outs)),
            pltpu.SemaphoreType.DMA((n_rows,)),
            pltpu.SemaphoreType.DMA((n_rows,)),
        ],
        compiler_params=pltpu.CompilerParams(collective_id=2, has_side_effects=True),
        cost_estimate=pl.CostEstimate(
            flops=2 * out_rows * cols * total // 2,
            bytes_accessed=total * (vw * 2 + width) + out_rows * cols * 4,
            transcendentals=0,
        ),
    )(small_side, evicted, seg_c, v_loc, parent)


def local(codes, node_of_row, grad, hess, small_side, evicted, parent_hist):
    pairs = small_side.shape[0]
    nodes = 2 * pairs
    local_targets = grad.shape[1]
    targets = local_targets * lax.axis_size("outs")
    n_rows = lax.axis_size("rows")
    count, features = codes.shape
    feats = features // n_rows
    half = count // 2
    seg = (node_of_row[:, None] * BINS + codes).astype(jnp.int16)
    seg_p = jnp.transpose(seg.reshape(2, half, n_rows, feats), (2, 3, 0, 1)).reshape(n_rows, 2 * feats, half)
    v_loc = jnp.concatenate([grad.T, hess.T], axis=0)
    span = feats * BINS
    parent = parent_hist.reshape(2 * pairs * local_targets, span)
    if n_rows == 32:
        seg_t = (codes.T + node_of_row[None, :] * BINS).astype(jnp.int16)
        seg_c = seg_t.reshape(n_rows // 2, 2 * feats, 2, half).reshape(n_rows // 2, 4 * feats, half)
        hist, split_gain, best = pair_split(small_side, evicted, seg_c, v_loc, parent, nodes, targets)
    else:
        hist, split_gain, best = gather_hist(small_side, evicted, seg_p, v_loc, parent, nodes, targets)
    node_hist = hist.reshape(2, nodes, local_targets, span)
    return (node_hist, split_gain, best[:, 0])


def solution(mesh):
    return jax.shard_map(
        local,
        mesh=mesh,
        in_specs=(
            P("rows", None),
            P("rows"),
            P("rows", "outs"),
            P("rows", "outs"),
            P(),
            P(),
            P(None, None, "outs", "rows"),
        ),
        out_specs=(P(None, None, "outs", "rows"), P(None, "rows"), P()),
        check_vma=False,
    )
```

```python
import functools

import jax
import jax.numpy as jnp
import numpy as np
from jax import lax
from jax.experimental import pallas as pl
from jax.experimental.pallas import tpu as pltpu
from jax.sharding import PartitionSpec as P

BINS = 32


MESH_ID = pl.DeviceIdType.MESH


def row_stages(r, n_rows):
    chips = n_rows // 2
    nx = 4 if chips % 4 == 0 else chips
    ny = chips // nx
    chip = r // 2
    core = r % 2
    y = chip // nx
    x = chip % nx
    row = 2 * nx
    stages = [
        [y * row + (r - y * row + k) % row for k in range(1, row)],
        [(((y + k) % ny) * nx + x) * 2 + core for k in range(1, ny)],
    ]
    return [stage for stage in stages if stage]


def row_peers(r, n_rows):
    return [peer for stage in row_stages(r, n_rows) for peer in stage]


def exchange(part_fn, split_ref, best_ref, gbuf, mbuf, gsend, grecv, msend, mrecv, targets):
    n_rows = lax.axis_size("rows")
    n_outs = lax.axis_size("outs")
    r = lax.axis_index("rows")
    o = lax.axis_index("outs")
    nodes = gbuf.shape[1]
    halves = [(0, nodes // 2), (nodes // 2, nodes)]

    def part_copy(h, k, dst, slot):
        lo, hi = halves[h]
        return pltpu.make_async_remote_copy(
            src_ref=gbuf.at[o, pl.ds(lo, hi - lo)],
            dst_ref=gbuf.at[slot, pl.ds(lo, hi - lo)],
            send_sem=gsend.at[h, k],
            recv_sem=grecv.at[h, slot],
            device_id=(r, dst),
            device_id_type=MESH_ID,
        )

    sends = []
    for h, (lo, hi) in enumerate(halves):
        gbuf[o, lo:hi] = part_fn(lo, hi)
        for k in range(1, n_outs):
            copy = part_copy(h, k, (o + k) % n_outs, o)
            copy.start()
            sends.append(copy)
    for h in range(2):
        for k in range(1, n_outs):
            src = (o + n_outs - k) % n_outs
            part_copy(h, k, src, src).wait_recv()
    for copy in sends:
        copy.wait_send()
    acc = gbuf[0]
    for j in range(1, n_outs):
        acc = acc + gbuf[j]
    split = acc / targets
    split_ref[...] = split
    width = mbuf.shape[2]
    best = jnp.broadcast_to(jnp.max(split, axis=1, keepdims=True), (split.shape[0], width))
    base = 0
    for peers in row_stages(r, n_rows):
        mbuf[base] = best
        sends = []
        for j, peer in enumerate(peers):
            copy = pltpu.make_async_remote_copy(
                src_ref=mbuf.at[base],
                dst_ref=mbuf.at[base + 1 + j],
                send_sem=msend.at[base + 1 + j],
                recv_sem=mrecv.at[base + 1 + j],
                device_id=(peer, o),
                device_id_type=MESH_ID,
            )
            copy.start()
            sends.append(copy)
        for copy in sends:
            copy.wait_recv()
        for copy in sends:
            copy.wait_send()
        for j in range(len(peers)):
            best = jnp.maximum(best, mbuf[base + 1 + j])
        base += len(peers) + 1
    best_ref[...] = best


def block_hist(acc_ref, v, s, nodes):
    tl = v.shape[0] // 2
    half = s.shape[1]
    feats = s.shape[0] // 2
    one = jnp.ones((), jnp.bfloat16)
    zero = jnp.zeros((), jnp.bfloat16)
    bins = lax.broadcasted_iota(jnp.int32, (BINS, half), 0)
    for h in range(2):
        vh = v[:, h * half : (h + 1) * half]
        node = s[h : h + 1] >> 5
        onehot = jnp.concatenate(
            [jnp.where((s[2 * f + h : 2 * f + h + 1] & (BINS - 1)) == bins, one, zero) for f in range(feats)],
            axis=0,
        )
        blocks = []
        for c in range(2):
            vc = vh[c * tl : (c + 1) * tl]
            for n in range(nodes):
                blocks.append(jnp.where(node == n, vc, zero))
        vals = jnp.concatenate(blocks, axis=0)
        acc_ref[...] += lax.dot_general(
            vals, onehot, (((1,), (1,)), ((), ())), preferred_element_type=jnp.float32
        )


def relay_gather(acc_ref, seg_ref, v_ref, vbuf, sbuf, vsend, fsend, vrecv, s_copy, send_seg, nodes):
    n_rows = lax.axis_size("rows")
    r = lax.axis_index("rows")
    o = lax.axis_index("outs")
    core = r % 2
    chip = r // 2
    y = chip // 4
    x = chip % 4
    a = x + core * (y - x)
    b = y + core * (x - y)
    partner = chip * 2 + 1 - core

    def dev(da, db):
        ap = (a + da + 4) % 4
        bp = (b + db + 4) % 4
        return ((1 - core) * (bp * 4 + ap) + core * (ap * 4 + bp)) * 2 + core

    def copy(src, sem, peer, slot):
        return pltpu.make_async_remote_copy(
            src_ref=src, dst_ref=vbuf.at[slot], send_sem=sem, recv_sem=vrecv.at[slot],
            device_id=(peer, o), device_id_type=MESH_ID,
        )

    def arrive(slot):
        copy(vbuf.at[slot], vsend.at[0], partner, slot).wait_recv()
        s_copy(0, slot, slot).wait_recv()

    def compute(slot):
        block_hist(acc_ref, vbuf[slot], sbuf[slot].astype(jnp.int32), nodes)

    started = []

    def start(src, sem, peer, slot):
        c = copy(src, sem, peer, slot)
        c.start()
        started.append(c)

    start(v_ref, fsend.at[0], partner, r)
    for j, (da, db) in enumerate([(1, 0), (-1, 0), (0, 1), (0, -1)]):
        start(v_ref, vsend.at[j], dev(da, db), r)
    lax.fori_loop(1, n_rows, send_seg, 0)

    sem = 4
    for j, da in enumerate([-1, 1, -2]):
        slot = dev(da, 0)
        arrive(slot)
        if da == -1:
            start(vbuf.at[slot], vsend.at[sem], dev(1, 0), slot)
            sem += 1
        start(vbuf.at[slot], vsend.at[sem], dev(0, 1), slot)
        start(vbuf.at[slot], vsend.at[sem + 1], dev(0, -1), slot)
        sem += 2
        start(vbuf.at[slot], fsend.at[1 + j], partner, slot)
        compute(slot)

    def row_step(db, relay, first):
        def body(i, carry):
            slot = dev((i * 3) % 4, db)
            arrive(slot)
            if relay:
                copy(vbuf.at[slot], vsend.at[11 + i], dev(0, -db), slot).start()
            copy(vbuf.at[slot], fsend.at[first + i], partner, slot).start()
            compute(slot)
            return carry

        return body

    def row_drain(db, relay, first):
        def body(i, carry):
            slot = dev((i * 3) % 4, db)
            if relay:
                copy(vbuf.at[slot], vsend.at[11 + i], dev(0, -db), slot).wait_send()
            copy(vbuf.at[slot], fsend.at[first + i], partner, slot).wait_send()
            return carry

        return body

    rows_plan = [(-1, True, 4, 0, 2), (1, False, 8, 0, 2), (-1, False, 4, 2, 4), (1, True, 8, 2, 4), (2, False, 12, 0, 4)]
    for db, relay, first, lo, hi in rows_plan:
        lax.fori_loop(lo, hi, row_step(db, relay, first), 0)

    def take_partner(k, carry):
        slot = ((chip + 16 - k) % 16) * 2 + 1 - core
        arrive(slot)
        compute(slot)
        return carry

    lax.fori_loop(0, 16, take_partner, 0)
    for c in started:
        c.wait_send()
    for db, relay, first, lo, hi in rows_plan:
        lax.fori_loop(lo, hi, row_drain(db, relay, first), 0)


def gather_hist_kernel(
    small_ref, evict_ref, seg_ref, v_ref, parent_ref, hist_ref, split_ref, best_ref,
    acc_ref, vbuf, sbuf, vsend, fsend, vrecv, ssend, srecv, gbuf, mbuf, gsend, grecv, msend, mrecv,
    *, nodes, targets,
):
    n_rows = lax.axis_size("rows")
    chips = n_rows // 2
    r = lax.axis_index("rows")
    o = lax.axis_index("outs")
    core = r % 2
    chip = r // 2
    partner = chip * 2 + 1 - core
    barrier = pltpu.get_barrier_semaphore()

    def greet(k, carry):
        pl.semaphore_signal(barrier, 1, device_id=((r + k) % n_rows, o), device_id_type=MESH_ID)
        return carry

    lax.fori_loop(1, n_rows, greet, 0)
    n_outs = lax.axis_size("outs")
    for k in range(1, n_outs):
        pl.semaphore_signal(barrier, 1, device_id=(r, (o + k) % n_outs), device_id_type=MESH_ID)
    acc_ref[...] = jnp.zeros_like(acc_ref)
    block_hist(acc_ref, v_ref[...], seg_ref[r].astype(jnp.int32), nodes)
    pl.semaphore_wait(barrier, n_rows - 1 + n_outs - 1)

    def s_copy(k, peer, slot):
        return pltpu.make_async_remote_copy(
            src_ref=seg_ref.at[peer], dst_ref=sbuf.at[slot], send_sem=ssend.at[k], recv_sem=srecv.at[slot],
            device_id=(peer, o), device_id_type=MESH_ID,
        )

    def v_copy(k, peer, slot):
        return pltpu.make_async_remote_copy(
            src_ref=v_ref, dst_ref=vbuf.at[slot], send_sem=vsend.at[k], recv_sem=vrecv.at[slot],
            device_id=(peer, o), device_id_type=MESH_ID,
        )

    def f_copy(k, slot):
        return pltpu.make_async_remote_copy(
            src_ref=vbuf.at[slot], dst_ref=vbuf.at[slot], send_sem=fsend.at[k], recv_sem=vrecv.at[slot],
            device_id=(partner, o), device_id_type=MESH_ID,
        )

    def send_seg(k, carry):
        s_copy(k, (r + k) % n_rows, r).start()
        return carry

    def drain(k, carry):
        s_copy(k, (r + k) % n_rows, r).wait_send()
        return carry

    if chips == 16:
        relay_gather(acc_ref, seg_ref, v_ref, vbuf, sbuf, vsend, fsend, vrecv, s_copy, send_seg, nodes)
        lax.fori_loop(1, n_rows, drain, 0)
    else:
        own = pltpu.make_async_remote_copy(
            src_ref=v_ref, dst_ref=vbuf.at[r], send_sem=fsend.at[0], recv_sem=vrecv.at[r],
            device_id=(partner, o), device_id_type=MESH_ID,
        )
        own.start()

        def send(k, carry):
            v_copy(k, ((chip + k) % chips) * 2 + core, r).start()
            return carry

        lax.fori_loop(1, chips, send, 0)

        lax.fori_loop(1, n_rows, send_seg, 0)

        def take_direct(k, carry):
            src = ((chip + chips - k) % chips) * 2 + core
            v_copy(k, src, src).wait_recv()
            f_copy(k, src).start()
            s_copy(k, src, src).wait_recv()
            block_hist(acc_ref, vbuf[src], sbuf[src].astype(jnp.int32), nodes)
            return carry

        lax.fori_loop(1, chips, take_direct, 0)

        def take_forwarded(k, carry):
            src = ((chip + chips - k) % chips) * 2 + 1 - core
            f_copy(k, src).wait_recv()
            s_copy(k, src, src).wait_recv()
            block_hist(acc_ref, vbuf[src], sbuf[src].astype(jnp.int32), nodes)
            return carry

        lax.fori_loop(0, chips, take_forwarded, 0)

        lax.fori_loop(1, n_rows, drain, 0)

        def drain_v(k, carry):
            v_copy(k, ((chip + k) % chips) * 2 + core, r).wait_send()
            return carry

        lax.fori_loop(1, chips, drain_v, 0)
        own.wait_send()

        def drain_f(k, carry):
            f_copy(k, ((chip + chips - k) % chips) * 2 + core).wait_send()
            return carry

        lax.fori_loop(1, chips, drain_f, 0)


    node_hist(acc_ref, parent_ref, small_ref, evict_ref, hist_ref, nodes)
    exchange(functools.partial(gain_terms, hist_ref, nodes), split_ref, best_ref, gbuf, mbuf, gsend, grecv, msend, mrecv, targets)


def node_hist(acc_ref, parent_ref, small_ref, evict_ref, hist_ref, nodes):
    pairs = nodes // 2
    tl = acc_ref.shape[0] // (2 * nodes)
    for c in range(2):
        for p in range(pairs):
            lo = c * nodes * tl + 2 * p * tl
            a = acc_ref[lo : lo + tl]
            b = acc_ref[lo + tl : lo + 2 * tl]
            base = (c * pairs + p) * tl
            parent = parent_ref[base : base + tl]
            small = small_ref[p] == 0
            gone = evict_ref[p] == 1
            child = jnp.where(small, a, b)
            rebuilt = jnp.where(small, b, a)
            sibling = jnp.where(gone, rebuilt, parent - child)
            hist_ref[lo : lo + tl] = jnp.where(small, child, sibling)
            hist_ref[lo + tl : lo + 2 * tl] = jnp.where(small, sibling, child)


def group_scan(x, reverse):
    span = x.shape[1]
    lane = lax.broadcasted_iota(jnp.int32, x.shape, 1) % BINS
    shift = 1
    while shift < BINS:
        if reverse:
            moved = pltpu.roll(x, span - shift, 1)
            x = x + jnp.where(lane + shift < BINS, moved, 0.0)
        else:
            moved = pltpu.roll(x, shift, 1)
            x = x + jnp.where(lane >= shift, moved, 0.0)
        shift *= 2
    return x


def gain_terms(hist_ref, nodes, lo, hi):
    rows, span = hist_ref.shape
    half = rows // 2
    tl = half // nodes
    count = (hi - lo) * tl
    lane = lax.broadcasted_iota(jnp.int32, (count, span), 1) % BINS
    left_g = group_scan(hist_ref[lo * tl : hi * tl], False)
    left_h = group_scan(hist_ref[half + lo * tl : half + hi * tl], False)
    total_g = group_scan(jnp.where(lane == BINS - 1, left_g, 0.0), True)
    total_h = group_scan(jnp.where(lane == BINS - 1, left_h, 0.0), True)

    def score(a, s):
        return a * a / (jnp.maximum(s, 0.0) + 1.0)

    gain = (
        score(left_g, left_h) + score(total_g - left_g, total_h - left_h) - score(total_g, total_h)
    )
    return jnp.sum(gain.reshape(hi - lo, tl, span), axis=1)


def gather_hist(small_side, evicted, seg_p, v_loc, parent, nodes, targets):
    n_rows, width, half = seg_p.shape
    n_outs = lax.axis_size("outs")
    vw, rows = v_loc.shape
    feats = width // 2
    out_rows = vw * nodes
    cols = feats * BINS
    total = n_rows * rows
    vmem = pl.BlockSpec(memory_space=pltpu.VMEM)
    smem = pl.BlockSpec(memory_space=pltpu.SMEM)
    return pl.pallas_call(
        functools.partial(gather_hist_kernel, nodes=nodes, targets=targets),
        out_shape=(
            jax.ShapeDtypeStruct((out_rows, cols), jnp.float32),
            jax.ShapeDtypeStruct((nodes, cols), jnp.float32),
            jax.ShapeDtypeStruct((nodes, 128), jnp.float32),
        ),
        in_specs=[smem, smem, vmem, vmem, vmem],
        out_specs=(vmem, vmem, vmem),
        scratch_shapes=[
            pltpu.VMEM((out_rows, cols), jnp.float32),
            pltpu.VMEM((n_rows, vw, rows), v_loc.dtype),
            pltpu.VMEM((n_rows, width, half), seg_p.dtype),
            pltpu.SemaphoreType.DMA((n_rows // 2,)),
            pltpu.SemaphoreType.DMA((n_rows // 2,)),
            pltpu.SemaphoreType.DMA((n_rows,)),
            pltpu.SemaphoreType.DMA((n_rows,)),
            pltpu.SemaphoreType.DMA((n_rows,)),
            pltpu.VMEM((n_outs, nodes, cols), jnp.float32),
            pltpu.VMEM((n_rows, nodes, 128), jnp.float32),
            pltpu.SemaphoreType.DMA((2, n_outs)),
            pltpu.SemaphoreType.DMA((2, n_outs)),
            pltpu.SemaphoreType.DMA((n_rows,)),
            pltpu.SemaphoreType.DMA((n_rows,)),
        ],
        compiler_params=pltpu.CompilerParams(collective_id=1, has_side_effects=True),
        cost_estimate=pl.CostEstimate(
            flops=2 * out_rows * cols * total,
            bytes_accessed=total * (vw * 2 + feats * 2) + out_rows * cols * 4,
            transcendentals=0,
        ),
    )(small_side, evicted, seg_p, v_loc, parent)


def forward_order(i):
    return (3 * i + (i // 2) * (2 * i - 1)) % 4


def pair_split_kernel(
    small_ref, evict_ref, seg_ref, v_ref, parent_ref, hist_ref, split_ref, best_ref,
    acc_ref, vbuf, sbuf, pbuf, vsend, vrecv, ssend, srecv, psend, precv, gbuf, mbuf, gsend, grecv, msend, mrecv,
    *, nodes, targets,
):
    n_rows = lax.axis_size("rows")
    n_outs = lax.axis_size("outs")
    r = lax.axis_index("rows")
    o = lax.axis_index("outs")
    core = r % 2
    chip = r // 2
    y = chip // 4
    x = chip % 4
    a = x + core * (y - x)
    b = y + core * (x - y)
    partner = chip * 2 + 1 - core
    barrier = pltpu.get_barrier_semaphore()

    def greet(k, carry):
        pl.semaphore_signal(barrier, 1, device_id=((r + k) % n_rows, o), device_id_type=MESH_ID)
        return carry

    lax.fori_loop(1, n_rows, greet, 0)
    for k in range(1, n_outs):
        pl.semaphore_signal(barrier, 1, device_id=(r, (o + k) % n_outs), device_id_type=MESH_ID)
    acc_ref[...] = jnp.zeros_like(acc_ref)
    block_hist(acc_ref, v_ref[...], seg_ref[chip].astype(jnp.int32), nodes)
    pl.semaphore_wait(barrier, n_rows - 1 + n_outs - 1)

    def dev(da, db):
        ap = (a + da + 4) % 4
        bp = (b + db + 4) % 4
        return ((1 - core) * (bp * 4 + ap) + core * (ap * 4 + bp)) * 2 + core

    def copy(src, sem, peer, slot):
        return pltpu.make_async_remote_copy(
            src_ref=src, dst_ref=vbuf.at[slot], send_sem=sem, recv_sem=vrecv.at[slot],
            device_id=(peer, o), device_id_type=MESH_ID,
        )

    def s_copy(k, peer, slot):
        return pltpu.make_async_remote_copy(
            src_ref=seg_ref.at[peer // 2], dst_ref=sbuf.at[slot], send_sem=ssend.at[k], recv_sem=srecv.at[slot],
            device_id=(peer, o), device_id_type=MESH_ID,
        )

    def seg_peer(k):
        return ((chip + k) % 16) * 2 + core

    def arrive(slot):
        copy(vbuf.at[slot], vsend.at[0], partner, slot).wait_recv()
        s_copy(0, slot, slot).wait_recv()

    def compute(slot):
        block_hist(acc_ref, vbuf[slot], sbuf[slot].astype(jnp.int32), nodes)

    started = []

    def start(src, sem, peer, slot):
        c = copy(src, sem, peer, slot)
        c.start()
        started.append(c)

    for j, (da, db) in enumerate([(1, 0), (-1, 0), (0, 1), (0, -1)]):
        start(v_ref, vsend.at[j], dev(da, db), r)

    def send_seg(k, carry):
        s_copy(k, seg_peer(k), r).start()
        return carry

    lax.fori_loop(1, 16, send_seg, 0)

    def row_step(db, relay):
        def body(i, carry):
            slot = dev(forward_order(i), db)
            arrive(slot)
            if relay:
                copy(vbuf.at[slot], vsend.at[11 + i], dev(0, 1), slot).start()
            compute(slot)
            return carry

        return body

    sem = 4
    for da in [-1, 1, None, -2]:
        if da is None:
            for db, relay in [(-1, True), (1, False)]:
                lax.fori_loop(0, 1, row_step(db, relay), 0)
            continue
        slot = dev(da, 0)
        arrive(slot)
        if da == -1:
            start(vbuf.at[slot], vsend.at[sem], dev(1, 0), slot)
            sem += 1
        start(vbuf.at[slot], vsend.at[sem], dev(0, 1), slot)
        start(vbuf.at[slot], vsend.at[sem + 1], dev(0, -1), slot)
        sem += 2
        compute(slot)
    for db, relay, lo in [(-1, True, 1), (1, False, 1), (-2, False, 0)]:
        lax.fori_loop(lo, 4, row_step(db, relay), 0)

    span = hist_ref.shape[1]
    mine = pl.ds(pl.multiple_of(core * span, span), span)
    theirs = pl.ds(pl.multiple_of((1 - core) * span, span), span)
    swap = pltpu.make_async_remote_copy(
        src_ref=acc_ref.at[:, theirs], dst_ref=pbuf, send_sem=psend, recv_sem=precv,
        device_id=(partner, o), device_id_type=MESH_ID,
    )
    swap.start()
    swap.wait_recv()
    hist_ref[...] = acc_ref[:, mine] + pbuf[...]
    swap.wait_send()
    for c in started:
        c.wait_send()

    def relay_drain(i, carry):
        slot = dev(forward_order(i), -1)
        copy(vbuf.at[slot], vsend.at[11 + i], dev(0, 1), slot).wait_send()
        return carry

    lax.fori_loop(0, 4, relay_drain, 0)

    def drain(k, carry):
        s_copy(k, seg_peer(k), r).wait_send()
        return carry

    lax.fori_loop(1, 16, drain, 0)

    node_hist(hist_ref, parent_ref, small_ref, evict_ref, hist_ref, nodes)
    exchange(functools.partial(gain_terms, hist_ref, nodes), split_ref, best_ref, gbuf, mbuf, gsend, grecv, msend, mrecv, targets)


def pair_split(small_side, evicted, seg_c, v_loc, parent, nodes, targets):
    chips, width, half = seg_c.shape
    n_rows = 2 * chips
    n_outs = lax.axis_size("outs")
    vw, rows = v_loc.shape
    cols = width // 2 * BINS
    span = cols // 2
    out_rows = vw * nodes
    total = n_rows * rows
    vmem = pl.BlockSpec(memory_space=pltpu.VMEM)
    smem = pl.BlockSpec(memory_space=pltpu.SMEM)
    return pl.pallas_call(
        functools.partial(pair_split_kernel, nodes=nodes, targets=targets),
        out_shape=(
            jax.ShapeDtypeStruct((out_rows, span), jnp.float32),
            jax.ShapeDtypeStruct((nodes, span), jnp.float32),
            jax.ShapeDtypeStruct((nodes, 128), jnp.float32),
        ),
        in_specs=[smem, smem, vmem, vmem, vmem],
        out_specs=(vmem, vmem, vmem),
        scratch_shapes=[
            pltpu.VMEM((out_rows, cols), jnp.float32),
            pltpu.VMEM((n_rows, vw, rows), v_loc.dtype),
            pltpu.VMEM((n_rows, width, half), seg_c.dtype),
            pltpu.VMEM((out_rows, span), jnp.float32),
            pltpu.SemaphoreType.DMA((chips,)),
            pltpu.SemaphoreType.DMA((n_rows,)),
            pltpu.SemaphoreType.DMA((chips,)),
            pltpu.SemaphoreType.DMA((n_rows,)),
            pltpu.SemaphoreType.DMA(()),
            pltpu.SemaphoreType.DMA(()),
            pltpu.VMEM((n_outs, nodes, span), jnp.float32),
            pltpu.VMEM((n_rows, nodes, 128), jnp.float32),
            pltpu.SemaphoreType.DMA((2, n_outs)),
            pltpu.SemaphoreType.DMA((2, n_outs)),
            pltpu.SemaphoreType.DMA((n_rows,)),
            pltpu.SemaphoreType.DMA((n_rows,)),
        ],
        compiler_params=pltpu.CompilerParams(collective_id=2, has_side_effects=True),
        cost_estimate=pl.CostEstimate(
            flops=2 * out_rows * cols * total // 2,
            bytes_accessed=total * (vw * 2 + width) + out_rows * cols * 4,
            transcendentals=0,
        ),
    )(small_side, evicted, seg_c, v_loc, parent)


def local(codes, node_of_row, grad, hess, small_side, evicted, parent_hist):
    pairs = small_side.shape[0]
    nodes = 2 * pairs
    local_targets = grad.shape[1]
    targets = local_targets * lax.axis_size("outs")
    n_rows = lax.axis_size("rows")
    count, features = codes.shape
    feats = features // n_rows
    half = count // 2
    seg = (node_of_row[:, None] * BINS + codes).astype(jnp.int16)
    seg_p = jnp.transpose(seg.reshape(2, half, n_rows, feats), (2, 3, 0, 1)).reshape(n_rows, 2 * feats, half)
    v_loc = jnp.concatenate([grad.T, hess.T], axis=0)
    span = feats * BINS
    parent = parent_hist.reshape(2 * pairs * local_targets, span)
    if n_rows == 32:
        seg_t = (codes.T + node_of_row[None, :] * BINS).astype(jnp.int16)
        seg_c = seg_t.reshape(n_rows // 2, 2 * feats, 2, half).reshape(n_rows // 2, 4 * feats, half)
        hist, split_gain, best = pair_split(small_side, evicted, seg_c, v_loc, parent, nodes, targets)
    else:
        hist, split_gain, best = gather_hist(small_side, evicted, seg_p, v_loc, parent, nodes, targets)
    node_hist = hist.reshape(2, nodes, local_targets, span)
    return (node_hist, split_gain, best[:, 0])


def solution(mesh):
    return jax.shard_map(
        local,
        mesh=mesh,
        in_specs=(
            P("rows", None),
            P("rows"),
            P("rows", "outs"),
            P("rows", "outs"),
            P(),
            P(),
            P(None, None, "outs", "rows"),
        ),
        out_specs=(P(None, None, "outs", "rows"), P(None, "rows"), P()),
        check_vma=False,
    )
```

```python
import functools

import jax
import jax.numpy as jnp
import numpy as np
from jax import lax
from jax.experimental import pallas as pl
from jax.experimental.pallas import tpu as pltpu
from jax.sharding import PartitionSpec as P

BINS = 32


MESH_ID = pl.DeviceIdType.MESH


def row_stages(r, n_rows):
    chips = n_rows // 2
    nx = 4 if chips % 4 == 0 else chips
    ny = chips // nx
    chip = r // 2
    core = r % 2
    y = chip // nx
    x = chip % nx
    row = 2 * nx
    stages = [
        [y * row + (r - y * row + k) % row for k in range(1, row)],
        [(((y + k) % ny) * nx + x) * 2 + core for k in range(1, ny)],
    ]
    return [stage for stage in stages if stage]


def row_peers(r, n_rows):
    return [peer for stage in row_stages(r, n_rows) for peer in stage]


def exchange(part_fn, split_ref, best_ref, gbuf, mbuf, gsend, grecv, msend, mrecv, targets):
    n_rows = lax.axis_size("rows")
    n_outs = lax.axis_size("outs")
    r = lax.axis_index("rows")
    o = lax.axis_index("outs")
    nodes = gbuf.shape[1]
    halves = [(0, nodes // 2), (nodes // 2, nodes)]

    def part_copy(h, k, dst, slot):
        lo, hi = halves[h]
        return pltpu.make_async_remote_copy(
            src_ref=gbuf.at[o, pl.ds(lo, hi - lo)],
            dst_ref=gbuf.at[slot, pl.ds(lo, hi - lo)],
            send_sem=gsend.at[h, k],
            recv_sem=grecv.at[h, slot],
            device_id=(r, dst),
            device_id_type=MESH_ID,
        )

    sends = []
    for h, (lo, hi) in enumerate(halves):
        gbuf[o, lo:hi] = part_fn(lo, hi)
        for k in range(1, n_outs):
            copy = part_copy(h, k, (o + k) % n_outs, o)
            copy.start()
            sends.append(copy)
    for h in range(2):
        for k in range(1, n_outs):
            src = (o + n_outs - k) % n_outs
            part_copy(h, k, src, src).wait_recv()
    for copy in sends:
        copy.wait_send()
    acc = gbuf[0]
    for j in range(1, n_outs):
        acc = acc + gbuf[j]
    split = acc / targets
    split_ref[...] = split
    width = mbuf.shape[2]
    best = jnp.broadcast_to(jnp.max(split, axis=1, keepdims=True), (split.shape[0], width))
    base = 0
    for peers in row_stages(r, n_rows):
        mbuf[base] = best
        sends = []
        for j, peer in enumerate(peers):
            copy = pltpu.make_async_remote_copy(
                src_ref=mbuf.at[base],
                dst_ref=mbuf.at[base + 1 + j],
                send_sem=msend.at[base + 1 + j],
                recv_sem=mrecv.at[base + 1 + j],
                device_id=(peer, o),
                device_id_type=MESH_ID,
            )
            copy.start()
            sends.append(copy)
        for copy in sends:
            copy.wait_recv()
        for copy in sends:
            copy.wait_send()
        for j in range(len(peers)):
            best = jnp.maximum(best, mbuf[base + 1 + j])
        base += len(peers) + 1
    best_ref[...] = best


def block_hist(acc_ref, v, s, nodes):
    tl = v.shape[0] // 2
    half = s.shape[1]
    feats = s.shape[0] // 2
    one = jnp.ones((), jnp.bfloat16)
    zero = jnp.zeros((), jnp.bfloat16)
    bins = lax.broadcasted_iota(jnp.int32, (BINS, half), 0)
    for h in range(2):
        vh = v[:, h * half : (h + 1) * half]
        node = s[h : h + 1] >> 5
        onehot = jnp.concatenate(
            [jnp.where((s[2 * f + h : 2 * f + h + 1] & (BINS - 1)) == bins, one, zero) for f in range(feats)],
            axis=0,
        )
        blocks = []
        for c in range(2):
            vc = vh[c * tl : (c + 1) * tl]
            for n in range(nodes):
                blocks.append(jnp.where(node == n, vc, zero))
        vals = jnp.concatenate(blocks, axis=0)
        acc_ref[...] += lax.dot_general(
            vals, onehot, (((1,), (1,)), ((), ())), preferred_element_type=jnp.float32
        )


def relay_gather(acc_ref, seg_ref, v_ref, vbuf, sbuf, vsend, fsend, vrecv, s_copy, send_seg, nodes):
    n_rows = lax.axis_size("rows")
    r = lax.axis_index("rows")
    o = lax.axis_index("outs")
    core = r % 2
    chip = r // 2
    y = chip // 4
    x = chip % 4
    a = x + core * (y - x)
    b = y + core * (x - y)
    partner = chip * 2 + 1 - core

    def dev(da, db):
        ap = (a + da + 4) % 4
        bp = (b + db + 4) % 4
        return ((1 - core) * (bp * 4 + ap) + core * (ap * 4 + bp)) * 2 + core

    def copy(src, sem, peer, slot):
        return pltpu.make_async_remote_copy(
            src_ref=src, dst_ref=vbuf.at[slot], send_sem=sem, recv_sem=vrecv.at[slot],
            device_id=(peer, o), device_id_type=MESH_ID,
        )

    def arrive(slot):
        copy(vbuf.at[slot], vsend.at[0], partner, slot).wait_recv()
        s_copy(0, slot, slot).wait_recv()

    def compute(slot):
        block_hist(acc_ref, vbuf[slot], sbuf[slot].astype(jnp.int32), nodes)

    started = []

    def start(src, sem, peer, slot):
        c = copy(src, sem, peer, slot)
        c.start()
        started.append(c)

    start(v_ref, fsend.at[0], partner, r)
    for j, (da, db) in enumerate([(1, 0), (-1, 0), (0, 1), (0, -1)]):
        start(v_ref, vsend.at[j], dev(da, db), r)
    lax.fori_loop(1, n_rows, send_seg, 0)

    sem = 4
    for j, da in enumerate([-1, 1, -2]):
        slot = dev(da, 0)
        arrive(slot)
        if da == -1:
            start(vbuf.at[slot], vsend.at[sem], dev(1, 0), slot)
            sem += 1
        start(vbuf.at[slot], vsend.at[sem], dev(0, 1), slot)
        start(vbuf.at[slot], vsend.at[sem + 1], dev(0, -1), slot)
        sem += 2
        start(vbuf.at[slot], fsend.at[1 + j], partner, slot)
        compute(slot)

    def row_step(db, relay, first):
        def body(i, carry):
            slot = dev((i * 3) % 4, db)
            arrive(slot)
            if relay:
                copy(vbuf.at[slot], vsend.at[11 + i], dev(0, -db), slot).start()
            copy(vbuf.at[slot], fsend.at[first + i], partner, slot).start()
            compute(slot)
            return carry

        return body

    def row_drain(db, relay, first):
        def body(i, carry):
            slot = dev((i * 3) % 4, db)
            if relay:
                copy(vbuf.at[slot], vsend.at[11 + i], dev(0, -db), slot).wait_send()
            copy(vbuf.at[slot], fsend.at[first + i], partner, slot).wait_send()
            return carry

        return body

    rows_plan = [(-1, True, 4, 0, 2), (1, False, 8, 0, 2), (-1, False, 4, 2, 4), (1, True, 8, 2, 4), (2, False, 12, 0, 4)]
    for db, relay, first, lo, hi in rows_plan:
        lax.fori_loop(lo, hi, row_step(db, relay, first), 0)

    def take_partner(k, carry):
        slot = ((chip + 16 - k) % 16) * 2 + 1 - core
        arrive(slot)
        compute(slot)
        return carry

    lax.fori_loop(0, 16, take_partner, 0)
    for c in started:
        c.wait_send()
    for db, relay, first, lo, hi in rows_plan:
        lax.fori_loop(lo, hi, row_drain(db, relay, first), 0)


def gather_hist_kernel(
    small_ref, evict_ref, seg_ref, v_ref, parent_ref, hist_ref, split_ref, best_ref,
    acc_ref, vbuf, sbuf, vsend, fsend, vrecv, ssend, srecv, gbuf, mbuf, gsend, grecv, msend, mrecv,
    *, nodes, targets,
):
    n_rows = lax.axis_size("rows")
    chips = n_rows // 2
    r = lax.axis_index("rows")
    o = lax.axis_index("outs")
    core = r % 2
    chip = r // 2
    partner = chip * 2 + 1 - core
    barrier = pltpu.get_barrier_semaphore()

    def greet(k, carry):
        pl.semaphore_signal(barrier, 1, device_id=((r + k) % n_rows, o), device_id_type=MESH_ID)
        return carry

    lax.fori_loop(1, n_rows, greet, 0)
    n_outs = lax.axis_size("outs")
    for k in range(1, n_outs):
        pl.semaphore_signal(barrier, 1, device_id=(r, (o + k) % n_outs), device_id_type=MESH_ID)
    acc_ref[...] = jnp.zeros_like(acc_ref)
    block_hist(acc_ref, v_ref[...], seg_ref[r].astype(jnp.int32), nodes)
    pl.semaphore_wait(barrier, n_rows - 1 + n_outs - 1)

    def s_copy(k, peer, slot):
        return pltpu.make_async_remote_copy(
            src_ref=seg_ref.at[peer], dst_ref=sbuf.at[slot], send_sem=ssend.at[k], recv_sem=srecv.at[slot],
            device_id=(peer, o), device_id_type=MESH_ID,
        )

    def v_copy(k, peer, slot):
        return pltpu.make_async_remote_copy(
            src_ref=v_ref, dst_ref=vbuf.at[slot], send_sem=vsend.at[k], recv_sem=vrecv.at[slot],
            device_id=(peer, o), device_id_type=MESH_ID,
        )

    def f_copy(k, slot):
        return pltpu.make_async_remote_copy(
            src_ref=vbuf.at[slot], dst_ref=vbuf.at[slot], send_sem=fsend.at[k], recv_sem=vrecv.at[slot],
            device_id=(partner, o), device_id_type=MESH_ID,
        )

    def send_seg(k, carry):
        s_copy(k, (r + k) % n_rows, r).start()
        return carry

    def drain(k, carry):
        s_copy(k, (r + k) % n_rows, r).wait_send()
        return carry

    if chips == 16:
        relay_gather(acc_ref, seg_ref, v_ref, vbuf, sbuf, vsend, fsend, vrecv, s_copy, send_seg, nodes)
        lax.fori_loop(1, n_rows, drain, 0)
    else:
        own = pltpu.make_async_remote_copy(
            src_ref=v_ref, dst_ref=vbuf.at[r], send_sem=fsend.at[0], recv_sem=vrecv.at[r],
            device_id=(partner, o), device_id_type=MESH_ID,
        )
        own.start()

        def send(k, carry):
            v_copy(k, ((chip + k) % chips) * 2 + core, r).start()
            return carry

        lax.fori_loop(1, chips, send, 0)

        lax.fori_loop(1, n_rows, send_seg, 0)

        def take_direct(k, carry):
            src = ((chip + chips - k) % chips) * 2 + core
            v_copy(k, src, src).wait_recv()
            f_copy(k, src).start()
            s_copy(k, src, src).wait_recv()
            block_hist(acc_ref, vbuf[src], sbuf[src].astype(jnp.int32), nodes)
            return carry

        lax.fori_loop(1, chips, take_direct, 0)

        def take_forwarded(k, carry):
            src = ((chip + chips - k) % chips) * 2 + 1 - core
            f_copy(k, src).wait_recv()
            s_copy(k, src, src).wait_recv()
            block_hist(acc_ref, vbuf[src], sbuf[src].astype(jnp.int32), nodes)
            return carry

        lax.fori_loop(0, chips, take_forwarded, 0)

        lax.fori_loop(1, n_rows, drain, 0)

        def drain_v(k, carry):
            v_copy(k, ((chip + k) % chips) * 2 + core, r).wait_send()
            return carry

        lax.fori_loop(1, chips, drain_v, 0)
        own.wait_send()

        def drain_f(k, carry):
            f_copy(k, ((chip + chips - k) % chips) * 2 + core).wait_send()
            return carry

        lax.fori_loop(1, chips, drain_f, 0)


    node_hist(acc_ref, parent_ref, small_ref, evict_ref, hist_ref, nodes)
    exchange(functools.partial(gain_terms, hist_ref, nodes), split_ref, best_ref, gbuf, mbuf, gsend, grecv, msend, mrecv, targets)


def node_hist(acc_ref, parent_ref, small_ref, evict_ref, hist_ref, nodes):
    pairs = nodes // 2
    tl = acc_ref.shape[0] // (2 * nodes)
    for c in range(2):
        for p in range(pairs):
            lo = c * nodes * tl + 2 * p * tl
            a = acc_ref[lo : lo + tl]
            b = acc_ref[lo + tl : lo + 2 * tl]
            base = (c * pairs + p) * tl
            parent = parent_ref[base : base + tl]
            small = small_ref[p] == 0
            gone = evict_ref[p] == 1
            child = jnp.where(small, a, b)
            rebuilt = jnp.where(small, b, a)
            sibling = jnp.where(gone, rebuilt, parent - child)
            hist_ref[lo : lo + tl] = jnp.where(small, child, sibling)
            hist_ref[lo + tl : lo + 2 * tl] = jnp.where(small, sibling, child)


def group_scan(x, reverse):
    span = x.shape[1]
    lane = lax.broadcasted_iota(jnp.int32, x.shape, 1) % BINS
    shift = 1
    while shift < BINS:
        if reverse:
            moved = pltpu.roll(x, span - shift, 1)
            x = x + jnp.where(lane + shift < BINS, moved, 0.0)
        else:
            moved = pltpu.roll(x, shift, 1)
            x = x + jnp.where(lane >= shift, moved, 0.0)
        shift *= 2
    return x


def gain_terms(hist_ref, nodes, lo, hi):
    rows, span = hist_ref.shape
    half = rows // 2
    tl = half // nodes
    count = (hi - lo) * tl
    lane = lax.broadcasted_iota(jnp.int32, (count, span), 1) % BINS
    left_g = group_scan(hist_ref[lo * tl : hi * tl], False)
    left_h = group_scan(hist_ref[half + lo * tl : half + hi * tl], False)
    total_g = group_scan(jnp.where(lane == BINS - 1, left_g, 0.0), True)
    total_h = group_scan(jnp.where(lane == BINS - 1, left_h, 0.0), True)

    def score(a, s):
        return a * a / (jnp.maximum(s, 0.0) + 1.0)

    gain = (
        score(left_g, left_h) + score(total_g - left_g, total_h - left_h) - score(total_g, total_h)
    )
    return jnp.sum(gain.reshape(hi - lo, tl, span), axis=1)


def gather_hist(small_side, evicted, seg_p, v_loc, parent, nodes, targets):
    n_rows, width, half = seg_p.shape
    n_outs = lax.axis_size("outs")
    vw, rows = v_loc.shape
    feats = width // 2
    out_rows = vw * nodes
    cols = feats * BINS
    total = n_rows * rows
    vmem = pl.BlockSpec(memory_space=pltpu.VMEM)
    smem = pl.BlockSpec(memory_space=pltpu.SMEM)
    return pl.pallas_call(
        functools.partial(gather_hist_kernel, nodes=nodes, targets=targets),
        out_shape=(
            jax.ShapeDtypeStruct((out_rows, cols), jnp.float32),
            jax.ShapeDtypeStruct((nodes, cols), jnp.float32),
            jax.ShapeDtypeStruct((nodes, 128), jnp.float32),
        ),
        in_specs=[smem, smem, vmem, vmem, vmem],
        out_specs=(vmem, vmem, vmem),
        scratch_shapes=[
            pltpu.VMEM((out_rows, cols), jnp.float32),
            pltpu.VMEM((n_rows, vw, rows), v_loc.dtype),
            pltpu.VMEM((n_rows, width, half), seg_p.dtype),
            pltpu.SemaphoreType.DMA((n_rows // 2,)),
            pltpu.SemaphoreType.DMA((n_rows // 2,)),
            pltpu.SemaphoreType.DMA((n_rows,)),
            pltpu.SemaphoreType.DMA((n_rows,)),
            pltpu.SemaphoreType.DMA((n_rows,)),
            pltpu.VMEM((n_outs, nodes, cols), jnp.float32),
            pltpu.VMEM((n_rows, nodes, 128), jnp.float32),
            pltpu.SemaphoreType.DMA((2, n_outs)),
            pltpu.SemaphoreType.DMA((2, n_outs)),
            pltpu.SemaphoreType.DMA((n_rows,)),
            pltpu.SemaphoreType.DMA((n_rows,)),
        ],
        compiler_params=pltpu.CompilerParams(collective_id=1, has_side_effects=True),
        cost_estimate=pl.CostEstimate(
            flops=2 * out_rows * cols * total,
            bytes_accessed=total * (vw * 2 + feats * 2) + out_rows * cols * 4,
            transcendentals=0,
        ),
    )(small_side, evicted, seg_p, v_loc, parent)


def forward_order(i):
    return (3 * i + (i // 2) * (2 * i - 1)) % 4


def pair_split_kernel(
    small_ref, evict_ref, seg_ref, v_ref, parent_ref, hist_ref, split_ref, best_ref,
    acc_ref, vbuf, sbuf, pbuf, vsend, vrecv, ssend, srecv, psend, precv, gbuf, mbuf, gsend, grecv, msend, mrecv,
    *, nodes, targets,
):
    n_rows = lax.axis_size("rows")
    n_outs = lax.axis_size("outs")
    r = lax.axis_index("rows")
    o = lax.axis_index("outs")
    core = r % 2
    chip = r // 2
    y = chip // 4
    x = chip % 4
    a = x + core * (y - x)
    b = y + core * (x - y)
    partner = chip * 2 + 1 - core
    barrier = pltpu.get_barrier_semaphore()

    def greet(k, carry):
        pl.semaphore_signal(barrier, 1, device_id=((r + k) % n_rows, o), device_id_type=MESH_ID)
        return carry

    lax.fori_loop(1, n_rows, greet, 0)
    for k in range(1, n_outs):
        pl.semaphore_signal(barrier, 1, device_id=(r, (o + k) % n_outs), device_id_type=MESH_ID)
    acc_ref[...] = jnp.zeros_like(acc_ref)
    block_hist(acc_ref, v_ref[...], seg_ref[chip].astype(jnp.int32), nodes)
    pl.semaphore_wait(barrier, n_rows - 1 + n_outs - 1)

    def dev(da, db):
        ap = (a + da + 4) % 4
        bp = (b + db + 4) % 4
        return ((1 - core) * (bp * 4 + ap) + core * (ap * 4 + bp)) * 2 + core

    def copy(src, sem, peer, slot):
        return pltpu.make_async_remote_copy(
            src_ref=src, dst_ref=vbuf.at[slot], send_sem=sem, recv_sem=vrecv.at[slot],
            device_id=(peer, o), device_id_type=MESH_ID,
        )

    def s_copy(k, peer, slot):
        return pltpu.make_async_remote_copy(
            src_ref=seg_ref.at[peer // 2], dst_ref=sbuf.at[slot], send_sem=ssend.at[k], recv_sem=srecv.at[slot],
            device_id=(peer, o), device_id_type=MESH_ID,
        )

    def seg_peer(k):
        return ((chip + k) % 16) * 2 + core

    def arrive(slot):
        copy(vbuf.at[slot], vsend.at[0], partner, slot).wait_recv()
        s_copy(0, slot, slot).wait_recv()

    def compute(slot):
        block_hist(acc_ref, vbuf[slot], sbuf[slot].astype(jnp.int32), nodes)

    started = []

    def start(src, sem, peer, slot):
        c = copy(src, sem, peer, slot)
        c.start()
        started.append(c)

    for j, (da, db) in enumerate([(1, 0), (-1, 0), (0, 1), (0, -1)]):
        start(v_ref, vsend.at[j], dev(da, db), r)

    def send_seg(k, carry):
        s_copy(k, seg_peer(k), r).start()
        return carry

    lax.fori_loop(1, 16, send_seg, 0)

    def row_step(db, relay):
        def body(i, carry):
            slot = dev(forward_order(i), db)
            arrive(slot)
            if relay:
                copy(vbuf.at[slot], vsend.at[11 + i], dev(0, 1), slot).start()
            compute(slot)
            return carry

        return body

    sem = 4
    for da in [-1, 1, None, -2]:
        if da is None:
            for db, relay in [(-1, True), (1, False)]:
                lax.fori_loop(0, 1, row_step(db, relay), 0)
            continue
        slot = dev(da, 0)
        arrive(slot)
        if da == -1:
            start(vbuf.at[slot], vsend.at[sem], dev(1, 0), slot)
            sem += 1
        start(vbuf.at[slot], vsend.at[sem], dev(0, 1), slot)
        start(vbuf.at[slot], vsend.at[sem + 1], dev(0, -1), slot)
        sem += 2
        compute(slot)
    below = row_step(-1, True)
    above = row_step(1, False)

    def both_rows(i, carry):
        return above(i, below(i, carry))

    lax.fori_loop(1, 4, both_rows, 0)
    lax.fori_loop(0, 4, row_step(-2, False), 0)

    span = hist_ref.shape[1]
    mine = pl.ds(pl.multiple_of(core * span, span), span)
    theirs = pl.ds(pl.multiple_of((1 - core) * span, span), span)
    swap = pltpu.make_async_remote_copy(
        src_ref=acc_ref.at[:, theirs], dst_ref=pbuf, send_sem=psend, recv_sem=precv,
        device_id=(partner, o), device_id_type=MESH_ID,
    )
    swap.start()
    swap.wait_recv()
    hist_ref[...] = acc_ref[:, mine] + pbuf[...]
    swap.wait_send()
    for c in started:
        c.wait_send()

    def relay_drain(i, carry):
        slot = dev(forward_order(i), -1)
        copy(vbuf.at[slot], vsend.at[11 + i], dev(0, 1), slot).wait_send()
        return carry

    lax.fori_loop(0, 4, relay_drain, 0)

    def drain(k, carry):
        s_copy(k, seg_peer(k), r).wait_send()
        return carry

    lax.fori_loop(1, 16, drain, 0)

    node_hist(hist_ref, parent_ref, small_ref, evict_ref, hist_ref, nodes)
    exchange(functools.partial(gain_terms, hist_ref, nodes), split_ref, best_ref, gbuf, mbuf, gsend, grecv, msend, mrecv, targets)


def pair_split(small_side, evicted, seg_c, v_loc, parent, nodes, targets):
    chips, width, half = seg_c.shape
    n_rows = 2 * chips
    n_outs = lax.axis_size("outs")
    vw, rows = v_loc.shape
    cols = width // 2 * BINS
    span = cols // 2
    out_rows = vw * nodes
    total = n_rows * rows
    vmem = pl.BlockSpec(memory_space=pltpu.VMEM)
    smem = pl.BlockSpec(memory_space=pltpu.SMEM)
    return pl.pallas_call(
        functools.partial(pair_split_kernel, nodes=nodes, targets=targets),
        out_shape=(
            jax.ShapeDtypeStruct((out_rows, span), jnp.float32),
            jax.ShapeDtypeStruct((nodes, span), jnp.float32),
            jax.ShapeDtypeStruct((nodes, 128), jnp.float32),
        ),
        in_specs=[smem, smem, vmem, vmem, vmem],
        out_specs=(vmem, vmem, vmem),
        scratch_shapes=[
            pltpu.VMEM((out_rows, cols), jnp.float32),
            pltpu.VMEM((n_rows, vw, rows), v_loc.dtype),
            pltpu.VMEM((n_rows, width, half), seg_c.dtype),
            pltpu.VMEM((out_rows, span), jnp.float32),
            pltpu.SemaphoreType.DMA((chips,)),
            pltpu.SemaphoreType.DMA((n_rows,)),
            pltpu.SemaphoreType.DMA((chips,)),
            pltpu.SemaphoreType.DMA((n_rows,)),
            pltpu.SemaphoreType.DMA(()),
            pltpu.SemaphoreType.DMA(()),
            pltpu.VMEM((n_outs, nodes, span), jnp.float32),
            pltpu.VMEM((n_rows, nodes, 128), jnp.float32),
            pltpu.SemaphoreType.DMA((2, n_outs)),
            pltpu.SemaphoreType.DMA((2, n_outs)),
            pltpu.SemaphoreType.DMA((n_rows,)),
            pltpu.SemaphoreType.DMA((n_rows,)),
        ],
        compiler_params=pltpu.CompilerParams(collective_id=2, has_side_effects=True),
        cost_estimate=pl.CostEstimate(
            flops=2 * out_rows * cols * total // 2,
            bytes_accessed=total * (vw * 2 + width) + out_rows * cols * 4,
            transcendentals=0,
        ),
    )(small_side, evicted, seg_c, v_loc, parent)


def local(codes, node_of_row, grad, hess, small_side, evicted, parent_hist):
    pairs = small_side.shape[0]
    nodes = 2 * pairs
    local_targets = grad.shape[1]
    targets = local_targets * lax.axis_size("outs")
    n_rows = lax.axis_size("rows")
    count, features = codes.shape
    feats = features // n_rows
    half = count // 2
    seg = (node_of_row[:, None] * BINS + codes).astype(jnp.int16)
    seg_p = jnp.transpose(seg.reshape(2, half, n_rows, feats), (2, 3, 0, 1)).reshape(n_rows, 2 * feats, half)
    v_loc = jnp.concatenate([grad.T, hess.T], axis=0)
    span = feats * BINS
    parent = parent_hist.reshape(2 * pairs * local_targets, span)
    if n_rows == 32:
        seg_t = (codes.T + node_of_row[None, :] * BINS).astype(jnp.int16)
        seg_c = seg_t.reshape(n_rows // 2, 2 * feats, 2, half).reshape(n_rows // 2, 4 * feats, half)
        hist, split_gain, best = pair_split(small_side, evicted, seg_c, v_loc, parent, nodes, targets)
    else:
        hist, split_gain, best = gather_hist(small_side, evicted, seg_p, v_loc, parent, nodes, targets)
    node_hist = hist.reshape(2, nodes, local_targets, span)
    return (node_hist, split_gain, best[:, 0])


def solution(mesh):
    return jax.shard_map(
        local,
        mesh=mesh,
        in_specs=(
            P("rows", None),
            P("rows"),
            P("rows", "outs"),
            P("rows", "outs"),
            P(),
            P(),
            P(None, None, "outs", "rows"),
        ),
        out_specs=(P(None, None, "outs", "rows"), P(None, "rows"), P()),
        check_vma=False,
    )
```

```python
import functools

import jax
import jax.numpy as jnp
import numpy as np
from jax import lax
from jax.experimental import pallas as pl
from jax.experimental.pallas import tpu as pltpu
from jax.sharding import PartitionSpec as P

BINS = 32


MESH_ID = pl.DeviceIdType.MESH


def row_stages(r, n_rows):
    chips = n_rows // 2
    nx = 4 if chips % 4 == 0 else chips
    ny = chips // nx
    chip = r // 2
    core = r % 2
    y = chip // nx
    x = chip % nx
    row = 2 * nx
    stages = [
        [y * row + (r - y * row + k) % row for k in range(1, row)],
        [(((y + k) % ny) * nx + x) * 2 + core for k in range(1, ny)],
    ]
    return [stage for stage in stages if stage]


def row_peers(r, n_rows):
    return [peer for stage in row_stages(r, n_rows) for peer in stage]


def exchange(part_fn, split_ref, best_ref, gbuf, mbuf, gsend, grecv, msend, mrecv, targets):
    n_rows = lax.axis_size("rows")
    n_outs = lax.axis_size("outs")
    r = lax.axis_index("rows")
    o = lax.axis_index("outs")
    nodes = gbuf.shape[1]
    halves = [(0, nodes // 2), (nodes // 2, nodes)]

    def part_copy(h, k, dst, slot):
        lo, hi = halves[h]
        return pltpu.make_async_remote_copy(
            src_ref=gbuf.at[o, pl.ds(lo, hi - lo)],
            dst_ref=gbuf.at[slot, pl.ds(lo, hi - lo)],
            send_sem=gsend.at[h, k],
            recv_sem=grecv.at[h, slot],
            device_id=(r, dst),
            device_id_type=MESH_ID,
        )

    sends = []
    for h, (lo, hi) in enumerate(halves):
        gbuf[o, lo:hi] = part_fn(lo, hi)
        for k in range(1, n_outs):
            copy = part_copy(h, k, (o + k) % n_outs, o)
            copy.start()
            sends.append(copy)
    for h in range(2):
        for k in range(1, n_outs):
            src = (o + n_outs - k) % n_outs
            part_copy(h, k, src, src).wait_recv()
    for copy in sends:
        copy.wait_send()
    acc = gbuf[0]
    for j in range(1, n_outs):
        acc = acc + gbuf[j]
    split = acc / targets
    split_ref[...] = split
    width = mbuf.shape[2]
    best = jnp.broadcast_to(jnp.max(split, axis=1, keepdims=True), (split.shape[0], width))
    base = 0
    for peers in row_stages(r, n_rows):
        mbuf[base] = best
        sends = []
        for j, peer in enumerate(peers):
            copy = pltpu.make_async_remote_copy(
                src_ref=mbuf.at[base],
                dst_ref=mbuf.at[base + 1 + j],
                send_sem=msend.at[base + 1 + j],
                recv_sem=mrecv.at[base + 1 + j],
                device_id=(peer, o),
                device_id_type=MESH_ID,
            )
            copy.start()
            sends.append(copy)
        for copy in sends:
            copy.wait_recv()
        for copy in sends:
            copy.wait_send()
        for j in range(len(peers)):
            best = jnp.maximum(best, mbuf[base + 1 + j])
        base += len(peers) + 1
    best_ref[...] = best


def block_hist(acc_ref, v, s, nodes):
    tl = v.shape[0] // 2
    half = s.shape[1]
    feats = s.shape[0] // 2
    one = jnp.ones((), jnp.bfloat16)
    zero = jnp.zeros((), jnp.bfloat16)
    bins = lax.broadcasted_iota(jnp.int32, (BINS, half), 0)
    for h in range(2):
        vh = v[:, h * half : (h + 1) * half]
        node = s[h : h + 1] >> 5
        onehot = jnp.concatenate(
            [jnp.where((s[2 * f + h : 2 * f + h + 1] & (BINS - 1)) == bins, one, zero) for f in range(feats)],
            axis=0,
        )
        blocks = []
        for c in range(2):
            vc = vh[c * tl : (c + 1) * tl]
            for n in range(nodes):
                blocks.append(jnp.where(node == n, vc, zero))
        vals = jnp.concatenate(blocks, axis=0)
        acc_ref[...] += lax.dot_general(
            vals, onehot, (((1,), (1,)), ((), ())), preferred_element_type=jnp.float32
        )


def relay_gather(acc_ref, seg_ref, v_ref, vbuf, sbuf, vsend, fsend, vrecv, s_copy, send_seg, nodes):
    n_rows = lax.axis_size("rows")
    r = lax.axis_index("rows")
    o = lax.axis_index("outs")
    core = r % 2
    chip = r // 2
    y = chip // 4
    x = chip % 4
    a = x + core * (y - x)
    b = y + core * (x - y)
    partner = chip * 2 + 1 - core

    def dev(da, db):
        ap = (a + da + 4) % 4
        bp = (b + db + 4) % 4
        return ((1 - core) * (bp * 4 + ap) + core * (ap * 4 + bp)) * 2 + core

    def copy(src, sem, peer, slot):
        return pltpu.make_async_remote_copy(
            src_ref=src, dst_ref=vbuf.at[slot], send_sem=sem, recv_sem=vrecv.at[slot],
            device_id=(peer, o), device_id_type=MESH_ID,
        )

    def arrive(slot):
        copy(vbuf.at[slot], vsend.at[0], partner, slot).wait_recv()
        s_copy(0, slot, slot).wait_recv()

    def compute(slot):
        block_hist(acc_ref, vbuf[slot], sbuf[slot].astype(jnp.int32), nodes)

    started = []

    def start(src, sem, peer, slot):
        c = copy(src, sem, peer, slot)
        c.start()
        started.append(c)

    start(v_ref, fsend.at[0], partner, r)
    for j, (da, db) in enumerate([(1, 0), (-1, 0), (0, 1), (0, -1)]):
        start(v_ref, vsend.at[j], dev(da, db), r)
    lax.fori_loop(1, n_rows, send_seg, 0)

    sem = 4
    for j, da in enumerate([-1, 1, -2]):
        slot = dev(da, 0)
        arrive(slot)
        if da == -1:
            start(vbuf.at[slot], vsend.at[sem], dev(1, 0), slot)
            sem += 1
        start(vbuf.at[slot], vsend.at[sem], dev(0, 1), slot)
        start(vbuf.at[slot], vsend.at[sem + 1], dev(0, -1), slot)
        sem += 2
        start(vbuf.at[slot], fsend.at[1 + j], partner, slot)
        compute(slot)

    def row_step(db, relay, first):
        def body(i, carry):
            slot = dev((i * 3) % 4, db)
            arrive(slot)
            if relay:
                copy(vbuf.at[slot], vsend.at[11 + i], dev(0, -db), slot).start()
            copy(vbuf.at[slot], fsend.at[first + i], partner, slot).start()
            compute(slot)
            return carry

        return body

    def row_drain(db, relay, first):
        def body(i, carry):
            slot = dev((i * 3) % 4, db)
            if relay:
                copy(vbuf.at[slot], vsend.at[11 + i], dev(0, -db), slot).wait_send()
            copy(vbuf.at[slot], fsend.at[first + i], partner, slot).wait_send()
            return carry

        return body

    rows_plan = [(-1, True, 4, 0, 2), (1, False, 8, 0, 2), (-1, False, 4, 2, 4), (1, True, 8, 2, 4), (2, False, 12, 0, 4)]
    for db, relay, first, lo, hi in rows_plan:
        lax.fori_loop(lo, hi, row_step(db, relay, first), 0)

    def take_partner(k, carry):
        slot = ((chip + 16 - k) % 16) * 2 + 1 - core
        arrive(slot)
        compute(slot)
        return carry

    lax.fori_loop(0, 16, take_partner, 0)
    for c in started:
        c.wait_send()
    for db, relay, first, lo, hi in rows_plan:
        lax.fori_loop(lo, hi, row_drain(db, relay, first), 0)


def gather_hist_kernel(
    small_ref, evict_ref, seg_ref, v_ref, parent_ref, hist_ref, split_ref, best_ref,
    acc_ref, vbuf, sbuf, vsend, fsend, vrecv, ssend, srecv, gbuf, mbuf, gsend, grecv, msend, mrecv,
    *, nodes, targets,
):
    n_rows = lax.axis_size("rows")
    chips = n_rows // 2
    r = lax.axis_index("rows")
    o = lax.axis_index("outs")
    core = r % 2
    chip = r // 2
    partner = chip * 2 + 1 - core
    barrier = pltpu.get_barrier_semaphore()

    def greet(k, carry):
        pl.semaphore_signal(barrier, 1, device_id=((r + k) % n_rows, o), device_id_type=MESH_ID)
        return carry

    lax.fori_loop(1, n_rows, greet, 0)
    n_outs = lax.axis_size("outs")
    for k in range(1, n_outs):
        pl.semaphore_signal(barrier, 1, device_id=(r, (o + k) % n_outs), device_id_type=MESH_ID)
    acc_ref[...] = jnp.zeros_like(acc_ref)
    block_hist(acc_ref, v_ref[...], seg_ref[r].astype(jnp.int32), nodes)
    pl.semaphore_wait(barrier, n_rows - 1 + n_outs - 1)

    def s_copy(k, peer, slot):
        return pltpu.make_async_remote_copy(
            src_ref=seg_ref.at[peer], dst_ref=sbuf.at[slot], send_sem=ssend.at[k], recv_sem=srecv.at[slot],
            device_id=(peer, o), device_id_type=MESH_ID,
        )

    def v_copy(k, peer, slot):
        return pltpu.make_async_remote_copy(
            src_ref=v_ref, dst_ref=vbuf.at[slot], send_sem=vsend.at[k], recv_sem=vrecv.at[slot],
            device_id=(peer, o), device_id_type=MESH_ID,
        )

    def f_copy(k, slot):
        return pltpu.make_async_remote_copy(
            src_ref=vbuf.at[slot], dst_ref=vbuf.at[slot], send_sem=fsend.at[k], recv_sem=vrecv.at[slot],
            device_id=(partner, o), device_id_type=MESH_ID,
        )

    def send_seg(k, carry):
        s_copy(k, (r + k) % n_rows, r).start()
        return carry

    def drain(k, carry):
        s_copy(k, (r + k) % n_rows, r).wait_send()
        return carry

    if chips == 16:
        relay_gather(acc_ref, seg_ref, v_ref, vbuf, sbuf, vsend, fsend, vrecv, s_copy, send_seg, nodes)
        lax.fori_loop(1, n_rows, drain, 0)
    else:
        own = pltpu.make_async_remote_copy(
            src_ref=v_ref, dst_ref=vbuf.at[r], send_sem=fsend.at[0], recv_sem=vrecv.at[r],
            device_id=(partner, o), device_id_type=MESH_ID,
        )
        own.start()

        def send(k, carry):
            v_copy(k, ((chip + k) % chips) * 2 + core, r).start()
            return carry

        lax.fori_loop(1, chips, send, 0)

        lax.fori_loop(1, n_rows, send_seg, 0)

        def take_direct(k, carry):
            src = ((chip + chips - k) % chips) * 2 + core
            v_copy(k, src, src).wait_recv()
            f_copy(k, src).start()
            s_copy(k, src, src).wait_recv()
            block_hist(acc_ref, vbuf[src], sbuf[src].astype(jnp.int32), nodes)
            return carry

        lax.fori_loop(1, chips, take_direct, 0)

        def take_forwarded(k, carry):
            src = ((chip + chips - k) % chips) * 2 + 1 - core
            f_copy(k, src).wait_recv()
            s_copy(k, src, src).wait_recv()
            block_hist(acc_ref, vbuf[src], sbuf[src].astype(jnp.int32), nodes)
            return carry

        lax.fori_loop(0, chips, take_forwarded, 0)

        lax.fori_loop(1, n_rows, drain, 0)

        def drain_v(k, carry):
            v_copy(k, ((chip + k) % chips) * 2 + core, r).wait_send()
            return carry

        lax.fori_loop(1, chips, drain_v, 0)
        own.wait_send()

        def drain_f(k, carry):
            f_copy(k, ((chip + chips - k) % chips) * 2 + core).wait_send()
            return carry

        lax.fori_loop(1, chips, drain_f, 0)


    node_hist(acc_ref, parent_ref, small_ref, evict_ref, hist_ref, nodes)
    exchange(functools.partial(gain_terms, hist_ref, nodes), split_ref, best_ref, gbuf, mbuf, gsend, grecv, msend, mrecv, targets)


def node_hist(acc_ref, parent_ref, small_ref, evict_ref, hist_ref, nodes):
    pairs = nodes // 2
    tl = acc_ref.shape[0] // (2 * nodes)
    for c in range(2):
        for p in range(pairs):
            lo = c * nodes * tl + 2 * p * tl
            a = acc_ref[lo : lo + tl]
            b = acc_ref[lo + tl : lo + 2 * tl]
            base = (c * pairs + p) * tl
            parent = parent_ref[base : base + tl]
            small = small_ref[p] == 0
            gone = evict_ref[p] == 1
            child = jnp.where(small, a, b)
            rebuilt = jnp.where(small, b, a)
            sibling = jnp.where(gone, rebuilt, parent - child)
            hist_ref[lo : lo + tl] = jnp.where(small, child, sibling)
            hist_ref[lo + tl : lo + 2 * tl] = jnp.where(small, sibling, child)


def group_scan(x, reverse):
    span = x.shape[1]
    lane = lax.broadcasted_iota(jnp.int32, x.shape, 1) % BINS
    shift = 1
    while shift < BINS:
        if reverse:
            moved = pltpu.roll(x, span - shift, 1)
            x = x + jnp.where(lane + shift < BINS, moved, 0.0)
        else:
            moved = pltpu.roll(x, shift, 1)
            x = x + jnp.where(lane >= shift, moved, 0.0)
        shift *= 2
    return x


def gain_terms(hist_ref, nodes, lo, hi):
    rows, span = hist_ref.shape
    half = rows // 2
    tl = half // nodes
    count = (hi - lo) * tl
    lane = lax.broadcasted_iota(jnp.int32, (count, span), 1) % BINS
    left_g = group_scan(hist_ref[lo * tl : hi * tl], False)
    left_h = group_scan(hist_ref[half + lo * tl : half + hi * tl], False)
    total_g = group_scan(jnp.where(lane == BINS - 1, left_g, 0.0), True)
    total_h = group_scan(jnp.where(lane == BINS - 1, left_h, 0.0), True)

    def score(a, s):
        return a * a / (jnp.maximum(s, 0.0) + 1.0)

    gain = (
        score(left_g, left_h) + score(total_g - left_g, total_h - left_h) - score(total_g, total_h)
    )
    return jnp.sum(gain.reshape(hi - lo, tl, span), axis=1)


def gather_hist(small_side, evicted, seg_p, v_loc, parent, nodes, targets):
    n_rows, width, half = seg_p.shape
    n_outs = lax.axis_size("outs")
    vw, rows = v_loc.shape
    feats = width // 2
    out_rows = vw * nodes
    cols = feats * BINS
    total = n_rows * rows
    vmem = pl.BlockSpec(memory_space=pltpu.VMEM)
    smem = pl.BlockSpec(memory_space=pltpu.SMEM)
    return pl.pallas_call(
        functools.partial(gather_hist_kernel, nodes=nodes, targets=targets),
        out_shape=(
            jax.ShapeDtypeStruct((out_rows, cols), jnp.float32),
            jax.ShapeDtypeStruct((nodes, cols), jnp.float32),
            jax.ShapeDtypeStruct((nodes, 128), jnp.float32),
        ),
        in_specs=[smem, smem, vmem, vmem, vmem],
        out_specs=(vmem, vmem, vmem),
        scratch_shapes=[
            pltpu.VMEM((out_rows, cols), jnp.float32),
            pltpu.VMEM((n_rows, vw, rows), v_loc.dtype),
            pltpu.VMEM((n_rows, width, half), seg_p.dtype),
            pltpu.SemaphoreType.DMA((n_rows // 2,)),
            pltpu.SemaphoreType.DMA((n_rows // 2,)),
            pltpu.SemaphoreType.DMA((n_rows,)),
            pltpu.SemaphoreType.DMA((n_rows,)),
            pltpu.SemaphoreType.DMA((n_rows,)),
            pltpu.VMEM((n_outs, nodes, cols), jnp.float32),
            pltpu.VMEM((n_rows, nodes, 128), jnp.float32),
            pltpu.SemaphoreType.DMA((2, n_outs)),
            pltpu.SemaphoreType.DMA((2, n_outs)),
            pltpu.SemaphoreType.DMA((n_rows,)),
            pltpu.SemaphoreType.DMA((n_rows,)),
        ],
        compiler_params=pltpu.CompilerParams(collective_id=1, has_side_effects=True),
        cost_estimate=pl.CostEstimate(
            flops=2 * out_rows * cols * total,
            bytes_accessed=total * (vw * 2 + feats * 2) + out_rows * cols * 4,
            transcendentals=0,
        ),
    )(small_side, evicted, seg_p, v_loc, parent)


def forward_order(i):
    return (3 * i + (i // 2) * (2 * i - 1)) % 4


def pair_split_kernel(
    small_ref, evict_ref, seg_ref, v_ref, parent_ref, hist_ref, split_ref, best_ref,
    acc_ref, vbuf, sbuf, pbuf, vsend, vrecv, ssend, srecv, psend, precv, gbuf, mbuf, gsend, grecv, msend, mrecv,
    *, nodes, targets,
):
    n_rows = lax.axis_size("rows")
    n_outs = lax.axis_size("outs")
    r = lax.axis_index("rows")
    o = lax.axis_index("outs")
    core = r % 2
    chip = r // 2
    y = chip // 4
    x = chip % 4
    a = x + core * (y - x)
    b = y + core * (x - y)
    partner = chip * 2 + 1 - core
    barrier = pltpu.get_barrier_semaphore()

    def greet(k, carry):
        pl.semaphore_signal(barrier, 1, device_id=((r + k) % n_rows, o), device_id_type=MESH_ID)
        return carry

    lax.fori_loop(1, n_rows, greet, 0)
    for k in range(1, n_outs):
        pl.semaphore_signal(barrier, 1, device_id=(r, (o + k) % n_outs), device_id_type=MESH_ID)
    acc_ref[...] = jnp.zeros_like(acc_ref)
    block_hist(acc_ref, v_ref[...], seg_ref[chip].astype(jnp.int32), nodes)
    pl.semaphore_wait(barrier, n_rows - 1 + n_outs - 1)

    def dev(da, db):
        ap = (a + da + 4) % 4
        bp = (b + db + 4) % 4
        return ((1 - core) * (bp * 4 + ap) + core * (ap * 4 + bp)) * 2 + core

    def copy(src, sem, peer, slot):
        return pltpu.make_async_remote_copy(
            src_ref=src, dst_ref=vbuf.at[slot], send_sem=sem, recv_sem=vrecv.at[slot],
            device_id=(peer, o), device_id_type=MESH_ID,
        )

    def s_copy(k, peer, slot):
        return pltpu.make_async_remote_copy(
            src_ref=seg_ref.at[peer // 2], dst_ref=sbuf.at[slot], send_sem=ssend.at[k], recv_sem=srecv.at[slot],
            device_id=(peer, o), device_id_type=MESH_ID,
        )

    def seg_peer(k):
        return ((chip + k) % 16) * 2 + core

    def arrive(slot):
        copy(vbuf.at[slot], vsend.at[0], partner, slot).wait_recv()
        s_copy(0, slot, slot).wait_recv()

    def compute(slot):
        block_hist(acc_ref, vbuf[slot], sbuf[slot].astype(jnp.int32), nodes)

    started = []

    def start(src, sem, peer, slot):
        c = copy(src, sem, peer, slot)
        c.start()
        started.append(c)

    for j, (da, db) in enumerate([(1, 0), (-1, 0), (0, 1), (0, -1)]):
        start(v_ref, vsend.at[j], dev(da, db), r)

    def send_seg(k, carry):
        s_copy(k, seg_peer(k), r).start()
        return carry

    lax.fori_loop(1, 16, send_seg, 0)

    def row_step(db, relay):
        def body(i, carry):
            slot = dev(forward_order(i), db)
            arrive(slot)
            if relay:
                copy(vbuf.at[slot], vsend.at[11 + i], dev(0, 1), slot).start()
            compute(slot)
            return carry

        return body

    sem = 4
    for da in [-1, 1, None, -2]:
        if da is None:
            for db, relay in [(-1, True), (1, False)]:
                lax.fori_loop(0, 1, row_step(db, relay), 0)
            continue
        slot = dev(da, 0)
        arrive(slot)
        if da == -1:
            start(vbuf.at[slot], vsend.at[sem], dev(1, 0), slot)
            sem += 1
        start(vbuf.at[slot], vsend.at[sem], dev(0, 1), slot)
        start(vbuf.at[slot], vsend.at[sem + 1], dev(0, -1), slot)
        sem += 2
        compute(slot)
    below = row_step(-1, True)
    above = row_step(1, False)

    beyond = row_step(-2, False)

    def both_rows(i, carry):
        return beyond(i - 1, above(i, below(i, carry)))

    lax.fori_loop(1, 4, both_rows, 0)
    lax.fori_loop(3, 4, beyond, 0)

    span = hist_ref.shape[1]
    mine = pl.ds(pl.multiple_of(core * span, span), span)
    theirs = pl.ds(pl.multiple_of((1 - core) * span, span), span)
    swap = pltpu.make_async_remote_copy(
        src_ref=acc_ref.at[:, theirs], dst_ref=pbuf, send_sem=psend, recv_sem=precv,
        device_id=(partner, o), device_id_type=MESH_ID,
    )
    swap.start()
    swap.wait_recv()
    hist_ref[...] = acc_ref[:, mine] + pbuf[...]
    swap.wait_send()
    for c in started:
        c.wait_send()

    def relay_drain(i, carry):
        slot = dev(forward_order(i), -1)
        copy(vbuf.at[slot], vsend.at[11 + i], dev(0, 1), slot).wait_send()
        return carry

    lax.fori_loop(0, 4, relay_drain, 0)

    def drain(k, carry):
        s_copy(k, seg_peer(k), r).wait_send()
        return carry

    lax.fori_loop(1, 16, drain, 0)

    node_hist(hist_ref, parent_ref, small_ref, evict_ref, hist_ref, nodes)
    exchange(functools.partial(gain_terms, hist_ref, nodes), split_ref, best_ref, gbuf, mbuf, gsend, grecv, msend, mrecv, targets)


def pair_split(small_side, evicted, seg_c, v_loc, parent, nodes, targets):
    chips, width, half = seg_c.shape
    n_rows = 2 * chips
    n_outs = lax.axis_size("outs")
    vw, rows = v_loc.shape
    cols = width // 2 * BINS
    span = cols // 2
    out_rows = vw * nodes
    total = n_rows * rows
    vmem = pl.BlockSpec(memory_space=pltpu.VMEM)
    smem = pl.BlockSpec(memory_space=pltpu.SMEM)
    return pl.pallas_call(
        functools.partial(pair_split_kernel, nodes=nodes, targets=targets),
        out_shape=(
            jax.ShapeDtypeStruct((out_rows, span), jnp.float32),
            jax.ShapeDtypeStruct((nodes, span), jnp.float32),
            jax.ShapeDtypeStruct((nodes, 128), jnp.float32),
        ),
        in_specs=[smem, smem, vmem, vmem, vmem],
        out_specs=(vmem, vmem, vmem),
        scratch_shapes=[
            pltpu.VMEM((out_rows, cols), jnp.float32),
            pltpu.VMEM((n_rows, vw, rows), v_loc.dtype),
            pltpu.VMEM((n_rows, width, half), seg_c.dtype),
            pltpu.VMEM((out_rows, span), jnp.float32),
            pltpu.SemaphoreType.DMA((chips,)),
            pltpu.SemaphoreType.DMA((n_rows,)),
            pltpu.SemaphoreType.DMA((chips,)),
            pltpu.SemaphoreType.DMA((n_rows,)),
            pltpu.SemaphoreType.DMA(()),
            pltpu.SemaphoreType.DMA(()),
            pltpu.VMEM((n_outs, nodes, span), jnp.float32),
            pltpu.VMEM((n_rows, nodes, 128), jnp.float32),
            pltpu.SemaphoreType.DMA((2, n_outs)),
            pltpu.SemaphoreType.DMA((2, n_outs)),
            pltpu.SemaphoreType.DMA((n_rows,)),
            pltpu.SemaphoreType.DMA((n_rows,)),
        ],
        compiler_params=pltpu.CompilerParams(collective_id=2, has_side_effects=True),
        cost_estimate=pl.CostEstimate(
            flops=2 * out_rows * cols * total // 2,
            bytes_accessed=total * (vw * 2 + width) + out_rows * cols * 4,
            transcendentals=0,
        ),
    )(small_side, evicted, seg_c, v_loc, parent)


def local(codes, node_of_row, grad, hess, small_side, evicted, parent_hist):
    pairs = small_side.shape[0]
    nodes = 2 * pairs
    local_targets = grad.shape[1]
    targets = local_targets * lax.axis_size("outs")
    n_rows = lax.axis_size("rows")
    count, features = codes.shape
    feats = features // n_rows
    half = count // 2
    seg = (node_of_row[:, None] * BINS + codes).astype(jnp.int16)
    seg_p = jnp.transpose(seg.reshape(2, half, n_rows, feats), (2, 3, 0, 1)).reshape(n_rows, 2 * feats, half)
    v_loc = jnp.concatenate([grad.T, hess.T], axis=0)
    span = feats * BINS
    parent = parent_hist.reshape(2 * pairs * local_targets, span)
    if n_rows == 32:
        seg_t = (codes.T + node_of_row[None, :] * BINS).astype(jnp.int16)
        seg_c = seg_t.reshape(n_rows // 2, 2 * feats, 2, half).reshape(n_rows // 2, 4 * feats, half)
        hist, split_gain, best = pair_split(small_side, evicted, seg_c, v_loc, parent, nodes, targets)
    else:
        hist, split_gain, best = gather_hist(small_side, evicted, seg_p, v_loc, parent, nodes, targets)
    node_hist = hist.reshape(2, nodes, local_targets, span)
    return (node_hist, split_gain, best[:, 0])


def solution(mesh):
    return jax.shard_map(
        local,
        mesh=mesh,
        in_specs=(
            P("rows", None),
            P("rows"),
            P("rows", "outs"),
            P("rows", "outs"),
            P(),
            P(),
            P(None, None, "outs", "rows"),
        ),
        out_specs=(P(None, None, "outs", "rows"), P(None, "rows"), P()),
        check_vma=False,
    )
```

```python
import functools

import jax
import jax.numpy as jnp
import numpy as np
from jax import lax
from jax.experimental import pallas as pl
from jax.experimental.pallas import tpu as pltpu
from jax.sharding import PartitionSpec as P

BINS = 32


MESH_ID = pl.DeviceIdType.MESH


def row_stages(r, n_rows):
    chips = n_rows // 2
    nx = 4 if chips % 4 == 0 else chips
    ny = chips // nx
    chip = r // 2
    core = r % 2
    y = chip // nx
    x = chip % nx
    row = 2 * nx
    stages = [
        [y * row + (r - y * row + k) % row for k in range(1, row)],
        [(((y + k) % ny) * nx + x) * 2 + core for k in range(1, ny)],
    ]
    return [stage for stage in stages if stage]


def row_peers(r, n_rows):
    return [peer for stage in row_stages(r, n_rows) for peer in stage]


def exchange(part_fn, split_ref, best_ref, gbuf, mbuf, gsend, grecv, msend, mrecv, targets):
    n_rows = lax.axis_size("rows")
    n_outs = lax.axis_size("outs")
    r = lax.axis_index("rows")
    o = lax.axis_index("outs")
    nodes = gbuf.shape[1]
    halves = [(0, nodes // 2), (nodes // 2, nodes)]

    def part_copy(h, k, dst, slot):
        lo, hi = halves[h]
        return pltpu.make_async_remote_copy(
            src_ref=gbuf.at[o, pl.ds(lo, hi - lo)],
            dst_ref=gbuf.at[slot, pl.ds(lo, hi - lo)],
            send_sem=gsend.at[h, k],
            recv_sem=grecv.at[h, slot],
            device_id=(r, dst),
            device_id_type=MESH_ID,
        )

    sends = []
    for h, (lo, hi) in enumerate(halves):
        gbuf[o, lo:hi] = part_fn(lo, hi)
        for k in range(1, n_outs):
            copy = part_copy(h, k, (o + k) % n_outs, o)
            copy.start()
            sends.append(copy)
    for h in range(2):
        for k in range(1, n_outs):
            src = (o + n_outs - k) % n_outs
            part_copy(h, k, src, src).wait_recv()
    for copy in sends:
        copy.wait_send()
    acc = gbuf[0]
    for j in range(1, n_outs):
        acc = acc + gbuf[j]
    split = acc / targets
    split_ref[...] = split
    width = mbuf.shape[2]
    best = jnp.broadcast_to(jnp.max(split, axis=1, keepdims=True), (split.shape[0], width))
    base = 0
    for peers in row_stages(r, n_rows):
        mbuf[base] = best
        sends = []
        for j, peer in enumerate(peers):
            copy = pltpu.make_async_remote_copy(
                src_ref=mbuf.at[base],
                dst_ref=mbuf.at[base + 1 + j],
                send_sem=msend.at[base + 1 + j],
                recv_sem=mrecv.at[base + 1 + j],
                device_id=(peer, o),
                device_id_type=MESH_ID,
            )
            copy.start()
            sends.append(copy)
        for copy in sends:
            copy.wait_recv()
        for copy in sends:
            copy.wait_send()
        for j in range(len(peers)):
            best = jnp.maximum(best, mbuf[base + 1 + j])
        base += len(peers) + 1
    best_ref[...] = best


def block_hist(acc_ref, v, s, nodes):
    tl = v.shape[0] // 2
    half = s.shape[1]
    feats = s.shape[0] // 2
    one = jnp.ones((), jnp.bfloat16)
    zero = jnp.zeros((), jnp.bfloat16)
    bins = lax.broadcasted_iota(jnp.int32, (BINS, half), 0)
    for h in range(2):
        vh = v[:, h * half : (h + 1) * half]
        node = s[h : h + 1] >> 5
        onehot = jnp.concatenate(
            [jnp.where((s[2 * f + h : 2 * f + h + 1] & (BINS - 1)) == bins, one, zero) for f in range(feats)],
            axis=0,
        )
        blocks = []
        for c in range(2):
            vc = vh[c * tl : (c + 1) * tl]
            for n in range(nodes):
                blocks.append(jnp.where(node == n, vc, zero))
        vals = jnp.concatenate(blocks, axis=0)
        acc_ref[...] += lax.dot_general(
            vals, onehot, (((1,), (1,)), ((), ())), preferred_element_type=jnp.float32
        )


def relay_gather(acc_ref, seg_ref, v_ref, vbuf, sbuf, vsend, fsend, vrecv, s_copy, send_seg, nodes):
    n_rows = lax.axis_size("rows")
    r = lax.axis_index("rows")
    o = lax.axis_index("outs")
    core = r % 2
    chip = r // 2
    y = chip // 4
    x = chip % 4
    a = x + core * (y - x)
    b = y + core * (x - y)
    partner = chip * 2 + 1 - core

    def dev(da, db):
        ap = (a + da + 4) % 4
        bp = (b + db + 4) % 4
        return ((1 - core) * (bp * 4 + ap) + core * (ap * 4 + bp)) * 2 + core

    def copy(src, sem, peer, slot):
        return pltpu.make_async_remote_copy(
            src_ref=src, dst_ref=vbuf.at[slot], send_sem=sem, recv_sem=vrecv.at[slot],
            device_id=(peer, o), device_id_type=MESH_ID,
        )

    def arrive(slot):
        copy(vbuf.at[slot], vsend.at[0], partner, slot).wait_recv()
        s_copy(0, slot, slot).wait_recv()

    def compute(slot):
        block_hist(acc_ref, vbuf[slot], sbuf[slot].astype(jnp.int32), nodes)

    started = []

    def start(src, sem, peer, slot):
        c = copy(src, sem, peer, slot)
        c.start()
        started.append(c)

    start(v_ref, fsend.at[0], partner, r)
    for j, (da, db) in enumerate([(1, 0), (-1, 0), (0, 1), (0, -1)]):
        start(v_ref, vsend.at[j], dev(da, db), r)
    lax.fori_loop(1, n_rows, send_seg, 0)

    sem = 4
    for j, da in enumerate([-1, 1, -2]):
        slot = dev(da, 0)
        arrive(slot)
        if da == -1:
            start(vbuf.at[slot], vsend.at[sem], dev(1, 0), slot)
            sem += 1
        start(vbuf.at[slot], vsend.at[sem], dev(0, 1), slot)
        start(vbuf.at[slot], vsend.at[sem + 1], dev(0, -1), slot)
        sem += 2
        start(vbuf.at[slot], fsend.at[1 + j], partner, slot)
        compute(slot)

    def row_step(db, relay, first):
        def body(i, carry):
            slot = dev((i * 3) % 4, db)
            arrive(slot)
            if relay:
                copy(vbuf.at[slot], vsend.at[11 + i], dev(0, -db), slot).start()
            copy(vbuf.at[slot], fsend.at[first + i], partner, slot).start()
            compute(slot)
            return carry

        return body

    def row_drain(db, relay, first):
        def body(i, carry):
            slot = dev((i * 3) % 4, db)
            if relay:
                copy(vbuf.at[slot], vsend.at[11 + i], dev(0, -db), slot).wait_send()
            copy(vbuf.at[slot], fsend.at[first + i], partner, slot).wait_send()
            return carry

        return body

    rows_plan = [(-1, True, 4, 0, 2), (1, False, 8, 0, 2), (-1, False, 4, 2, 4), (1, True, 8, 2, 4), (2, False, 12, 0, 4)]
    for db, relay, first, lo, hi in rows_plan:
        lax.fori_loop(lo, hi, row_step(db, relay, first), 0)

    def take_partner(k, carry):
        slot = ((chip + 16 - k) % 16) * 2 + 1 - core
        arrive(slot)
        compute(slot)
        return carry

    lax.fori_loop(0, 16, take_partner, 0)
    for c in started:
        c.wait_send()
    for db, relay, first, lo, hi in rows_plan:
        lax.fori_loop(lo, hi, row_drain(db, relay, first), 0)


def gather_hist_kernel(
    small_ref, evict_ref, seg_ref, v_ref, parent_ref, hist_ref, split_ref, best_ref,
    acc_ref, vbuf, sbuf, vsend, fsend, vrecv, ssend, srecv, gbuf, mbuf, gsend, grecv, msend, mrecv,
    *, nodes, targets,
):
    n_rows = lax.axis_size("rows")
    chips = n_rows // 2
    r = lax.axis_index("rows")
    o = lax.axis_index("outs")
    core = r % 2
    chip = r // 2
    partner = chip * 2 + 1 - core
    barrier = pltpu.get_barrier_semaphore()

    def greet(k, carry):
        pl.semaphore_signal(barrier, 1, device_id=((r + k) % n_rows, o), device_id_type=MESH_ID)
        return carry

    lax.fori_loop(1, n_rows, greet, 0)
    n_outs = lax.axis_size("outs")
    for k in range(1, n_outs):
        pl.semaphore_signal(barrier, 1, device_id=(r, (o + k) % n_outs), device_id_type=MESH_ID)
    acc_ref[...] = jnp.zeros_like(acc_ref)
    block_hist(acc_ref, v_ref[...], seg_ref[r].astype(jnp.int32), nodes)
    pl.semaphore_wait(barrier, n_rows - 1 + n_outs - 1)

    def s_copy(k, peer, slot):
        return pltpu.make_async_remote_copy(
            src_ref=seg_ref.at[peer], dst_ref=sbuf.at[slot], send_sem=ssend.at[k], recv_sem=srecv.at[slot],
            device_id=(peer, o), device_id_type=MESH_ID,
        )

    def v_copy(k, peer, slot):
        return pltpu.make_async_remote_copy(
            src_ref=v_ref, dst_ref=vbuf.at[slot], send_sem=vsend.at[k], recv_sem=vrecv.at[slot],
            device_id=(peer, o), device_id_type=MESH_ID,
        )

    def f_copy(k, slot):
        return pltpu.make_async_remote_copy(
            src_ref=vbuf.at[slot], dst_ref=vbuf.at[slot], send_sem=fsend.at[k], recv_sem=vrecv.at[slot],
            device_id=(partner, o), device_id_type=MESH_ID,
        )

    def send_seg(k, carry):
        s_copy(k, (r + k) % n_rows, r).start()
        return carry

    def drain(k, carry):
        s_copy(k, (r + k) % n_rows, r).wait_send()
        return carry

    if chips == 16:
        relay_gather(acc_ref, seg_ref, v_ref, vbuf, sbuf, vsend, fsend, vrecv, s_copy, send_seg, nodes)
        lax.fori_loop(1, n_rows, drain, 0)
    else:
        own = pltpu.make_async_remote_copy(
            src_ref=v_ref, dst_ref=vbuf.at[r], send_sem=fsend.at[0], recv_sem=vrecv.at[r],
            device_id=(partner, o), device_id_type=MESH_ID,
        )
        own.start()

        def send(k, carry):
            v_copy(k, ((chip + k) % chips) * 2 + core, r).start()
            return carry

        lax.fori_loop(1, chips, send, 0)

        lax.fori_loop(1, n_rows, send_seg, 0)

        def take_direct(k, carry):
            src = ((chip + chips - k) % chips) * 2 + core
            v_copy(k, src, src).wait_recv()
            f_copy(k, src).start()
            s_copy(k, src, src).wait_recv()
            block_hist(acc_ref, vbuf[src], sbuf[src].astype(jnp.int32), nodes)
            return carry

        lax.fori_loop(1, chips, take_direct, 0)

        def take_forwarded(k, carry):
            src = ((chip + chips - k) % chips) * 2 + 1 - core
            f_copy(k, src).wait_recv()
            s_copy(k, src, src).wait_recv()
            block_hist(acc_ref, vbuf[src], sbuf[src].astype(jnp.int32), nodes)
            return carry

        lax.fori_loop(0, chips, take_forwarded, 0)

        lax.fori_loop(1, n_rows, drain, 0)

        def drain_v(k, carry):
            v_copy(k, ((chip + k) % chips) * 2 + core, r).wait_send()
            return carry

        lax.fori_loop(1, chips, drain_v, 0)
        own.wait_send()

        def drain_f(k, carry):
            f_copy(k, ((chip + chips - k) % chips) * 2 + core).wait_send()
            return carry

        lax.fori_loop(1, chips, drain_f, 0)


    node_hist(acc_ref, parent_ref, small_ref, evict_ref, hist_ref, nodes)
    exchange(functools.partial(gain_terms, hist_ref, nodes), split_ref, best_ref, gbuf, mbuf, gsend, grecv, msend, mrecv, targets)


def node_hist(acc_ref, parent_ref, small_ref, evict_ref, hist_ref, nodes):
    pairs = nodes // 2
    tl = acc_ref.shape[0] // (2 * nodes)
    for c in range(2):
        for p in range(pairs):
            lo = c * nodes * tl + 2 * p * tl
            a = acc_ref[lo : lo + tl]
            b = acc_ref[lo + tl : lo + 2 * tl]
            base = (c * pairs + p) * tl
            parent = parent_ref[base : base + tl]
            small = small_ref[p] == 0
            gone = evict_ref[p] == 1
            child = jnp.where(small, a, b)
            rebuilt = jnp.where(small, b, a)
            sibling = jnp.where(gone, rebuilt, parent - child)
            hist_ref[lo : lo + tl] = jnp.where(small, child, sibling)
            hist_ref[lo + tl : lo + 2 * tl] = jnp.where(small, sibling, child)


def group_scan(x, reverse):
    span = x.shape[1]
    lane = lax.broadcasted_iota(jnp.int32, x.shape, 1) % BINS
    shift = 1
    while shift < BINS:
        if reverse:
            moved = pltpu.roll(x, span - shift, 1)
            x = x + jnp.where(lane + shift < BINS, moved, 0.0)
        else:
            moved = pltpu.roll(x, shift, 1)
            x = x + jnp.where(lane >= shift, moved, 0.0)
        shift *= 2
    return x


def gain_terms(hist_ref, nodes, lo, hi):
    rows, span = hist_ref.shape
    half = rows // 2
    tl = half // nodes
    count = (hi - lo) * tl
    lane = lax.broadcasted_iota(jnp.int32, (count, span), 1) % BINS
    left_g = group_scan(hist_ref[lo * tl : hi * tl], False)
    left_h = group_scan(hist_ref[half + lo * tl : half + hi * tl], False)
    total_g = group_scan(jnp.where(lane == BINS - 1, left_g, 0.0), True)
    total_h = group_scan(jnp.where(lane == BINS - 1, left_h, 0.0), True)

    def score(a, s):
        return a * a / (jnp.maximum(s, 0.0) + 1.0)

    gain = (
        score(left_g, left_h) + score(total_g - left_g, total_h - left_h) - score(total_g, total_h)
    )
    return jnp.sum(gain.reshape(hi - lo, tl, span), axis=1)


def gather_hist(small_side, evicted, seg_p, v_loc, parent, nodes, targets):
    n_rows, width, half = seg_p.shape
    n_outs = lax.axis_size("outs")
    vw, rows = v_loc.shape
    feats = width // 2
    out_rows = vw * nodes
    cols = feats * BINS
    total = n_rows * rows
    vmem = pl.BlockSpec(memory_space=pltpu.VMEM)
    smem = pl.BlockSpec(memory_space=pltpu.SMEM)
    return pl.pallas_call(
        functools.partial(gather_hist_kernel, nodes=nodes, targets=targets),
        out_shape=(
            jax.ShapeDtypeStruct((out_rows, cols), jnp.float32),
            jax.ShapeDtypeStruct((nodes, cols), jnp.float32),
            jax.ShapeDtypeStruct((nodes, 128), jnp.float32),
        ),
        in_specs=[smem, smem, vmem, vmem, vmem],
        out_specs=(vmem, vmem, vmem),
        scratch_shapes=[
            pltpu.VMEM((out_rows, cols), jnp.float32),
            pltpu.VMEM((n_rows, vw, rows), v_loc.dtype),
            pltpu.VMEM((n_rows, width, half), seg_p.dtype),
            pltpu.SemaphoreType.DMA((n_rows // 2,)),
            pltpu.SemaphoreType.DMA((n_rows // 2,)),
            pltpu.SemaphoreType.DMA((n_rows,)),
            pltpu.SemaphoreType.DMA((n_rows,)),
            pltpu.SemaphoreType.DMA((n_rows,)),
            pltpu.VMEM((n_outs, nodes, cols), jnp.float32),
            pltpu.VMEM((n_rows, nodes, 128), jnp.float32),
            pltpu.SemaphoreType.DMA((2, n_outs)),
            pltpu.SemaphoreType.DMA((2, n_outs)),
            pltpu.SemaphoreType.DMA((n_rows,)),
            pltpu.SemaphoreType.DMA((n_rows,)),
        ],
        compiler_params=pltpu.CompilerParams(collective_id=1, has_side_effects=True),
        cost_estimate=pl.CostEstimate(
            flops=2 * out_rows * cols * total,
            bytes_accessed=total * (vw * 2 + feats * 2) + out_rows * cols * 4,
            transcendentals=0,
        ),
    )(small_side, evicted, seg_p, v_loc, parent)


def forward_order(i):
    return (3 * i + (i // 2) * (2 * i - 1)) % 4


def pair_split_kernel(
    small_ref, evict_ref, seg_ref, v_ref, parent_ref, hist_ref, split_ref, best_ref,
    acc_ref, vbuf, sbuf, pbuf, vsend, vrecv, ssend, srecv, psend, precv, gbuf, mbuf, gsend, grecv, msend, mrecv,
    *, nodes, targets,
):
    n_rows = lax.axis_size("rows")
    n_outs = lax.axis_size("outs")
    r = lax.axis_index("rows")
    o = lax.axis_index("outs")
    core = r % 2
    chip = r // 2
    y = chip // 4
    x = chip % 4
    a = x + core * (y - x)
    b = y + core * (x - y)
    partner = chip * 2 + 1 - core
    barrier = pltpu.get_barrier_semaphore()

    def greet(k, carry):
        pl.semaphore_signal(barrier, 1, device_id=((r + k) % n_rows, o), device_id_type=MESH_ID)
        return carry

    lax.fori_loop(1, n_rows, greet, 0)
    for k in range(1, n_outs):
        pl.semaphore_signal(barrier, 1, device_id=(r, (o + k) % n_outs), device_id_type=MESH_ID)
    acc_ref[...] = jnp.zeros_like(acc_ref)
    block_hist(acc_ref, v_ref[...], seg_ref[chip].astype(jnp.int32), nodes)
    pl.semaphore_wait(barrier, n_rows - 1 + n_outs - 1)

    def dev(da, db):
        ap = (a + da + 4) % 4
        bp = (b + db + 4) % 4
        return ((1 - core) * (bp * 4 + ap) + core * (ap * 4 + bp)) * 2 + core

    def copy(src, sem, peer, slot):
        return pltpu.make_async_remote_copy(
            src_ref=src, dst_ref=vbuf.at[slot], send_sem=sem, recv_sem=vrecv.at[slot],
            device_id=(peer, o), device_id_type=MESH_ID,
        )

    def s_copy(k, peer, slot):
        return pltpu.make_async_remote_copy(
            src_ref=seg_ref.at[peer // 2], dst_ref=sbuf.at[slot], send_sem=ssend.at[k], recv_sem=srecv.at[slot],
            device_id=(peer, o), device_id_type=MESH_ID,
        )

    def seg_peer(k):
        return ((chip + k) % 16) * 2 + core

    def arrive(slot):
        copy(vbuf.at[slot], vsend.at[0], partner, slot).wait_recv()
        s_copy(0, slot, slot).wait_recv()

    def compute(slot):
        block_hist(acc_ref, vbuf[slot], sbuf[slot].astype(jnp.int32), nodes)

    started = []

    def start(src, sem, peer, slot):
        c = copy(src, sem, peer, slot)
        c.start()
        started.append(c)

    for j, (da, db) in enumerate([(1, 0), (-1, 0), (0, 1), (0, -1)]):
        start(v_ref, vsend.at[j], dev(da, db), r)

    def send_seg(k, carry):
        s_copy(k, seg_peer(k), r).start()
        return carry

    lax.fori_loop(1, 16, send_seg, 0)

    def row_step(db, relay):
        def body(i, carry):
            slot = dev(forward_order(i), db)
            arrive(slot)
            if relay:
                copy(vbuf.at[slot], vsend.at[11 + i], dev(0, 1), slot).start()
            compute(slot)
            return carry

        return body

    sem = 4

    def first_axis(da, sem):
        slot = dev(da, 0)
        arrive(slot)
        if da == -1:
            start(vbuf.at[slot], vsend.at[sem], dev(1, 0), slot)
            sem += 1
        start(vbuf.at[slot], vsend.at[sem], dev(0, 1), slot)
        start(vbuf.at[slot], vsend.at[sem + 1], dev(0, -1), slot)
        compute(slot)
        return sem + 2

    for da in [-1, 1]:
        sem = first_axis(da, sem)
    below = row_step(-1, True)
    above = row_step(1, False)
    lax.fori_loop(0, 1, below, 0)
    lax.fori_loop(0, 1, above, 0)

    def both_rows(i, carry):
        return above(i, below(i, carry))

    lax.fori_loop(1, 2, both_rows, 0)
    sem = first_axis(-2, sem)
    lax.fori_loop(2, 4, both_rows, 0)
    lax.fori_loop(0, 4, row_step(-2, False), 0)

    span = hist_ref.shape[1]
    mine = pl.ds(pl.multiple_of(core * span, span), span)
    theirs = pl.ds(pl.multiple_of((1 - core) * span, span), span)
    swap = pltpu.make_async_remote_copy(
        src_ref=acc_ref.at[:, theirs], dst_ref=pbuf, send_sem=psend, recv_sem=precv,
        device_id=(partner, o), device_id_type=MESH_ID,
    )
    swap.start()
    swap.wait_recv()
    hist_ref[...] = acc_ref[:, mine] + pbuf[...]
    swap.wait_send()
    for c in started:
        c.wait_send()

    def relay_drain(i, carry):
        slot = dev(forward_order(i), -1)
        copy(vbuf.at[slot], vsend.at[11 + i], dev(0, 1), slot).wait_send()
        return carry

    lax.fori_loop(0, 4, relay_drain, 0)

    def drain(k, carry):
        s_copy(k, seg_peer(k), r).wait_send()
        return carry

    lax.fori_loop(1, 16, drain, 0)

    node_hist(hist_ref, parent_ref, small_ref, evict_ref, hist_ref, nodes)
    exchange(functools.partial(gain_terms, hist_ref, nodes), split_ref, best_ref, gbuf, mbuf, gsend, grecv, msend, mrecv, targets)


def pair_split(small_side, evicted, seg_c, v_loc, parent, nodes, targets):
    chips, width, half = seg_c.shape
    n_rows = 2 * chips
    n_outs = lax.axis_size("outs")
    vw, rows = v_loc.shape
    cols = width // 2 * BINS
    span = cols // 2
    out_rows = vw * nodes
    total = n_rows * rows
    vmem = pl.BlockSpec(memory_space=pltpu.VMEM)
    smem = pl.BlockSpec(memory_space=pltpu.SMEM)
    return pl.pallas_call(
        functools.partial(pair_split_kernel, nodes=nodes, targets=targets),
        out_shape=(
            jax.ShapeDtypeStruct((out_rows, span), jnp.float32),
            jax.ShapeDtypeStruct((nodes, span), jnp.float32),
            jax.ShapeDtypeStruct((nodes, 128), jnp.float32),
        ),
        in_specs=[smem, smem, vmem, vmem, vmem],
        out_specs=(vmem, vmem, vmem),
        scratch_shapes=[
            pltpu.VMEM((out_rows, cols), jnp.float32),
            pltpu.VMEM((n_rows, vw, rows), v_loc.dtype),
            pltpu.VMEM((n_rows, width, half), seg_c.dtype),
            pltpu.VMEM((out_rows, span), jnp.float32),
            pltpu.SemaphoreType.DMA((chips,)),
            pltpu.SemaphoreType.DMA((n_rows,)),
            pltpu.SemaphoreType.DMA((chips,)),
            pltpu.SemaphoreType.DMA((n_rows,)),
            pltpu.SemaphoreType.DMA(()),
            pltpu.SemaphoreType.DMA(()),
            pltpu.VMEM((n_outs, nodes, span), jnp.float32),
            pltpu.VMEM((n_rows, nodes, 128), jnp.float32),
            pltpu.SemaphoreType.DMA((2, n_outs)),
            pltpu.SemaphoreType.DMA((2, n_outs)),
            pltpu.SemaphoreType.DMA((n_rows,)),
            pltpu.SemaphoreType.DMA((n_rows,)),
        ],
        compiler_params=pltpu.CompilerParams(collective_id=2, has_side_effects=True),
        cost_estimate=pl.CostEstimate(
            flops=2 * out_rows * cols * total // 2,
            bytes_accessed=total * (vw * 2 + width) + out_rows * cols * 4,
            transcendentals=0,
        ),
    )(small_side, evicted, seg_c, v_loc, parent)


def local(codes, node_of_row, grad, hess, small_side, evicted, parent_hist):
    pairs = small_side.shape[0]
    nodes = 2 * pairs
    local_targets = grad.shape[1]
    targets = local_targets * lax.axis_size("outs")
    n_rows = lax.axis_size("rows")
    count, features = codes.shape
    feats = features // n_rows
    half = count // 2
    seg = (node_of_row[:, None] * BINS + codes).astype(jnp.int16)
    seg_p = jnp.transpose(seg.reshape(2, half, n_rows, feats), (2, 3, 0, 1)).reshape(n_rows, 2 * feats, half)
    v_loc = jnp.concatenate([grad.T, hess.T], axis=0)
    span = feats * BINS
    parent = parent_hist.reshape(2 * pairs * local_targets, span)
    if n_rows == 32:
        seg_t = (codes.T + node_of_row[None, :] * BINS).astype(jnp.int16)
        seg_c = seg_t.reshape(n_rows // 2, 2 * feats, 2, half).reshape(n_rows // 2, 4 * feats, half)
        hist, split_gain, best = pair_split(small_side, evicted, seg_c, v_loc, parent, nodes, targets)
    else:
        hist, split_gain, best = gather_hist(small_side, evicted, seg_p, v_loc, parent, nodes, targets)
    node_hist = hist.reshape(2, nodes, local_targets, span)
    return (node_hist, split_gain, best[:, 0])


def solution(mesh):
    return jax.shard_map(
        local,
        mesh=mesh,
        in_specs=(
            P("rows", None),
            P("rows"),
            P("rows", "outs"),
            P("rows", "outs"),
            P(),
            P(),
            P(None, None, "outs", "rows"),
        ),
        out_specs=(P(None, None, "outs", "rows"), P(None, "rows"), P()),
        check_vma=False,
    )
```
